128 devices in a mesh: lon: 16 (over y, x_hi, core), lat: 8 (over x_lo, z).
Axes of the slice: x: 4 (x_hi: 2, x_lo: 2; x = x_hi * 2 + x_lo), y: 4, z: 4, core: 2. Of those that a mesh axis runs over, the one named last changes fastest.
Arguments:
- coarse: bfloat16 [12, 16, 16384], P(None, None, ('lon', 'lat')), may hold values from -6 to 6
- target: float32 [4, 16, 16384], P(None, 'lat', 'lon'), may hold values from -6 to 6
- noise: float32 [4, 16, 16384], P(None, 'lat', 'lon'), may hold values from -6 to 6
- land_mask: int32 [16, 16384], P('lat', 'lon'), may hold values 0 or 1
- level_index: int32 [8, 16], P('lat', 'lon'), may hold values from 0 to 31
- frozen_first: bfloat16 [3, 3, 128, 12], replicated, may hold values from -0.625 to 0.625
- frozen_middle: bfloat16 [3, 3, 128, 128], replicated, may hold values from -0.1875 to 0.1875
- frozen_last: bfloat16 [3, 3, 4, 128], replicated, may hold values from -0.1875 to 0.1875
- diffuse_in: bfloat16 [3, 3, 128, 20], replicated, may hold values from -0.4375 to 0.4375
- diffuse_down: bfloat16 [3, 3, 256, 128], replicated, may hold values from -0.1875 to 0.1875
- diffuse_up: bfloat16 [3, 3, 128, 256], replicated, may hold values from -0.125 to 0.125
- diffuse_out: bfloat16 [3, 3, 4, 128], replicated, may hold values from -0.1875 to 0.1875
Outputs:
- denoised: float32 [4, 16, 16384], P(None, 'lat', 'lon')
- grad_in: float32 [3, 3, 128, 20], replicated
- grad_down: float32 [3, 3, 256, 128], replicated
- grad_up: float32 [3, 3, 128, 256], replicated
- grad_last: float32 [3, 3, 4, 128], replicated
The draws below stay inside these ranges and needn't reach their ends.
All inputs are finite; a program needn't handle non-finite values. No bound on the sum of `land_mask` on one device may be relied on, other than what follows from the above.
Results may differ from the reference program's by a relative error of at most 0.0044.
Values may be sent and summed in bfloat16 or wider, within the bound.
No kernel may reach another device: no remote copies, remote signals or barrier semaphores. Data moves between devices by JAX's collectives and lax.ppermute only.
A program may use at most 128 MiB of HBM per device.

```python
import math
import jax
import jax.numpy as jnp
from jax import lax

C_IN = 12
C_OUT = 4
HID1 = 128
HID2 = 256
LEVELS = 32
LAT_DEV = 2
LON_DEV = 1024
CAT = 20
NLAT = 16
NLON = 16384
N_LON = 16
N_LAT = 8


def place_ends(values, own_key, low, high):
    longest = values.shape.index(max(values.shape))
    spots = []
    for shift in (0, 1):
        where = [jax.random.randint(jax.random.fold_in(own_key, axis), (), 0, length) for axis, length in enumerate(values.shape)]
        where[longest] = (where[longest] + shift) % values.shape[longest]
        spots.append(tuple(where))
    return values.at[spots[0]].set(low).at[spots[1]].set(high)


def shard_levels(own_key, shape, split, least, top_value):
    loudness, own = 1.0, jax.random.fold_in(own_key, 6)
    for position, shards_of in split:
        draws = jnp.exp(jax.random.uniform(jax.random.fold_in(own, position), (shards_of,), jnp.float32, least / len(split), top_value / len(split)))
        loudness = loudness * jnp.repeat(draws, shape[position] // shards_of).reshape([-1 if axis == position else 1 for axis in range(len(shape))])
    return loudness


def scatter_about(rng, shape, width, limit, pieces=(), held_as=jnp.bfloat16):
    result = jax.random.normal(rng, shape, jnp.float32) * width
    if len(pieces) > 0:
        result = shard_levels(rng, shape, pieces, -0.22, 0.18) * result
    return jnp.clip(result, min=-limit, max=limit).astype(held_as)


def setup_inputs(seed: int = 0) -> dict:
    keys = jax.random.split(jax.random.key(seed), 13)
    return {
        "coarse": scatter_about(keys[0], (C_IN, NLAT, NLON), 1.0, 6.0, ((2, 128),)),
        "target": scatter_about(keys[1], (C_OUT, NLAT, NLON), 1.0, 6.0, ((1, 8), (2, 16)), jnp.float32),
        "noise": scatter_about(keys[2], (C_OUT, NLAT, NLON), 1.0, 6.0, ((1, 8), (2, 16)), jnp.float32),
        "land_mask": place_ends((jax.random.randint(keys[3], (NLAT, NLON), 0, 10) < 3).astype(jnp.int32), jax.random.fold_in(keys[3], 1), 0, 1),
        "level_index": place_ends(jax.random.randint(keys[4], (N_LAT, N_LON), 0, LEVELS), jax.random.fold_in(keys[4], 1), 0, LEVELS - 1).astype(jnp.int32),
        "frozen_first": scatter_about(keys[5], (3, 3, HID1, C_IN), (9 * C_IN) ** -0.5, 0.625),
        "frozen_middle": scatter_about(keys[6], (3, 3, HID1, HID1), (9 * HID1) ** -0.5, 0.1875),
        "frozen_last": scatter_about(keys[7], (3, 3, C_OUT, HID1), (9 * HID1) ** -0.5, 0.1875),
        "diffuse_in": scatter_about(keys[8], (3, 3, HID1, CAT), (9 * CAT) ** -0.5, 0.4375),
        "diffuse_down": scatter_about(keys[9], (3, 3, HID2, HID1), (9 * HID1) ** -0.5, 0.1875),
        "diffuse_up": scatter_about(keys[10], (3, 3, HID1, HID2), (9 * HID2) ** -0.5, 0.125),
        "diffuse_out": scatter_about(keys[11], (3, 3, C_OUT, HID1), (9 * HID1) ** -0.5, 0.1875),
    }


def conv_valid(padded, weight):
    height = padded.shape[1] - 2
    breadth = padded.shape[2] - 2
    total = jnp.zeros((weight.shape[2], height * breadth), jnp.float32)
    for row_tap in range(3):
        for col_tap in range(3):
            tile = padded[:, row_tap:row_tap + height, col_tap:col_tap + breadth].reshape(padded.shape[0], height * breadth)
            total = total + jnp.dot(weight[row_tap, col_tap], tile, preferred_element_type=jnp.float32)
    return total.reshape(weight.shape[2], height, breadth)

def weight_grad(padded, cotangent):
    outer = cotangent.shape[0]
    height = cotangent.shape[1]
    breadth = cotangent.shape[2]
    flat = cotangent.reshape(outer, height * breadth)
    taps = []
    for row_tap in range(3):
        for col_tap in range(3):
            tile = padded[:, row_tap:row_tap + height, col_tap:col_tap + breadth].reshape(padded.shape[0], height * breadth)
            taps.append(lax.dot_general(flat, tile, (((1,), (1,)), ((), ())), preferred_element_type=jnp.float32))
    return jnp.stack(taps, 0).reshape(3, 3, outer, padded.shape[0])

def input_grad(padded, weight):
    height = padded.shape[1] - 2
    breadth = padded.shape[2] - 2
    total = jnp.zeros((weight.shape[3], height * breadth), jnp.float32)
    for row_tap in range(3):
        for col_tap in range(3):
            tile = padded[:, row_tap:row_tap + height, col_tap:col_tap + breadth].reshape(padded.shape[0], height * breadth)
            total = total + jnp.dot(weight[2 - row_tap, 2 - col_tap].T, tile, preferred_element_type=jnp.float32)
    return total.reshape(weight.shape[3], height, breadth)

def silu_grad(pre):
    sigmo = jax.nn.sigmoid(pre)
    return sigmo * (1.0 + pre * (1.0 - sigmo))

def regression(inputs, frozen_first, frozen_middle, frozen_last, widen):
    first = jax.nn.silu(conv_valid(widen(inputs), frozen_first)).astype(jnp.bfloat16)
    second = jax.nn.silu(conv_valid(widen(first), frozen_middle)).astype(jnp.bfloat16)
    return conv_valid(widen(second), frozen_last).astype(jnp.bfloat16)

def train_step(mean, coarse_tile, target, noise, land_mask, sigma, diffuse_in, diffuse_down, diffuse_up, diffuse_out, widen, scale, reduce_fn):
    residual = target - mean.astype(jnp.float32)
    noisy = residual + sigma * noise
    variance = sigma * sigma + 0.25
    c_in = lax.rsqrt(variance)
    c_skip = 0.25 / variance
    c_out = 0.5 * sigma * c_in
    lam = variance / (0.25 * sigma * sigma)
    net_in = jnp.concatenate([mean, (c_in * noisy).astype(jnp.bfloat16), coarse_tile], 0)
    pad_in = widen(net_in)
    pre_a = conv_valid(pad_in, diffuse_in)
    act_a = jax.nn.silu(pre_a).astype(jnp.bfloat16)
    chan_one = act_a.shape[0]
    height = act_a.shape[1]
    breadth = act_a.shape[2]
    pooled = act_a.astype(jnp.float32).reshape(chan_one, height // 2, 2, breadth // 2, 2).mean((2, 4)).astype(jnp.bfloat16)
    pad_pool = widen(pooled)
    pre_b = conv_valid(pad_pool, diffuse_down)
    act_b = jax.nn.silu(pre_b).astype(jnp.bfloat16)
    chan_two = act_b.shape[0]
    upsampled = jnp.broadcast_to(act_b[:, :, None, :, None], (chan_two, height // 2, 2, breadth // 2, 2)).reshape(chan_two, height, breadth)
    pad_up = widen(upsampled)
    pre_c = conv_valid(pad_up, diffuse_up)
    act_c = (jax.nn.silu(pre_c) + act_a.astype(jnp.float32)).astype(jnp.bfloat16)
    pad_c = widen(act_c)
    field = conv_valid(pad_c, diffuse_out)
    denoised = c_skip * noisy + c_out * field
    weight_map = 1.0 + land_mask.astype(jnp.float32)
    loss_grad = 2.0 * scale * weight_map * lam * (denoised - residual)
    grad_f = (c_out * loss_grad).astype(jnp.bfloat16)
    grad_last = reduce_fn(weight_grad(pad_c, grad_f))
    back_c = input_grad(widen(grad_f), diffuse_out)
    grad_pre_c = (back_c * silu_grad(pre_c)).astype(jnp.bfloat16)
    grad_up = reduce_fn(weight_grad(pad_up, grad_pre_c))
    back_up = input_grad(widen(grad_pre_c), diffuse_up)
    back_b = back_up.reshape(chan_two, height // 2, 2, breadth // 2, 2).sum((2, 4))
    grad_pre_b = (back_b * silu_grad(pre_b)).astype(jnp.bfloat16)
    grad_down = reduce_fn(weight_grad(pad_pool, grad_pre_b))
    back_pool = input_grad(widen(grad_pre_b), diffuse_down)
    spread = jnp.broadcast_to(back_pool[:, :, None, :, None], (chan_one, height // 2, 2, breadth // 2, 2)).reshape(chan_one, height, breadth)
    back_a = back_c + 0.25 * spread
    grad_pre_a = (back_a * silu_grad(pre_a)).astype(jnp.bfloat16)
    grad_in = reduce_fn(weight_grad(pad_in, grad_pre_a))
    return (denoised, (grad_in, grad_down, grad_up, grad_last))

def widen_global(field):
    wrapped = jnp.concatenate([field[:, :, -1:], field, field[:, :, :1]], axis=2)
    return jnp.pad(wrapped, ((0, 0), (1, 1), (0, 0)))

def keep_same(value):
    return value

def reference(coarse, target, noise, land_mask, level_index, frozen_first, frozen_middle, frozen_last, diffuse_in, diffuse_down, diffuse_up, diffuse_out):
    mean = regression(coarse, frozen_first, frozen_middle, frozen_last, widen_global)
    tile_sigma = 0.02 * 4000.0 ** (level_index.astype(jnp.float32) / (LEVELS - 1))
    sigma = jnp.broadcast_to(tile_sigma[:, None, :, None], (N_LAT, LAT_DEV, N_LON, LON_DEV)).reshape(NLAT, NLON)[None]
    scale = 1.0 / (C_OUT * math.sqrt(NLAT * NLON))
    denoised, grads = train_step(mean, coarse, target, noise, land_mask, sigma, diffuse_in, diffuse_down, diffuse_up, diffuse_out, widen_global, scale, keep_same)
    return (denoised, grads[0], grads[1], grads[2], grads[3])
```

```python
import math

import jax
import jax.numpy as jnp
from jax import lax
from jax.experimental import pallas as pl
from jax.experimental.pallas import tpu as pltpu
from jax.sharding import Mesh
from jax.sharding import PartitionSpec as P

LEVELS = 32
ROWS = 16
LOW = ROWS // 2
OWN = 128
HALO = 16
WIDE = OWN + 2 * HALO
WLOW = WIDE // 2
LANES = 256
HID1 = 128
HID2 = 256
BF = jnp.bfloat16
F32 = jnp.float32

LON = ("y", "x_hi", "core")
LAT = ("x_lo", "z")
CHIPS = ("y", "x_hi", "x_lo", "z")
STRIPS = LON + LAT

FIELDS = 24
UP_ROWS = 9 * HID1
DOWN_ROWS = 9 * HID2
BIG_ROWS = 2304
LAST_ROWS = 72
IN_ROWS = 9 * FIELDS
HALF_ROWS = 2560


def mm(x, w):
    return lax.dot_general(x, w, (((1,), (0,)), ((), ())), preferred_element_type=F32)


def mm_nt(x, w):
    return lax.dot_general(x, w, (((1,), (1,)), ((), ())), preferred_element_type=F32)


def mm_tn(x, w):
    return lax.dot_general(x, w, (((0,), (0,)), ((), ())), preferred_element_type=F32)


def back(x, axis):
    return pltpu.roll(x, x.shape[axis] - 1, axis)


def ahead(x, axis):
    return pltpu.roll(x, 1, axis)


def with_halo(own, left, right):
    lane = lax.broadcasted_iota(jnp.int32, own.shape, 1)
    halo = jnp.where(lane < HALO, right, jnp.where(lane >= OWN - HALO, left, 0.0))
    return jnp.concatenate([own, halo], axis=1)


def to_cells(stack):
    pad = OWN - stack.shape[0]
    if pad:
        stack = jnp.concatenate([stack, jnp.zeros((pad, LANES), F32)], axis=0)
    cells = stack.T
    return jnp.concatenate([cells[: OWN + HALO], cells[LANES - HALO :]], axis=0).astype(BF)


def to_lanes(cells):
    gap = jnp.zeros((LANES - WIDE, cells.shape[1]), cells.dtype)
    return jnp.concatenate([cells[: OWN + HALO], gap, cells[OWN + HALO :]], axis=0)


def lon_shifts(field):
    return jnp.concatenate([ahead(field, 1), field, back(field, 1)], axis=0)


def three_rows(ref, start, count):
    width = ref.shape[1]
    return jnp.concatenate(
        [ref[pl.ds(start + a, count)].reshape(count * width, ref.shape[2]) for a in range(3)], axis=1
    )


def lon_sum(taps, count, width, out):
    first, second, third = (
        taps[:, b * out : (b + 1) * out].reshape(count, width, out) for b in range(3)
    )
    return ahead(first, 1) + second + back(third, 1)


def four_channels(ref, row):
    sums = []
    for b in range(3):
        at = [(a * 3 + b) * 8 for a in range(3)]
        sums.append(
            ref[row, at[0] : at[0] + 8]
            + ref[row + 1, at[1] : at[1] + 8]
            + ref[row + 2, at[2] : at[2] + 8]
        )
    return ahead(sums[0], 1) + sums[1] + back(sums[2], 1)


def zero_edges(ref):
    edge = jnp.zeros(ref.shape[1:], ref.dtype)
    ref[0] = edge
    ref[ref.shape[0] - 1] = edge


def each(count, body, unroll=1):
    def step(i, carry):
        body(i)
        return carry

    lax.fori_loop(0, count, step, 0, unroll=unroll)


def pack_kernel(target, noise, land_mask, level, packed):
    power = level[...].astype(F32) / (LEVELS - 1)
    sigma = jnp.broadcast_to(0.02 * jnp.exp(power * math.log(4000.0)), (1, OWN))
    weight = 1.0 + land_mask[...].astype(F32)
    for p in range(packed.shape[0]):
        lanes = slice(p * OWN, (p + 1) * OWN)
        for r in range(2):
            packed[p, r, 0:1] = weight[r : r + 1, lanes]
            packed[p, r, 1:2] = sigma
            packed[p, r, 2:4] = jnp.zeros((2, OWN), F32)
            packed[p, r, 4:8] = target[:, r, lanes]
            packed[p, r, 8:12] = jnp.zeros((4, OWN), F32)
            packed[p, r, 12:16] = noise[:, r, lanes]


def stack_inputs(ref, weight, room):
    ref[...] = jnp.zeros_like(ref)
    count = weight.shape[2]
    for a in range(3):
        for b in range(3):
            ref[a, b * room : b * room + count] = weight[a, b].astype(F32)
    return ref[...].astype(BF).reshape(3 * OWN, OWN)


def stack_outputs(ref, weight):
    ref[...] = jnp.zeros_like(ref)
    for a in range(3):
        for b in range(3):
            at = (a * 3 + b) * 8 + 4
            ref[at : at + 4] = weight[a, b].astype(F32)
    return ref[...].astype(BF)


def step_kernel(
    scale,
    place,
    own,
    left,
    right,
    w_first,
    w_middle,
    w_last,
    w_in,
    w_down,
    w_up,
    w_out,
    grads,
    *rest,
):
    lats = 8
    tiles, scratch = rest[:lats], rest[lats:]
    (
        stack,
        stack_o,
        field,
        net,
        hid,
        act_c,
        taps,
        residuals,
        noisies,
        slope_a,
        act_a,
        pairs,
        pooled,
        act_b,
        slope_b,
        up_taps,
        phases,
        slope_c,
        grad_f,
        spread_f,
        back_c,
        grad_c,
        blocks,
        grad_b,
        grad_a,
        last_sum,
        den,
    ) = scratch
    for ref in (net, hid, pooled, up_taps, taps, grad_f, grad_c, grad_b):
        zero_edges(ref)
    first_w = stack_inputs(stack, w_first, 16)

    def gather(r):
        wide = with_halo(own[r], left[r], right[r])
        field[r] = wide
        net[r + 1] = to_cells(lon_shifts(wide[8:24]))

    each(ROWS, gather, 4)

    def first(i):
        pre = mm(three_rows(net, 4 * i, 4), first_w)
        hid[pl.ds(4 * i + 1, 4)] = jax.nn.silu(pre).astype(BF).reshape(4, WIDE, HID1)

    each(ROWS // 4, first)
    middle_w = jnp.concatenate([w_middle[a] for a in range(3)], axis=1)

    def second(i):
        pre = lon_sum(mm_nt(three_rows(hid, 4 * i, 4), middle_w), 4, WIDE, HID1)
        act_c[pl.ds(4 * i, 4)] = jax.nn.silu(pre).astype(BF)

    each(ROWS // 4, second)
    last_w = stack_outputs(stack_o, w_last)[0:72]

    def mean_taps(r):
        taps[r + 1] = mm_nt(last_w, to_lanes(act_c[r]))

    each(ROWS, mean_taps, 4)
    in_w = stack_inputs(stack, w_in, FIELDS)
    lane = lax.broadcasted_iota(jnp.int32, (8, LANES), 1)
    held = (lane < OWN + HALO) | (lane >= LANES - HALO)
    low_half = lax.broadcasted_iota(jnp.int32, (8, LANES), 0) < 4

    def enter(r):
        mean_r = four_channels(taps, r).astype(BF).astype(F32)
        sigma = jnp.where(held, jnp.broadcast_to(field[r, 1:2], (8, LANES)), 1.0)
        residual = field[r, 0:8] - mean_r
        noisy = residual + sigma * field[r, 16:24]
        variance = sigma * sigma + 0.25
        residuals[r] = residual
        noisies[r] = noisy
        scaled = (lax.rsqrt(variance) * noisy).astype(BF).astype(F32)
        both = jnp.where(low_half, pltpu.roll(mean_r, 4, 0), scaled)
        net[r + 1] = to_cells(lon_shifts(jnp.concatenate([both, field[r, 8:24]], axis=0)))

    each(ROWS, enter, 4)

    def level_one(i):
        pre = mm(three_rows(net, 4 * i, 4), in_w)
        gate = jax.nn.sigmoid(pre)
        slope_a[pl.ds(4 * i, 4)] = (gate * (1.0 + pre * (1.0 - gate))).reshape(4, WIDE, HID1)
        act = (pre * gate).astype(BF).reshape(4, WIDE, HID1)
        act_a[pl.ds(4 * i, 4)] = act
        wide = act.astype(F32)
        for k in range(2):
            pairs[k] = wide[2 * k] + wide[2 * k + 1]
            total = pairs[k, pl.ds(0, WLOW, stride=2)] + pairs[k, pl.ds(1, WLOW, stride=2)]
            pooled[2 * i + k + 1] = (0.25 * total).astype(BF)

    each(ROWS // 4, level_one)
    down_w = jnp.concatenate([w_down[a] for a in range(3)], axis=1)

    def level_two(i):
        pre = lon_sum(mm_nt(three_rows(pooled, 2 * i, 2), down_w), 2, WLOW, HID2)
        gate = jax.nn.sigmoid(pre)
        slope_b[pl.ds(2 * i, 2)] = gate * (1.0 + pre * (1.0 - gate))
        act_b[pl.ds(2 * i, 2)] = (pre * gate).astype(BF)

    each(LOW // 2, level_two)

    def up_products(i):
        low = act_b[pl.ds(2 * i, 2)].reshape(2 * WLOW, HID2)
        up_taps[pl.ds(2 * i + 1, 2)] = mm_nt(low, w_up[...]).reshape(2, WLOW, 9 * HID1)

    each(LOW // 2, up_products)

    def level_three(i):
        for pi in range(2):
            sums = []
            for b in range(3):
                total = None
                for a in range(3):
                    row = i + 1 + (pi + a - 1) // 2
                    at = (a * 3 + b) * HID1
                    part = up_taps[row, :, at : at + HID1]
                    total = part if total is None else total + part
                sums.append(total)
            phases[pi, pl.ds(0, WLOW, stride=2)] = ahead(sums[0], 0) + sums[1] + sums[2]
            phases[pi, pl.ds(1, WLOW, stride=2)] = sums[0] + sums[1] + back(sums[2], 0)
            row = 2 * i + pi
            pre = phases[pi]
            gate = jax.nn.sigmoid(pre)
            act_c[row] = (pre * gate + act_a[row].astype(F32)).astype(BF)
            slope_c[row] = gate * (1.0 + pre * (1.0 - gate))

    each(LOW, level_three)
    out_w = stack_outputs(stack_o, w_out)

    def field_taps(r):
        taps[r + 1] = mm_nt(out_w[0:72], to_lanes(act_c[r]))

    each(ROWS, field_taps, 4)

    def loss(r):
        value = four_channels(taps, r)
        sigma = jnp.where(held, jnp.broadcast_to(field[r, 1:2], (8, LANES)), 1.0)
        weight = jnp.broadcast_to(field[r, 0:1], (8, LANES))
        variance = sigma * sigma + 0.25
        c_out = 0.5 * sigma * lax.rsqrt(variance)
        lam = variance / (0.25 * sigma * sigma)
        denoised = (0.25 / variance) * noisies[r] + c_out * value
        den[r] = denoised[4:8, :OWN]
        loss_grad = (2.0 * scale) * weight * lam * (denoised - residuals[r])
        cot = (c_out * loss_grad).astype(BF).astype(F32)
        grad_f[r + 1] = jnp.where(low_half, 0.0, cot)

    each(ROWS, loss, 4)
    lat = place[1]
    for k in range(lats):
        tiles[k][...] = den[pl.ds(2 * lax.rem(lat + k, lats), 2)]
    last_sum[...] = jnp.zeros_like(last_sum)

    def last_grads(r):
        parts = []
        for a in range(3):
            cot = grad_f[r + 2 - a]
            parts += [back(cot, 1), cot, ahead(cot, 1)]
        cots = jnp.concatenate(parts + [jnp.zeros((8, LANES), F32)], axis=0)
        last_sum[...] += mm(cots[:, :OWN].astype(BF), act_c[r, 0:OWN])
        spread_f[r] = to_cells(cots)

    each(ROWS, last_grads, 4)
    near, far = place[0], 1 - place[0]

    def keep(half, at, value):
        grads[pl.ds(half, 1), at : at + value.shape[0]] = value.astype(BF)[None]

    keep(near, BIG_ROWS, last_sum[0:LAST_ROWS])
    keep(near, BIG_ROWS + LAST_ROWS, jnp.zeros((HALF_ROWS - BIG_ROWS - LAST_ROWS, OWN), F32))

    def back_three(i):
        wide = mm(spread_f[pl.ds(4 * i, 4)].reshape(4 * WIDE, OWN), out_w)
        wide = wide.reshape(4, WIDE, HID1)
        back_c[pl.ds(4 * i, 4)] = wide
        grad_c[pl.ds(4 * i + 1, 4)] = wide * slope_c[pl.ds(4 * i, 4)]

    each(ROWS // 4, back_three)

    def block_sums(i):
        even = [grad_c[2 * i + k, pl.ds(0, WLOW, stride=2)] for k in range(4)]
        odd = [grad_c[2 * i + k, pl.ds(1, WLOW, stride=2)] for k in range(4)]
        for a in range(3):
            e, o = even[2 - a] + even[3 - a], odd[2 - a] + odd[3 - a]
            for b, total in enumerate((o + back(e, 0), e + o, ahead(o, 0) + e)):
                at = (a * 3 + b) * HID1
                blocks[i, :, at : at + HID1] = total.astype(BF)

    each(LOW, block_sums)

    def back_two(i):
        low = mm(blocks[pl.ds(2 * i, 2)].reshape(2 * WLOW, 9 * HID1), w_up[...])
        cot = low.reshape(2, WLOW, HID2) * slope_b[pl.ds(2 * i, 2)]
        shifts = jnp.concatenate([back(cot, 1), cot, ahead(cot, 1)], axis=2)
        grad_b[pl.ds(2 * i + 1, 2)] = shifts.astype(BF)

    each(LOW // 2, back_two)
    own_low = lax.broadcasted_iota(jnp.int32, (LOW, WLOW, HID2), 1) < OWN // 2
    low_b = jnp.where(own_low, act_b[...].astype(F32), 0.0).astype(BF).reshape(LOW * WLOW, HID2)
    for k in range(3):
        left_side = blocks[:, :, 3 * HID1 * k : 3 * HID1 * (k + 1)].reshape(LOW * WLOW, 3 * HID1)
        up = mm_tn(left_side, low_b)
        keep(near, 3 * HID1 * k, up[:, :HID1])
        keep(near, 3 * HID1 * k + UP_ROWS, up[:, HID1:])
    own_one = lax.broadcasted_iota(jnp.int32, (LOW, WLOW, HID1), 1) < OWN // 2
    low_a = jnp.concatenate(
        [
            jnp.where(own_one, pooled[a : a + LOW].astype(F32), 0.0).astype(BF).reshape(LOW * WLOW, HID1)
            for a in range(3)
        ],
        axis=1,
    )
    for b in range(3):
        left_side = grad_b[1 : LOW + 1, :, HID2 * b : HID2 * (b + 1)].reshape(LOW * WLOW, HID2)
        down = mm_tn(left_side, low_a)
        for a in range(3):
            keep(far, (a * 3 + b) * HID2, down[:, HID1 * a : HID1 * (a + 1)])
    own_wide = lax.broadcasted_iota(jnp.int32, (WIDE, HID1), 0) < OWN

    def back_one(i):
        total = None
        for a in range(3):
            cot = grad_b[pl.ds(2 * i + 2 - a, 2)].reshape(2 * WLOW, 3 * HID2)
            part = mm(cot, w_down[a])
            total = part if total is None else total + part
        low = (0.25 * total).reshape(2, WLOW, HID1)
        for k in range(2):
            phases[k, pl.ds(0, WLOW, stride=2)] = low[k]
            phases[k, pl.ds(1, WLOW, stride=2)] = low[k]
            for pi in range(2):
                row = 4 * i + 2 * k + pi
                cot = (back_c[row] + phases[k]) * slope_a[row]
                grad_a[row] = jnp.where(own_wide, cot, 0.0).astype(BF)

    each(LOW // 2, back_one)
    inputs = mm_tn(three_rows(net, 0, ROWS), grad_a[...].reshape(ROWS * WIDE, HID1))
    for a in range(3):
        keep(far, BIG_ROWS + a * 3 * FIELDS, inputs[a * OWN : a * OWN + 3 * FIELDS])
    keep(far, BIG_ROWS + IN_ROWS, jnp.zeros((HALF_ROWS - BIG_ROWS - IN_ROWS, OWN), F32))


def unpack_kernel(place, mine, other, *rest):
    tiles, (tile, first, down, up, last) = rest[:8], rest[8:]
    a = pl.program_id(0)
    even = place[0] == 0

    def half(k, at, count):
        rows = pl.ds(pl.multiple_of(at, 8), count)
        if k == 0:
            return jnp.where(even, mine[rows].astype(F32), other[rows].astype(F32))
        return jnp.where(even, other[rows].astype(F32), mine[rows].astype(F32))

    low = half(0, a * (3 * HID1), 3 * HID1).reshape(3, HID1, HID1)
    high = half(0, a * (3 * HID1) + UP_ROWS, 3 * HID1).reshape(3, HID1, HID1)
    up[0] = jnp.concatenate([low, high], axis=2)
    down[0] = half(1, a * (3 * HID2), 3 * HID2).reshape(3, HID2, HID1)
    firsts = half(1, BIG_ROWS + a * (3 * FIELDS), 3 * FIELDS)
    lasts = half(0, BIG_ROWS + a * FIELDS, FIELDS)
    for b in range(3):
        first[0, b] = firsts[b * FIELDS : b * FIELDS + 20]
        last[0, b] = lasts[b * 8 + 4 : b * 8 + 8]

    @pl.when(a == 0)
    def _():
        for k in range(8):
            at = pl.multiple_of(lax.rem(place[1] + 8 - k, 8) * OWN, OWN)
            for r in range(2):
                tile[:, r, pl.ds(at, OWN)] = tiles[k][r]


def in_vmem(count):
    return [pl.BlockSpec(memory_space=pltpu.MemorySpace.VMEM) for _ in range(count)]


def in_smem():
    return pl.BlockSpec(memory_space=pltpu.MemorySpace.SMEM)


def pack(target, noise, land_mask, level_index):
    lats = target.shape[2] // OWN
    return pl.pallas_call(
        pack_kernel,
        out_shape=jax.ShapeDtypeStruct((lats, 2, 16, OWN), F32),
        in_specs=in_vmem(4),
        out_specs=in_vmem(1)[0],
        name="pack",
    )(target, noise, land_mask, level_index)


def step(scale, *operands):
    def kernel(*refs):
        step_kernel(scale, *refs)

    return pl.pallas_call(
        kernel,
        out_shape=(
            jax.ShapeDtypeStruct((2, HALF_ROWS, OWN), BF),
            *([jax.ShapeDtypeStruct((2, 4, OWN), F32)] * 8),
        ),
        in_specs=[in_smem(), *in_vmem(10)],
        out_specs=tuple(in_vmem(9)),
        scratch_shapes=[
            pltpu.VMEM((3, OWN, OWN), F32),
            pltpu.VMEM((OWN, OWN), F32),
            pltpu.VMEM((ROWS, FIELDS, LANES), F32),
            pltpu.VMEM((ROWS + 2, WIDE, OWN), BF),
            pltpu.VMEM((ROWS + 2, WIDE, HID1), BF),
            pltpu.VMEM((ROWS, WIDE, HID1), BF),
            pltpu.VMEM((ROWS + 2, 72, LANES), F32),
            pltpu.VMEM((ROWS, 8, LANES), F32),
            pltpu.VMEM((ROWS, 8, LANES), F32),
            pltpu.VMEM((ROWS, WIDE, HID1), F32),
            pltpu.VMEM((ROWS, WIDE, HID1), BF),
            pltpu.VMEM((2, WIDE, HID1), F32),
            pltpu.VMEM((LOW + 2, WLOW, HID1), BF),
            pltpu.VMEM((LOW, WLOW, HID2), BF),
            pltpu.VMEM((LOW, WLOW, HID2), F32),
            pltpu.VMEM((LOW + 2, WLOW, 9 * HID1), F32),
            pltpu.VMEM((2, WIDE, HID1), F32),
            pltpu.VMEM((ROWS, WIDE, HID1), F32),
            pltpu.VMEM((ROWS + 2, 8, LANES), F32),
            pltpu.VMEM((ROWS, WIDE, OWN), BF),
            pltpu.VMEM((ROWS, WIDE, HID1), F32),
            pltpu.VMEM((ROWS + 2, WIDE, HID1), F32),
            pltpu.VMEM((LOW, WLOW, 9 * HID1), BF),
            pltpu.VMEM((LOW + 2, WLOW, 3 * HID2), BF),
            pltpu.VMEM((ROWS, WIDE, HID1), BF),
            pltpu.VMEM((80, HID1), F32),
            pltpu.VMEM((ROWS, 4, OWN), F32),
        ],
        name="step",
    )(*operands)


def unpack(place, mine, other, tiles):
    whole = pl.BlockSpec((HALF_ROWS, OWN), lambda a: (0, 0))
    part = pl.BlockSpec((2, 4, OWN), lambda a: (0, 0, 0))

    def taps(rows, lanes):
        return pl.BlockSpec((1, 3, rows, lanes), lambda a: (a, 0, 0, 0))

    return pl.pallas_call(
        unpack_kernel,
        grid=(3,),
        out_shape=(
            jax.ShapeDtypeStruct((4, 2, 8 * OWN), F32),
            jax.ShapeDtypeStruct((3, 3, 20, HID1), F32),
            jax.ShapeDtypeStruct((3, 3, HID2, HID1), F32),
            jax.ShapeDtypeStruct((3, 3, HID1, HID2), F32),
            jax.ShapeDtypeStruct((3, 3, 4, HID1), F32),
        ),
        in_specs=[in_smem(), whole, whole, *([part] * 8)],
        out_specs=(
            pl.BlockSpec((4, 2, 8 * OWN), lambda a: (0, 0, 0)),
            taps(20, HID1),
            taps(HID2, HID1),
            taps(HID1, HID2),
            taps(4, HID1),
        ),
        name="unpack",
    )(place, mine, other, *tiles)


def all_to_all(value, axes):
    return lax.all_to_all(value, axes, split_axis=0, concat_axis=0, tiled=True)


def shift_by(value, axes, step):
    count = lax.axis_size(axes)
    return lax.ppermute(value, axes, [(i, (i + step) % count) for i in range(count)])


def local(
    coarse,
    target,
    noise,
    land_mask,
    level_index,
    frozen_first,
    frozen_middle,
    frozen_last,
    diffuse_in,
    diffuse_down,
    diffuse_up,
    diffuse_out,
):
    scale = 1.0 / (target.shape[0] * math.sqrt(target.shape[1] * target.shape[2] * lax.axis_size(STRIPS)))
    place = jnp.stack([lax.axis_index("core"), lax.axis_index(LAT)]).astype(jnp.int32)
    packed = all_to_all(pack(target, noise, land_mask, level_index), LAT).reshape(ROWS, 16, OWN)
    fields = jnp.concatenate([packed[:, :8], coarse.transpose(1, 0, 2).astype(F32), packed[:, 12:]], axis=1)
    grads, *tiles = step(
        scale,
        place,
        fields,
        shift_by(fields, STRIPS, 1),
        shift_by(fields, STRIPS, -1),
        frozen_first.transpose(0, 1, 3, 2),
        frozen_middle.reshape(3, 3 * HID1, HID1),
        frozen_last,
        diffuse_in.transpose(0, 1, 3, 2),
        diffuse_down.reshape(3, 3 * HID2, HID1),
        diffuse_up.reshape(9 * HID1, HID2),
        diffuse_out,
    )
    chips = lax.axis_size(CHIPS)
    half = grads[0].astype(F32) + shift_by(grads[1], "core", 1).astype(F32)
    with jax.named_scope("scatter"):
        parts = all_to_all(half.astype(BF).reshape(chips, HALF_ROWS // chips, OWN), CHIPS)
    with jax.named_scope("tiles"):
        tiles = [tiles[0], *(shift_by(tiles[k], LAT, k) for k in range(1, 8))]
    total = parts.astype(F32).sum(0).astype(BF)
    with jax.named_scope("spread"):
        mine = all_to_all(jnp.broadcast_to(total[None], parts.shape), CHIPS).reshape(HALF_ROWS, OWN)
    tile, first, down, up, last = unpack(place, mine, shift_by(mine, "core", 1), tiles)
    return (tile, first.transpose(0, 1, 3, 2), down, up, last)


def solution(mesh):
    fine = Mesh(mesh.devices.reshape(4, 2, 2, 2, 4), LON + LAT)
    tile = P(None, LAT, LON)
    return jax.shard_map(
        local,
        mesh=fine,
        in_specs=(
            P(None, None, STRIPS),
            tile,
            tile,
            P(LAT, LON),
            P(LAT, LON),
            *([P()] * 7),
        ),
        out_specs=(tile, P(), P(), P(), P()),
        check_vma=False,
    )
```

```python
import math

import jax
import jax.numpy as jnp
from jax import lax
from jax.experimental import pallas as pl
from jax.experimental.pallas import tpu as pltpu
from jax.sharding import Mesh
from jax.sharding import PartitionSpec as P

LEVELS = 32
ROWS = 16
LOW = ROWS // 2
OWN = 128
HALO = 16
WIDE = OWN + 2 * HALO
WLOW = WIDE // 2
LANES = 256
HID1 = 128
HID2 = 256
BF = jnp.bfloat16
F32 = jnp.float32

LON = ("y", "x_hi", "core")
LAT = ("x_lo", "z")
CHIPS = ("y", "x_hi", "x_lo", "z")
STRIPS = LON + LAT

FIELDS = 24
UP_ROWS = 9 * HID1
DOWN_ROWS = 9 * HID2
BIG_ROWS = 2304
LAST_ROWS = 72
IN_ROWS = 9 * FIELDS
HALF_ROWS = 2560
CELL_ROWS = 8
CHUNK = {
    "first": (4, 1),
    "second": (4, 1),
    "one": (4, 1),
    "two": (2, 1),
    "up": (2, 1),
    "back_three": (4, 1),
    "back_two": (2, 1),
    "back_one": (2, 1),
    "three": 1,
    "blocks": 1,
}


def mm(x, w):
    return lax.dot_general(x, w, (((1,), (0,)), ((), ())), preferred_element_type=F32)


def mm_nt(x, w):
    return lax.dot_general(x, w, (((1,), (1,)), ((), ())), preferred_element_type=F32)


def mm_tn(x, w):
    return lax.dot_general(x, w, (((0,), (0,)), ((), ())), preferred_element_type=F32)


def back(x, axis):
    return pltpu.roll(x, x.shape[axis] - 1, axis)


def ahead(x, axis):
    return pltpu.roll(x, 1, axis)


def with_halo(own, left, right):
    lane = lax.broadcasted_iota(jnp.int32, own.shape, 1)
    halo = jnp.where(lane < HALO, right, jnp.where(lane >= OWN - HALO, left, 0.0))
    return jnp.concatenate([own, halo], axis=1)


def to_cells(stack):
    pad = OWN - stack.shape[0]
    if pad:
        stack = jnp.concatenate([stack, jnp.zeros((pad, LANES), F32)], axis=0)
    cells = stack.T
    return jnp.concatenate([cells[: OWN + HALO], cells[LANES - HALO :]], axis=0).astype(BF)


def to_lanes(cells):
    gap = jnp.zeros((LANES - WIDE, cells.shape[1]), cells.dtype)
    return jnp.concatenate([cells[: OWN + HALO], gap, cells[OWN + HALO :]], axis=0)


def lon_shifts(field):
    return jnp.concatenate([ahead(field, 1), field, back(field, 1)], axis=0)


def three_rows(ref, start, count):
    width = ref.shape[1]
    return jnp.concatenate(
        [ref[pl.ds(start + a, count)].reshape(count * width, ref.shape[2]) for a in range(3)], axis=1
    )


def lon_sum(taps, count, width, out):
    first, second, third = (
        taps[:, b * out : (b + 1) * out].reshape(count, width, out) for b in range(3)
    )
    return ahead(first, 1) + second + back(third, 1)


def four_channels(ref, row):
    sums = []
    for b in range(3):
        at = [(a * 3 + b) * 8 for a in range(3)]
        sums.append(
            ref[row, at[0] : at[0] + 8]
            + ref[row + 1, at[1] : at[1] + 8]
            + ref[row + 2, at[2] : at[2] + 8]
        )
    return ahead(sums[0], 1) + sums[1] + back(sums[2], 1)


def zero_edges(ref):
    edge = jnp.zeros(ref.shape[1:], ref.dtype)
    ref[0] = edge
    ref[ref.shape[0] - 1] = edge


def each(count, body, unroll=1):
    def step(i, carry):
        body(i)
        return carry

    lax.fori_loop(0, count, step, 0, unroll=unroll)


def pack_kernel(target, noise, land_mask, level, packed):
    power = level[...].astype(F32) / (LEVELS - 1)
    sigma = jnp.broadcast_to(0.02 * jnp.exp(power * math.log(4000.0)), (1, OWN))
    weight = 1.0 + land_mask[...].astype(F32)
    for p in range(packed.shape[0]):
        lanes = slice(p * OWN, (p + 1) * OWN)
        for r in range(2):
            packed[p, r, 0:1] = weight[r : r + 1, lanes]
            packed[p, r, 1:2] = sigma
            packed[p, r, 2:4] = jnp.zeros((2, OWN), F32)
            packed[p, r, 4:8] = target[:, r, lanes]
            packed[p, r, 8:12] = jnp.zeros((4, OWN), F32)
            packed[p, r, 12:16] = noise[:, r, lanes]


def stack_inputs(ref, weight, room):
    ref[...] = jnp.zeros_like(ref)
    count = weight.shape[2]
    for a in range(3):
        for b in range(3):
            ref[a, b * room : b * room + count] = weight[a, b].astype(F32)
    return ref[...].astype(BF).reshape(3 * OWN, OWN)


def stack_outputs(ref, weight):
    ref[...] = jnp.zeros_like(ref)
    for a in range(3):
        for b in range(3):
            at = (a * 3 + b) * 8 + 4
            ref[at : at + 4] = weight[a, b].astype(F32)
    return ref[...].astype(BF)


def step_kernel(
    scale,
    place,
    own,
    left,
    right,
    w_first,
    w_middle,
    w_last,
    w_in,
    w_down,
    w_up,
    w_out,
    grads,
    tiles,
    *scratch,
):
    (
        stack,
        stack_o,
        field,
        net,
        hid,
        act_c,
        taps,
        residuals,
        noisies,
        slope_a,
        act_a,
        pairs,
        pooled,
        act_b,
        slope_b,
        up_taps,
        phases,
        slope_c,
        grad_f,
        spread_f,
        back_c,
        grad_c,
        blocks,
        grad_b,
        grad_a,
        last_sum,
        den,
    ) = scratch
    for ref in (net, hid, pooled, up_taps, taps, grad_f, grad_c, grad_b):
        zero_edges(ref)
    first_w = stack_inputs(stack, w_first, 16)

    def gather(r):
        wide = with_halo(own[r], left[r], right[r])
        field[r] = wide
        net[r + 1] = to_cells(lon_shifts(wide[8:24]))

    each(ROWS, gather, 4)

    n1, u1 = CHUNK["first"]

    def first(i):
        pre = mm(three_rows(net, n1 * i, n1), first_w)
        hid[pl.ds(n1 * i + 1, n1)] = jax.nn.silu(pre).astype(BF).reshape(n1, WIDE, HID1)

    each(ROWS // n1, first, u1)
    middle_w = jnp.concatenate([w_middle[a] for a in range(3)], axis=1)

    n2, u2 = CHUNK["second"]

    def second(i):
        pre = lon_sum(mm_nt(three_rows(hid, n2 * i, n2), middle_w), n2, WIDE, HID1)
        act_c[pl.ds(n2 * i, n2)] = jax.nn.silu(pre).astype(BF)

    each(ROWS // n2, second, u2)
    last_w = stack_outputs(stack_o, w_last)[0:72]

    def mean_taps(r):
        taps[r + 1] = mm_nt(last_w, to_lanes(act_c[r]))

    each(ROWS, mean_taps, 4)
    in_w = stack_inputs(stack, w_in, FIELDS)
    lane = lax.broadcasted_iota(jnp.int32, (8, LANES), 1)
    held = (lane < OWN + HALO) | (lane >= LANES - HALO)
    low_half = lax.broadcasted_iota(jnp.int32, (8, LANES), 0) < 4

    def enter(r):
        mean_r = four_channels(taps, r).astype(BF).astype(F32)
        sigma = jnp.where(held, jnp.broadcast_to(field[r, 1:2], (8, LANES)), 1.0)
        residual = field[r, 0:8] - mean_r
        noisy = residual + sigma * field[r, 16:24]
        variance = sigma * sigma + 0.25
        residuals[r] = residual
        noisies[r] = noisy
        scaled = (lax.rsqrt(variance) * noisy).astype(BF).astype(F32)
        both = jnp.where(low_half, pltpu.roll(mean_r, 4, 0), scaled)
        net[r + 1] = to_cells(lon_shifts(jnp.concatenate([both, field[r, 8:24]], axis=0)))

    each(ROWS, enter, 4)

    n3, u3 = CHUNK["one"]

    def level_one(i):
        pre = mm(three_rows(net, n3 * i, n3), in_w)
        gate = jax.nn.sigmoid(pre)
        slope_a[pl.ds(n3 * i, n3)] = (gate * (1.0 + pre * (1.0 - gate))).reshape(n3, WIDE, HID1)
        act = (pre * gate).astype(BF).reshape(n3, WIDE, HID1)
        act_a[pl.ds(n3 * i, n3)] = act
        wide = act.astype(F32)
        for k in range(n3 // 2):
            row = (n3 // 2) * i + k
            pairs[row] = wide[2 * k] + wide[2 * k + 1]
            total = pairs[row, pl.ds(0, WLOW, stride=2)] + pairs[row, pl.ds(1, WLOW, stride=2)]
            pooled[row + 1] = (0.25 * total).astype(BF)

    each(ROWS // n3, level_one, u3)
    down_w = jnp.concatenate([w_down[a] for a in range(3)], axis=1)

    n4, u4 = CHUNK["two"]

    def level_two(i):
        pre = lon_sum(mm_nt(three_rows(pooled, n4 * i, n4), down_w), n4, WLOW, HID2)
        gate = jax.nn.sigmoid(pre)
        slope_b[pl.ds(n4 * i, n4)] = gate * (1.0 + pre * (1.0 - gate))
        act_b[pl.ds(n4 * i, n4)] = (pre * gate).astype(BF)

    each(LOW // n4, level_two, u4)
    n5, u5 = CHUNK["up"]

    def up_products(i):
        low = act_b[pl.ds(n5 * i, n5)].reshape(n5 * WLOW, HID2)
        up_taps[pl.ds(n5 * i + 1, n5)] = mm_nt(low, w_up[...]).reshape(n5, WLOW, 9 * HID1)

    each(LOW // n5, up_products, u5)

    def level_three(i):
        for pi in range(2):
            sums = []
            for b in range(3):
                total = None
                for a in range(3):
                    row = i + 1 + (pi + a - 1) // 2
                    at = (a * 3 + b) * HID1
                    part = up_taps[row, :, at : at + HID1]
                    total = part if total is None else total + part
                sums.append(total)
            row = 2 * i + pi
            phases[row, pl.ds(0, WLOW, stride=2)] = ahead(sums[0], 0) + sums[1] + sums[2]
            phases[row, pl.ds(1, WLOW, stride=2)] = sums[0] + sums[1] + back(sums[2], 0)
            pre = phases[row]
            gate = jax.nn.sigmoid(pre)
            act_c[row] = (pre * gate + act_a[row].astype(F32)).astype(BF)
            slope_c[row] = gate * (1.0 + pre * (1.0 - gate))

    each(LOW, level_three, CHUNK["three"])
    out_w = stack_outputs(stack_o, w_out)

    def field_taps(r):
        taps[r + 1] = mm_nt(out_w[0:72], to_lanes(act_c[r]))

    each(ROWS, field_taps, 4)

    def loss(i):
        for k in range(2):
            r = 2 * i + k
            value = four_channels(taps, r)
            sigma = jnp.where(held, jnp.broadcast_to(field[r, 1:2], (8, LANES)), 1.0)
            weight = jnp.broadcast_to(field[r, 0:1], (8, LANES))
            variance = sigma * sigma + 0.25
            c_out = 0.5 * sigma * lax.rsqrt(variance)
            lam = variance / (0.25 * sigma * sigma)
            denoised = (0.25 / variance) * noisies[r] + c_out * value
            den[i, 4 * k : 4 * k + 4] = denoised[4:8, :OWN]
            loss_grad = (2.0 * scale) * weight * lam * (denoised - residuals[r])
            cot = (c_out * loss_grad).astype(BF).astype(F32)
            grad_f[r + 1] = jnp.where(low_half, 0.0, cot)

    each(LOW, loss, 2)
    tiles[...] = den[...].astype(BF)
    last_sum[...] = jnp.zeros_like(last_sum)

    def last_grads(r):
        parts = []
        for a in range(3):
            cot = grad_f[r + 2 - a]
            parts += [back(cot, 1), cot, ahead(cot, 1)]
        cots = jnp.concatenate(parts + [jnp.zeros((8, LANES), F32)], axis=0)
        last_sum[...] += mm(cots[:, :OWN].astype(BF), act_c[r, 0:OWN])
        spread_f[r] = to_cells(cots)

    each(ROWS, last_grads, 4)
    near, far = place[0], 1 - place[0]

    def keep(half, at, value):
        grads[pl.ds(half, 1), at : at + value.shape[0]] = value.astype(BF)[None]

    keep(near, BIG_ROWS, last_sum[0:LAST_ROWS])
    keep(near, BIG_ROWS + LAST_ROWS, jnp.zeros((HALF_ROWS - BIG_ROWS - LAST_ROWS, OWN), F32))

    n6, u6 = CHUNK["back_three"]

    def back_three(i):
        wide = mm(spread_f[pl.ds(n6 * i, n6)].reshape(n6 * WIDE, OWN), out_w)
        wide = wide.reshape(n6, WIDE, HID1)
        back_c[pl.ds(n6 * i, n6)] = wide
        grad_c[pl.ds(n6 * i + 1, n6)] = wide * slope_c[pl.ds(n6 * i, n6)]

    each(ROWS // n6, back_three, u6)

    def block_sums(i):
        even = [grad_c[2 * i + k, pl.ds(0, WLOW, stride=2)] for k in range(4)]
        odd = [grad_c[2 * i + k, pl.ds(1, WLOW, stride=2)] for k in range(4)]
        for a in range(3):
            e, o = even[2 - a] + even[3 - a], odd[2 - a] + odd[3 - a]
            for b, total in enumerate((o + back(e, 0), e + o, ahead(o, 0) + e)):
                at = (a * 3 + b) * HID1
                blocks[i, :, at : at + HID1] = total.astype(BF)

    each(LOW, block_sums, CHUNK["blocks"])

    n7, u7 = CHUNK["back_two"]

    def back_two(i):
        low = mm(blocks[pl.ds(n7 * i, n7)].reshape(n7 * WLOW, 9 * HID1), w_up[...])
        cot = low.reshape(n7, WLOW, HID2) * slope_b[pl.ds(n7 * i, n7)]
        shifts = jnp.concatenate([back(cot, 1), cot, ahead(cot, 1)], axis=2)
        grad_b[pl.ds(n7 * i + 1, n7)] = shifts.astype(BF)

    each(LOW // n7, back_two, u7)
    held_low = OWN // 2
    cells = LOW * held_low
    low_b = act_b[:, :held_low].reshape(cells, HID2)
    for k in range(3):
        at = 3 * HID1 * k
        up = mm_tn(blocks[:, :held_low, at : at + 3 * HID1].reshape(cells, 3 * HID1), low_b)
        keep(near, at, up[:, :HID1])
        keep(near, at + UP_ROWS, up[:, HID1:])
    low_a = jnp.concatenate(
        [pooled[a : a + LOW, :held_low].reshape(cells, HID1) for a in range(3)], axis=1
    )
    for b in range(3):
        at = HID2 * b
        down = mm_tn(grad_b[1 : LOW + 1, :held_low, at : at + HID2].reshape(cells, HID2), low_a)
        for a in range(3):
            keep(far, (a * 3 + b) * HID2, down[:, HID1 * a : HID1 * (a + 1)])
    n8, u8 = CHUNK["back_one"]

    def back_one(i):
        total = None
        for a in range(3):
            cot = grad_b[pl.ds(n8 * i + 2 - a, n8)].reshape(n8 * WLOW, 3 * HID2)
            part = mm(cot, w_down[a])
            total = part if total is None else total + part
        low = (0.25 * total).reshape(n8, WLOW, HID1)
        for k in range(n8):
            row = n8 * i + k
            phases[row, pl.ds(0, WLOW, stride=2)] = low[k]
            phases[row, pl.ds(1, WLOW, stride=2)] = low[k]
            spread = phases[row, 0:OWN]
            for pi in range(2):
                r = 2 * row + pi
                grad_a[r] = ((back_c[r, 0:OWN] + spread) * slope_a[r, 0:OWN]).astype(BF)

    each(LOW // n8, back_one, u8)
    near_cells = jnp.concatenate(
        [net[a : a + ROWS, :OWN].reshape(ROWS * OWN, OWN) for a in range(3)], axis=1
    )
    inputs = mm_tn(grad_a[...].reshape(ROWS * OWN, HID1), near_cells)
    for a in range(3):
        part = inputs[:, a * OWN : (a + 1) * OWN].T
        keep(far, BIG_ROWS + a * 3 * FIELDS, part[: 3 * FIELDS])
    keep(far, BIG_ROWS + IN_ROWS, jnp.zeros((HALF_ROWS - BIG_ROWS - IN_ROWS, OWN), F32))


def unpack_kernel(place, mine, other, tiles, tile, first, down, up, last):
    a = pl.program_id(0)
    even = place[0] == 0

    def half(k, at, count):
        rows = pl.ds(pl.multiple_of(at, 8), count)
        if k == 0:
            return jnp.where(even, mine[rows].astype(F32), other[rows].astype(F32))
        return jnp.where(even, other[rows].astype(F32), mine[rows].astype(F32))

    low = half(0, a * (3 * HID1), 3 * HID1).reshape(3, HID1, HID1)
    high = half(0, a * (3 * HID1) + UP_ROWS, 3 * HID1).reshape(3, HID1, HID1)
    up[0] = jnp.concatenate([low, high], axis=2)
    down[0] = half(1, a * (3 * HID2), 3 * HID2).reshape(3, HID2, HID1)
    firsts = half(1, BIG_ROWS + a * (3 * FIELDS), 3 * FIELDS)
    lasts = half(0, BIG_ROWS + a * FIELDS, FIELDS)
    for b in range(3):
        first[0, b] = firsts[b * FIELDS : b * FIELDS + 20]
        last[0, b] = lasts[b * 8 + 4 : b * 8 + 8]

    @pl.when(a == 0)
    def _():
        blocks = tiles[...].astype(F32)
        for k in range(8):
            for r in range(2):
                tile[:, r, k * OWN : (k + 1) * OWN] = blocks[k, 4 * r : 4 * r + 4]


def in_vmem(count):
    return [pl.BlockSpec(memory_space=pltpu.MemorySpace.VMEM) for _ in range(count)]


def in_smem():
    return pl.BlockSpec(memory_space=pltpu.MemorySpace.SMEM)


def pack(target, noise, land_mask, level_index):
    lats = target.shape[2] // OWN
    return pl.pallas_call(
        pack_kernel,
        out_shape=jax.ShapeDtypeStruct((lats, 2, 16, OWN), F32),
        in_specs=in_vmem(4),
        out_specs=in_vmem(1)[0],
        name="pack",
    )(target, noise, land_mask, level_index)


def step(scale, *operands):
    def kernel(*refs):
        step_kernel(scale, *refs)

    return pl.pallas_call(
        kernel,
        out_shape=(
            jax.ShapeDtypeStruct((2, HALF_ROWS, OWN), BF),
            jax.ShapeDtypeStruct((LOW, CELL_ROWS, OWN), BF),
        ),
        in_specs=[in_smem(), *in_vmem(10)],
        out_specs=tuple(in_vmem(2)),
        scratch_shapes=[
            pltpu.VMEM((3, OWN, OWN), F32),
            pltpu.VMEM((OWN, OWN), F32),
            pltpu.VMEM((ROWS, FIELDS, LANES), F32),
            pltpu.VMEM((ROWS + 2, WIDE, OWN), BF),
            pltpu.VMEM((ROWS + 2, WIDE, HID1), BF),
            pltpu.VMEM((ROWS, WIDE, HID1), BF),
            pltpu.VMEM((ROWS + 2, 72, LANES), F32),
            pltpu.VMEM((ROWS, 8, LANES), F32),
            pltpu.VMEM((ROWS, 8, LANES), F32),
            pltpu.VMEM((ROWS, WIDE, HID1), F32),
            pltpu.VMEM((ROWS, WIDE, HID1), BF),
            pltpu.VMEM((LOW, WIDE, HID1), F32),
            pltpu.VMEM((LOW + 2, WLOW, HID1), BF),
            pltpu.VMEM((LOW, WLOW, HID2), BF),
            pltpu.VMEM((LOW, WLOW, HID2), F32),
            pltpu.VMEM((LOW + 2, WLOW, 9 * HID1), F32),
            pltpu.VMEM((ROWS, WIDE, HID1), F32),
            pltpu.VMEM((ROWS, WIDE, HID1), F32),
            pltpu.VMEM((ROWS + 2, 8, LANES), F32),
            pltpu.VMEM((ROWS, WIDE, OWN), BF),
            pltpu.VMEM((ROWS, WIDE, HID1), F32),
            pltpu.VMEM((ROWS + 2, WIDE, HID1), F32),
            pltpu.VMEM((LOW, WLOW, 9 * HID1), BF),
            pltpu.VMEM((LOW + 2, WLOW, 3 * HID2), BF),
            pltpu.VMEM((ROWS, OWN, HID1), BF),
            pltpu.VMEM((80, HID1), F32),
            pltpu.VMEM((LOW, CELL_ROWS, OWN), F32),
        ],
        name="step",
    )(*operands)


def unpack(place, mine, other, tiles):
    whole = pl.BlockSpec((HALF_ROWS, OWN), lambda a: (0, 0))
    cells = pl.BlockSpec((8, CELL_ROWS, OWN), lambda a: (0, 0, 0))

    def taps(rows, lanes):
        return pl.BlockSpec((1, 3, rows, lanes), lambda a: (a, 0, 0, 0))

    return pl.pallas_call(
        unpack_kernel,
        grid=(3,),
        out_shape=(
            jax.ShapeDtypeStruct((4, 2, 8 * OWN), F32),
            jax.ShapeDtypeStruct((3, 3, 20, HID1), F32),
            jax.ShapeDtypeStruct((3, 3, HID2, HID1), F32),
            jax.ShapeDtypeStruct((3, 3, HID1, HID2), F32),
            jax.ShapeDtypeStruct((3, 3, 4, HID1), F32),
        ),
        in_specs=[in_smem(), whole, whole, cells],
        out_specs=(
            pl.BlockSpec((4, 2, 8 * OWN), lambda a: (0, 0, 0)),
            taps(20, HID1),
            taps(HID2, HID1),
            taps(HID1, HID2),
            taps(4, HID1),
        ),
        name="unpack",
    )(place, mine, other, tiles)


def all_to_all(value, axes):
    return lax.all_to_all(value, axes, split_axis=0, concat_axis=0, tiled=True)


def shift_by(value, axes, step):
    count = lax.axis_size(axes)
    return lax.ppermute(value, axes, [(i, (i + step) % count) for i in range(count)])


def local(
    coarse,
    target,
    noise,
    land_mask,
    level_index,
    frozen_first,
    frozen_middle,
    frozen_last,
    diffuse_in,
    diffuse_down,
    diffuse_up,
    diffuse_out,
):
    scale = 1.0 / (target.shape[0] * math.sqrt(target.shape[1] * target.shape[2] * lax.axis_size(STRIPS)))
    place = lax.axis_index("core").astype(jnp.int32)[None]
    packed = all_to_all(pack(target, noise, land_mask, level_index), LAT).reshape(ROWS, 16, OWN)
    fields = jnp.concatenate([packed[:, :8], coarse.transpose(1, 0, 2).astype(F32), packed[:, 12:]], axis=1)
    grads, tiles = step(
        scale,
        place,
        fields,
        shift_by(fields, STRIPS, 1),
        shift_by(fields, STRIPS, -1),
        frozen_first.transpose(0, 1, 3, 2),
        frozen_middle.reshape(3, 3 * HID1, HID1),
        frozen_last,
        diffuse_in.transpose(0, 1, 3, 2),
        diffuse_down.reshape(3, 3 * HID2, HID1),
        diffuse_up.reshape(9 * HID1, HID2),
        diffuse_out,
    )
    chips = lax.axis_size(CHIPS)
    rows = HALF_ROWS // chips
    lats = tiles.shape[0]
    half = grads[0].astype(F32) + shift_by(grads[1], "core", 1).astype(F32)
    blocks = jnp.broadcast_to(tiles[None], (chips // lats, *tiles.shape)).reshape(chips, CELL_ROWS, OWN)
    sent = jnp.concatenate([half.astype(BF).reshape(chips, rows, OWN), blocks], axis=1)
    parts = all_to_all(sent, CHIPS)
    total = parts[:, :rows].astype(F32).sum(0).astype(BF)
    seats = parts.reshape(chips // lats, lats, rows + CELL_ROWS, OWN)[:, :, rows:]
    tiles = lax.dynamic_index_in_dim(seats, lax.axis_index(("y", "x_hi")), 0, False)
    with jax.named_scope("spread"):
        mine = all_to_all(jnp.broadcast_to(total[None], (chips, rows, OWN)), CHIPS).reshape(HALF_ROWS, OWN)
    tile, first, down, up, last = unpack(place, mine, shift_by(mine, "core", 1), tiles)
    return (tile, first.transpose(0, 1, 3, 2), down, up, last)


def solution(mesh):
    fine = Mesh(mesh.devices.reshape(4, 2, 2, 2, 4), LON + LAT)
    tile = P(None, LAT, LON)
    return jax.shard_map(
        local,
        mesh=fine,
        in_specs=(
            P(None, None, STRIPS),
            tile,
            tile,
            P(LAT, LON),
            P(LAT, LON),
            *([P()] * 7),
        ),
        out_specs=(tile, P(), P(), P(), P()),
        check_vma=False,
    )
```

```python
import math

import jax
import jax.numpy as jnp
from jax import lax
from jax.experimental import pallas as pl
from jax.experimental.pallas import tpu as pltpu
from jax.sharding import Mesh
from jax.sharding import PartitionSpec as P

LEVELS = 32
ROWS = 16
LOW = ROWS // 2
OWN = 128
HALO = 16
WIDE = OWN + 2 * HALO
WLOW = WIDE // 2
LANES = 256
HID1 = 128
HID2 = 256
BF = jnp.bfloat16
F32 = jnp.float32

LON = ("y", "x_hi", "core")
LAT = ("x_lo", "z")
CHIPS = ("y", "x_hi", "x_lo", "z")
STRIPS = LON + LAT

FIELDS = 24
UP_ROWS = 9 * HID1
DOWN_ROWS = 9 * HID2
BIG_ROWS = 2304
LAST_ROWS = 72
IN_ROWS = 9 * FIELDS
HALF_ROWS = 2560
CELL_ROWS = 8
CHUNK = {
    "first": (8, 1),
    "second": (4, 2),
    "one": (8, 1),
    "two": (4, 2),
    "up": (8, 1),
    "back_three": (8, 1),
    "back_two": (2, 2),
    "back_one": (4, 1),
    "three": 2,
    "blocks": 4,
}
EDGE_ROWS = OWN // HALO


def mm(x, w):
    return lax.dot_general(x, w, (((1,), (0,)), ((), ())), preferred_element_type=F32)


def mm_nt(x, w):
    return lax.dot_general(x, w, (((1,), (1,)), ((), ())), preferred_element_type=F32)


def mm_tn(x, w):
    return lax.dot_general(x, w, (((0,), (0,)), ((), ())), preferred_element_type=F32)


def back(x, axis):
    return pltpu.roll(x, x.shape[axis] - 1, axis)


def ahead(x, axis):
    return pltpu.roll(x, 1, axis)


def with_halo(own, left, right):
    lane = lax.broadcasted_iota(jnp.int32, own.shape, 1)
    halo = jnp.where(lane < HALO, right, jnp.where(lane >= OWN - HALO, left, 0.0))
    return jnp.concatenate([own, halo], axis=1)


def to_cells(stack):
    pad = OWN - stack.shape[0]
    if pad:
        stack = jnp.concatenate([stack, jnp.zeros((pad, LANES), F32)], axis=0)
    cells = stack.T
    return jnp.concatenate([cells[: OWN + HALO], cells[LANES - HALO :]], axis=0).astype(BF)


def to_lanes(cells):
    gap = jnp.zeros((LANES - WIDE, cells.shape[1]), cells.dtype)
    return jnp.concatenate([cells[: OWN + HALO], gap, cells[OWN + HALO :]], axis=0)


def lon_shifts(field):
    return jnp.concatenate([ahead(field, 1), field, back(field, 1)], axis=0)


def three_rows(ref, start, count):
    width = ref.shape[1]
    return jnp.concatenate(
        [ref[pl.ds(start + a, count)].reshape(count * width, ref.shape[2]) for a in range(3)], axis=1
    )


def lon_sum(taps, count, width, out):
    first, second, third = (
        taps[:, b * out : (b + 1) * out].reshape(count, width, out) for b in range(3)
    )
    return ahead(first, 1) + second + back(third, 1)


def four_channels(ref, row):
    sums = []
    for b in range(3):
        at = [(a * 3 + b) * 8 for a in range(3)]
        sums.append(
            ref[row, at[0] : at[0] + 8]
            + ref[row + 1, at[1] : at[1] + 8]
            + ref[row + 2, at[2] : at[2] + 8]
        )
    return ahead(sums[0], 1) + sums[1] + back(sums[2], 1)


def zero_edges(ref):
    edge = jnp.zeros(ref.shape[1:], ref.dtype)
    ref[0] = edge
    ref[ref.shape[0] - 1] = edge


def each(count, body, unroll=1):
    def step(i, carry):
        body(i)
        return carry

    lax.fori_loop(0, count, step, 0, unroll=unroll)


def pack_kernel(target, noise, land_mask, level, packed):
    power = level[...].astype(F32) / (LEVELS - 1)
    sigma = jnp.broadcast_to(0.02 * jnp.exp(power * math.log(4000.0)), (1, OWN))
    weight = 1.0 + land_mask[...].astype(F32)
    for p in range(packed.shape[0]):
        lanes = slice(p * OWN, (p + 1) * OWN)
        for r in range(2):
            packed[p, r, 0:1] = weight[r : r + 1, lanes]
            packed[p, r, 1:2] = sigma
            packed[p, r, 2:4] = jnp.zeros((2, OWN), F32)
            packed[p, r, 4:8] = target[:, r, lanes]
            packed[p, r, 8:12] = jnp.zeros((4, OWN), F32)
            packed[p, r, 12:16] = noise[:, r, lanes]


def edges_kernel(packed, coarse, fields, first_columns, last_columns):
    lane = lax.broadcasted_iota(jnp.int32, (FIELDS, OWN), 1)
    for g in range(ROWS // EDGE_ROWS):
        firsts = lasts = jnp.zeros((FIELDS, OWN), F32)
        for j in range(EDGE_ROWS):
            r = g * EDGE_ROWS + j
            fields[r, 0:8] = packed[r, 0:8]
            fields[r, 8:20] = coarse[r]
            fields[r, 20:24] = packed[r, 12:16]
            row = fields[r]
            here = (lane >= j * HALO) & (lane < (j + 1) * HALO)
            at = j * HALO
            firsts = jnp.where(here, pltpu.roll(row, at, 1) if at else row, firsts)
            at = (j + 1) * HALO % OWN
            lasts = jnp.where(here, pltpu.roll(row, at, 1) if at else row, lasts)
        first_columns[g] = firsts
        last_columns[g] = lasts


def stack_inputs(ref, weight, room):
    ref[...] = jnp.zeros_like(ref)
    count = weight.shape[2]
    for a in range(3):
        for b in range(3):
            ref[a, b * room : b * room + count] = weight[a, b].astype(F32)
    return ref[...].astype(BF).reshape(3 * OWN, OWN)


def stack_outputs(ref, weight):
    ref[...] = jnp.zeros_like(ref)
    for a in range(3):
        for b in range(3):
            at = (a * 3 + b) * 8 + 4
            ref[at : at + 4] = weight[a, b].astype(F32)
    return ref[...].astype(BF)


def step_kernel(
    scale,
    place,
    own,
    left,
    right,
    w_first,
    w_middle,
    w_last,
    w_in,
    w_down,
    w_up,
    w_out,
    mine,
    other,
    tiles,
    *scratch,
):
    (
        stack,
        stack_o,
        field,
        net,
        hid,
        act_c,
        taps,
        residuals,
        noisies,
        slope_a,
        act_a,
        pairs,
        pooled,
        act_b,
        slope_b,
        up_taps,
        phases,
        slope_c,
        grad_f,
        spread_f,
        back_c,
        grad_c,
        blocks,
        grad_b,
        grad_a,
        last_sum,
        den,
        halves,
        sems,
    ) = scratch
    for ref in (net, hid, pooled, up_taps, taps, grad_f, grad_c, grad_b):
        zero_edges(ref)
    first_w = stack_inputs(stack, w_first, 16)

    def gather(g):
        from_left, from_right = left[g], right[g]
        for j in range(EDGE_ROWS):
            r = g * EDGE_ROWS + j
            at = OWN - HALO - j * HALO
            before = pltpu.roll(from_left, at, 1) if at else from_left
            after = pltpu.roll(from_right, OWN - j * HALO, 1) if j else from_right
            wide = with_halo(own[r], before, after)
            field[r] = wide
            net[r + 1] = to_cells(lon_shifts(wide[8:24]))

    each(ROWS // EDGE_ROWS, gather)

    n1, u1 = CHUNK["first"]

    def first(i):
        pre = mm(three_rows(net, n1 * i, n1), first_w)
        hid[pl.ds(n1 * i + 1, n1)] = jax.nn.silu(pre).astype(BF).reshape(n1, WIDE, HID1)

    each(ROWS // n1, first, u1)
    middle_w = jnp.concatenate([w_middle[a] for a in range(3)], axis=1)

    n2, u2 = CHUNK["second"]

    def second(i):
        pre = lon_sum(mm_nt(three_rows(hid, n2 * i, n2), middle_w), n2, WIDE, HID1)
        act_c[pl.ds(n2 * i, n2)] = jax.nn.silu(pre).astype(BF)

    each(ROWS // n2, second, u2)
    last_w = stack_outputs(stack_o, w_last)[0:72]

    def mean_taps(r):
        taps[r + 1] = mm_nt(last_w, to_lanes(act_c[r]))

    each(ROWS, mean_taps, 4)
    in_w = stack_inputs(stack, w_in, FIELDS)
    lane = lax.broadcasted_iota(jnp.int32, (8, LANES), 1)
    held = (lane < OWN + HALO) | (lane >= LANES - HALO)
    low_half = lax.broadcasted_iota(jnp.int32, (8, LANES), 0) < 4

    def enter(r):
        mean_r = four_channels(taps, r).astype(BF).astype(F32)
        sigma = jnp.where(held, jnp.broadcast_to(field[r, 1:2], (8, LANES)), 1.0)
        residual = field[r, 0:8] - mean_r
        noisy = residual + sigma * field[r, 16:24]
        variance = sigma * sigma + 0.25
        residuals[r] = residual
        noisies[r] = noisy
        scaled = (lax.rsqrt(variance) * noisy).astype(BF).astype(F32)
        both = jnp.where(low_half, pltpu.roll(mean_r, 4, 0), scaled)
        net[r + 1] = to_cells(lon_shifts(jnp.concatenate([both, field[r, 8:24]], axis=0)))

    each(ROWS, enter, 4)

    n3, u3 = CHUNK["one"]

    def level_one(i):
        pre = mm(three_rows(net, n3 * i, n3), in_w)
        gate = jax.nn.sigmoid(pre)
        slope_a[pl.ds(n3 * i, n3)] = (gate * (1.0 + pre * (1.0 - gate))).reshape(n3, WIDE, HID1)
        act = (pre * gate).astype(BF).reshape(n3, WIDE, HID1)
        act_a[pl.ds(n3 * i, n3)] = act
        wide = act.astype(F32)
        for k in range(n3 // 2):
            row = (n3 // 2) * i + k
            pairs[row] = wide[2 * k] + wide[2 * k + 1]
            total = pairs[row, pl.ds(0, WLOW, stride=2)] + pairs[row, pl.ds(1, WLOW, stride=2)]
            pooled[row + 1] = (0.25 * total).astype(BF)

    each(ROWS // n3, level_one, u3)
    down_w = jnp.concatenate([w_down[a] for a in range(3)], axis=1)

    n4, u4 = CHUNK["two"]

    def level_two(i):
        pre = lon_sum(mm_nt(three_rows(pooled, n4 * i, n4), down_w), n4, WLOW, HID2)
        gate = jax.nn.sigmoid(pre)
        slope_b[pl.ds(n4 * i, n4)] = gate * (1.0 + pre * (1.0 - gate))
        act_b[pl.ds(n4 * i, n4)] = (pre * gate).astype(BF)

    each(LOW // n4, level_two, u4)
    n5, u5 = CHUNK["up"]

    def up_products(i):
        low = act_b[pl.ds(n5 * i, n5)].reshape(n5 * WLOW, HID2)
        up_taps[pl.ds(n5 * i + 1, n5)] = mm_nt(low, w_up[...]).reshape(n5, WLOW, 9 * HID1)

    each(LOW // n5, up_products, u5)

    def level_three(i):
        for pi in range(2):
            sums = []
            for b in range(3):
                total = None
                for a in range(3):
                    row = i + 1 + (pi + a - 1) // 2
                    at = (a * 3 + b) * HID1
                    part = up_taps[row, :, at : at + HID1]
                    total = part if total is None else total + part
                sums.append(total)
            row = 2 * i + pi
            phases[row, pl.ds(0, WLOW, stride=2)] = ahead(sums[0], 0) + sums[1] + sums[2]
            phases[row, pl.ds(1, WLOW, stride=2)] = sums[0] + sums[1] + back(sums[2], 0)
            pre = phases[row]
            gate = jax.nn.sigmoid(pre)
            act_c[row] = (pre * gate + act_a[row].astype(F32)).astype(BF)
            slope_c[row] = gate * (1.0 + pre * (1.0 - gate))

    each(LOW, level_three, CHUNK["three"])
    out_w = stack_outputs(stack_o, w_out)

    def field_taps(r):
        taps[r + 1] = mm_nt(out_w[0:72], to_lanes(act_c[r]))

    each(ROWS, field_taps, 4)

    def loss(i):
        for k in range(2):
            r = 2 * i + k
            value = four_channels(taps, r)
            sigma = jnp.where(held, jnp.broadcast_to(field[r, 1:2], (8, LANES)), 1.0)
            weight = jnp.broadcast_to(field[r, 0:1], (8, LANES))
            variance = sigma * sigma + 0.25
            c_out = 0.5 * sigma * lax.rsqrt(variance)
            lam = variance / (0.25 * sigma * sigma)
            denoised = (0.25 / variance) * noisies[r] + c_out * value
            den[i, 4 * k : 4 * k + 4] = denoised[4:8, :OWN]
            loss_grad = (2.0 * scale) * weight * lam * (denoised - residuals[r])
            cot = (c_out * loss_grad).astype(BF).astype(F32)
            grad_f[r + 1] = jnp.where(low_half, 0.0, cot)

    each(LOW, loss, 2)
    tiles[...] = den[...].astype(BF)
    last_sum[...] = jnp.zeros_like(last_sum)

    def last_grads(r):
        parts = []
        for a in range(3):
            cot = grad_f[r + 2 - a]
            parts += [back(cot, 1), cot, ahead(cot, 1)]
        cots = jnp.concatenate(parts + [jnp.zeros((8, LANES), F32)], axis=0)
        last_sum[...] += mm(cots[:, :OWN].astype(BF), act_c[r, 0:OWN])
        spread_f[r] = to_cells(cots)

    each(ROWS, last_grads, 4)
    near, far = 0, 1

    def keep(half, at, value):
        halves[half, at : at + value.shape[0]] = value.astype(BF)

    def send(half):
        for core, target in ((half, mine), (1 - half, other)):

            @pl.when(place[0] == core)
            def _():
                pltpu.make_async_copy(halves.at[half], target, sems.at[half]).start()

    keep(near, BIG_ROWS, last_sum[0:LAST_ROWS])
    keep(near, BIG_ROWS + LAST_ROWS, jnp.zeros((HALF_ROWS - BIG_ROWS - LAST_ROWS, OWN), F32))

    n6, u6 = CHUNK["back_three"]

    def back_three(i):
        wide = mm(spread_f[pl.ds(n6 * i, n6)].reshape(n6 * WIDE, OWN), out_w)
        wide = wide.reshape(n6, WIDE, HID1)
        back_c[pl.ds(n6 * i, n6)] = wide
        grad_c[pl.ds(n6 * i + 1, n6)] = wide * slope_c[pl.ds(n6 * i, n6)]

    each(ROWS // n6, back_three, u6)

    def block_sums(i):
        even = [grad_c[2 * i + k, pl.ds(0, WLOW, stride=2)] for k in range(4)]
        odd = [grad_c[2 * i + k, pl.ds(1, WLOW, stride=2)] for k in range(4)]
        for a in range(3):
            e, o = even[2 - a] + even[3 - a], odd[2 - a] + odd[3 - a]
            for b, total in enumerate((o + back(e, 0), e + o, ahead(o, 0) + e)):
                at = (a * 3 + b) * HID1
                blocks[i, :, at : at + HID1] = total.astype(BF)

    each(LOW, block_sums, CHUNK["blocks"])

    n7, u7 = CHUNK["back_two"]

    def back_two(i):
        low = mm(blocks[pl.ds(n7 * i, n7)].reshape(n7 * WLOW, 9 * HID1), w_up[...])
        cot = low.reshape(n7, WLOW, HID2) * slope_b[pl.ds(n7 * i, n7)]
        shifts = jnp.concatenate([back(cot, 1), cot, ahead(cot, 1)], axis=2)
        grad_b[pl.ds(n7 * i + 1, n7)] = shifts.astype(BF)

    each(LOW // n7, back_two, u7)
    held_low = OWN // 2
    cells = LOW * held_low
    low_b = act_b[:, :held_low].reshape(cells, HID2)
    for k in range(3):
        at = 3 * HID1 * k
        up = mm_tn(blocks[:, :held_low, at : at + 3 * HID1].reshape(cells, 3 * HID1), low_b)
        keep(near, at, up[:, :HID1])
        keep(near, at + UP_ROWS, up[:, HID1:])
    send(near)
    low_a = jnp.concatenate(
        [pooled[a : a + LOW, :held_low].reshape(cells, HID1) for a in range(3)], axis=1
    )
    for b in range(3):
        at = HID2 * b
        down = mm_tn(grad_b[1 : LOW + 1, :held_low, at : at + HID2].reshape(cells, HID2), low_a)
        for a in range(3):
            keep(far, (a * 3 + b) * HID2, down[:, HID1 * a : HID1 * (a + 1)])
    n8, u8 = CHUNK["back_one"]

    def back_one(i):
        total = None
        for a in range(3):
            cot = grad_b[pl.ds(n8 * i + 2 - a, n8)].reshape(n8 * WLOW, 3 * HID2)
            part = mm(cot, w_down[a])
            total = part if total is None else total + part
        low = (0.25 * total).reshape(n8, WLOW, HID1)
        for k in range(n8):
            row = n8 * i + k
            phases[row, pl.ds(0, WLOW, stride=2)] = low[k]
            phases[row, pl.ds(1, WLOW, stride=2)] = low[k]
            spread = phases[row, 0:OWN]
            for pi in range(2):
                r = 2 * row + pi
                grad_a[r] = ((back_c[r, 0:OWN] + spread) * slope_a[r, 0:OWN]).astype(BF)

    each(LOW // n8, back_one, u8)
    near_cells = jnp.concatenate(
        [net[a : a + ROWS, :OWN].reshape(ROWS * OWN, OWN) for a in range(3)], axis=1
    )
    inputs = mm_tn(grad_a[...].reshape(ROWS * OWN, HID1), near_cells)
    for a in range(3):
        part = inputs[:, a * OWN : (a + 1) * OWN].T
        keep(far, BIG_ROWS + a * 3 * FIELDS, part[: 3 * FIELDS])
    keep(far, BIG_ROWS + IN_ROWS, jnp.zeros((HALF_ROWS - BIG_ROWS - IN_ROWS, OWN), F32))
    send(far)
    for half in (near, far):
        pltpu.make_async_copy(halves.at[half], mine, sems.at[half]).wait()


def unpack_kernel(place, mine, other, tiles, tile, first, down, up, last):
    a = pl.program_id(0)
    even = place[0] == 0

    def half(k, at, count):
        rows = pl.ds(pl.multiple_of(at, 8), count)
        if k == 0:
            return jnp.where(even, mine[rows].astype(F32), other[rows].astype(F32))
        return jnp.where(even, other[rows].astype(F32), mine[rows].astype(F32))

    low = half(0, a * (3 * HID1), 3 * HID1).reshape(3, HID1, HID1)
    high = half(0, a * (3 * HID1) + UP_ROWS, 3 * HID1).reshape(3, HID1, HID1)
    up[0] = jnp.concatenate([low, high], axis=2)
    down[0] = half(1, a * (3 * HID2), 3 * HID2).reshape(3, HID2, HID1)
    firsts = half(1, BIG_ROWS + a * (3 * FIELDS), 3 * FIELDS)
    lasts = half(0, BIG_ROWS + a * FIELDS, FIELDS)
    for b in range(3):
        first[0, b] = firsts[b * FIELDS : b * FIELDS + 20]
        last[0, b] = lasts[b * 8 + 4 : b * 8 + 8]

    @pl.when(a == 0)
    def _():
        blocks = tiles[...].astype(F32)
        for k in range(8):
            for r in range(2):
                tile[:, r, k * OWN : (k + 1) * OWN] = blocks[k, 4 * r : 4 * r + 4]


def in_vmem(count):
    return [pl.BlockSpec(memory_space=pltpu.MemorySpace.VMEM) for _ in range(count)]


def in_smem():
    return pl.BlockSpec(memory_space=pltpu.MemorySpace.SMEM)


def pack(target, noise, land_mask, level_index):
    lats = target.shape[2] // OWN
    return pl.pallas_call(
        pack_kernel,
        out_shape=jax.ShapeDtypeStruct((lats, 2, 16, OWN), F32),
        in_specs=in_vmem(4),
        out_specs=in_vmem(1)[0],
        name="pack",
    )(target, noise, land_mask, level_index)


def edges(packed, coarse):
    columns = jax.ShapeDtypeStruct((ROWS // EDGE_ROWS, FIELDS, OWN), F32)
    return pl.pallas_call(
        edges_kernel,
        out_shape=(jax.ShapeDtypeStruct((ROWS, FIELDS, OWN), F32), columns, columns),
        in_specs=in_vmem(2),
        out_specs=tuple(in_vmem(3)),
        name="edges",
    )(packed, coarse)


def step(scale, *operands):
    def kernel(*refs):
        step_kernel(scale, *refs)

    return pl.pallas_call(
        kernel,
        out_shape=(
            jax.ShapeDtypeStruct((HALF_ROWS, OWN), BF),
            jax.ShapeDtypeStruct((HALF_ROWS, OWN), BF),
            jax.ShapeDtypeStruct((LOW, CELL_ROWS, OWN), BF),
        ),
        in_specs=[in_smem(), *in_vmem(10)],
        out_specs=(*[pl.BlockSpec(memory_space=pl.ANY)] * 2, *in_vmem(1)),
        scratch_shapes=[
            pltpu.VMEM((3, OWN, OWN), F32),
            pltpu.VMEM((OWN, OWN), F32),
            pltpu.VMEM((ROWS, FIELDS, LANES), F32),
            pltpu.VMEM((ROWS + 2, WIDE, OWN), BF),
            pltpu.VMEM((ROWS + 2, WIDE, HID1), BF),
            pltpu.VMEM((ROWS, WIDE, HID1), BF),
            pltpu.VMEM((ROWS + 2, 72, LANES), F32),
            pltpu.VMEM((ROWS, 8, LANES), F32),
            pltpu.VMEM((ROWS, 8, LANES), F32),
            pltpu.VMEM((ROWS, WIDE, HID1), F32),
            pltpu.VMEM((ROWS, WIDE, HID1), BF),
            pltpu.VMEM((LOW, WIDE, HID1), F32),
            pltpu.VMEM((LOW + 2, WLOW, HID1), BF),
            pltpu.VMEM((LOW, WLOW, HID2), BF),
            pltpu.VMEM((LOW, WLOW, HID2), F32),
            pltpu.VMEM((LOW + 2, WLOW, 9 * HID1), F32),
            pltpu.VMEM((ROWS, WIDE, HID1), F32),
            pltpu.VMEM((ROWS, WIDE, HID1), F32),
            pltpu.VMEM((ROWS + 2, 8, LANES), F32),
            pltpu.VMEM((ROWS, WIDE, OWN), BF),
            pltpu.VMEM((ROWS, WIDE, HID1), F32),
            pltpu.VMEM((ROWS + 2, WIDE, HID1), F32),
            pltpu.VMEM((LOW, WLOW, 9 * HID1), BF),
            pltpu.VMEM((LOW + 2, WLOW, 3 * HID2), BF),
            pltpu.VMEM((ROWS, OWN, HID1), BF),
            pltpu.VMEM((80, HID1), F32),
            pltpu.VMEM((LOW, CELL_ROWS, OWN), F32),
            pltpu.VMEM((2, HALF_ROWS, OWN), BF),
            pltpu.SemaphoreType.DMA((2,)),
        ],
        name="step",
    )(*operands)


def unpack(place, mine, other, tiles):
    whole = pl.BlockSpec((HALF_ROWS, OWN), lambda a: (0, 0))
    cells = pl.BlockSpec((8, CELL_ROWS, OWN), lambda a: (0, 0, 0))

    def taps(rows, lanes):
        return pl.BlockSpec((1, 3, rows, lanes), lambda a: (a, 0, 0, 0))

    return pl.pallas_call(
        unpack_kernel,
        grid=(3,),
        out_shape=(
            jax.ShapeDtypeStruct((4, 2, 8 * OWN), F32),
            jax.ShapeDtypeStruct((3, 3, 20, HID1), F32),
            jax.ShapeDtypeStruct((3, 3, HID2, HID1), F32),
            jax.ShapeDtypeStruct((3, 3, HID1, HID2), F32),
            jax.ShapeDtypeStruct((3, 3, 4, HID1), F32),
        ),
        in_specs=[in_smem(), whole, whole, cells],
        out_specs=(
            pl.BlockSpec((4, 2, 8 * OWN), lambda a: (0, 0, 0)),
            taps(20, HID1),
            taps(HID2, HID1),
            taps(HID1, HID2),
            taps(4, HID1),
        ),
        name="unpack",
    )(place, mine, other, tiles)


def all_to_all(value, axes):
    return lax.all_to_all(value, axes, split_axis=0, concat_axis=0, tiled=True)


def shift_by(value, axes, step):
    count = lax.axis_size(axes)
    return lax.ppermute(value, axes, [(i, (i + step) % count) for i in range(count)])


def local(
    coarse,
    target,
    noise,
    land_mask,
    level_index,
    frozen_first,
    frozen_middle,
    frozen_last,
    diffuse_in,
    diffuse_down,
    diffuse_up,
    diffuse_out,
):
    scale = 1.0 / (target.shape[0] * math.sqrt(target.shape[1] * target.shape[2] * lax.axis_size(STRIPS)))
    place = lax.axis_index("core").astype(jnp.int32)[None]
    packed = all_to_all(pack(target, noise, land_mask, level_index), LAT).reshape(ROWS, 16, OWN)
    fields, first_columns, last_columns = edges(packed, coarse.transpose(1, 0, 2).astype(F32))
    grads, partner, tiles = step(
        scale,
        place,
        fields,
        shift_by(last_columns, STRIPS, 1),
        shift_by(first_columns, STRIPS, -1),
        frozen_first.transpose(0, 1, 3, 2),
        frozen_middle.reshape(3, 3 * HID1, HID1),
        frozen_last,
        diffuse_in.transpose(0, 1, 3, 2),
        diffuse_down.reshape(3, 3 * HID2, HID1),
        diffuse_up.reshape(9 * HID1, HID2),
        diffuse_out,
    )
    chips = lax.axis_size(CHIPS)
    rows = HALF_ROWS // chips
    lats = tiles.shape[0]
    half = grads.astype(F32) + shift_by(partner, "core", 1).astype(F32)
    blocks = jnp.broadcast_to(tiles[None], (chips // lats, *tiles.shape)).reshape(chips, CELL_ROWS, OWN)
    sent = jnp.concatenate([half.astype(BF).reshape(chips, rows, OWN), blocks], axis=1)
    parts = all_to_all(sent, CHIPS)
    total = parts[:, :rows].astype(F32).sum(0).astype(BF)
    seats = parts.reshape(chips // lats, lats, rows + CELL_ROWS, OWN)[:, :, rows:]
    tiles = lax.dynamic_index_in_dim(seats, lax.axis_index(("y", "x_hi")), 0, False)
    with jax.named_scope("spread"):
        mine = all_to_all(jnp.broadcast_to(total[None], (chips, rows, OWN)), CHIPS).reshape(HALF_ROWS, OWN)
    tile, first, down, up, last = unpack(place, mine, shift_by(mine, "core", 1), tiles)
    return (tile, first.transpose(0, 1, 3, 2), down, up, last)


def solution(mesh):
    fine = Mesh(mesh.devices.reshape(4, 2, 2, 2, 4), LON + LAT)
    tile = P(None, LAT, LON)
    return jax.shard_map(
        local,
        mesh=fine,
        in_specs=(
            P(None, None, STRIPS),
            tile,
            tile,
            P(LAT, LON),
            P(LAT, LON),
            *([P()] * 7),
        ),
        out_specs=(tile, P(), P(), P(), P()),
        check_vma=False,
    )
```

```python
import math

import jax
import jax.numpy as jnp
from jax import lax
from jax.experimental import pallas as pl
from jax.experimental.pallas import tpu as pltpu
from jax.sharding import Mesh
from jax.sharding import PartitionSpec as P

LEVELS = 32
ROWS = 16
LOW = ROWS // 2
OWN = 128
HALO = 16
WIDE = OWN + 2 * HALO
WLOW = WIDE // 2
LANES = 256
HID1 = 128
HID2 = 256
BF = jnp.bfloat16
F32 = jnp.float32

LON = ("y", "x_hi", "core")
LAT = ("x_lo", "z")
CHIPS = ("y", "x_hi", "x_lo", "z")
STRIPS = LON + LAT

FIELDS = 24
UP_ROWS = 9 * HID1
DOWN_ROWS = 9 * HID2
BIG_ROWS = 2304
LAST_ROWS = 72
IN_ROWS = 9 * FIELDS
HALF_ROWS = 2560
CELL_ROWS = 8
CHUNK = {
    "first": (8, 1),
    "second": (4, 2),
    "one": (8, 1),
    "two": (4, 2),
    "up": (8, 1),
    "back_three": (8, 1),
    "back_two": (2, 2),
    "back_one": (4, 1),
    "three": 2,
    "blocks": 4,
    "gather": 4,
    "taps": 4,
    "enter": 4,
    "last": 4,
    "loss": 2,
}


def mm(x, w):
    return lax.dot_general(x, w, (((1,), (0,)), ((), ())), preferred_element_type=F32)


def mm_nt(x, w):
    return lax.dot_general(x, w, (((1,), (1,)), ((), ())), preferred_element_type=F32)


def mm_tn(x, w):
    return lax.dot_general(x, w, (((0,), (0,)), ((), ())), preferred_element_type=F32)


def back(x, axis):
    return pltpu.roll(x, x.shape[axis] - 1, axis)


def ahead(x, axis):
    return pltpu.roll(x, 1, axis)


def with_halo(own, left, right):
    lane = lax.broadcasted_iota(jnp.int32, own.shape, 1)
    halo = jnp.where(lane < HALO, right, jnp.where(lane >= OWN - HALO, left, 0.0))
    return jnp.concatenate([own, halo], axis=1)


def to_cells(stack):
    pad = OWN - stack.shape[0]
    if pad:
        stack = jnp.concatenate([stack, jnp.zeros((pad, LANES), F32)], axis=0)
    cells = stack.T
    return jnp.concatenate([cells[: OWN + HALO], cells[LANES - HALO :]], axis=0).astype(BF)


def to_lanes(cells):
    gap = jnp.zeros((LANES - WIDE, cells.shape[1]), cells.dtype)
    return jnp.concatenate([cells[: OWN + HALO], gap, cells[OWN + HALO :]], axis=0)


def lon_shifts(field):
    return jnp.concatenate([ahead(field, 1), field, back(field, 1)], axis=0)


def three_rows(ref, start, count):
    width = ref.shape[1]
    return jnp.concatenate(
        [ref[pl.ds(start + a, count)].reshape(count * width, ref.shape[2]) for a in range(3)], axis=1
    )


def lon_sum(taps, count, width, out):
    first, second, third = (
        taps[:, b * out : (b + 1) * out].reshape(count, width, out) for b in range(3)
    )
    return ahead(first, 1) + second + back(third, 1)


def four_channels(ref, row):
    sums = []
    for b in range(3):
        at = [(a * 3 + b) * 8 for a in range(3)]
        sums.append(
            ref[row, at[0] : at[0] + 8]
            + ref[row + 1, at[1] : at[1] + 8]
            + ref[row + 2, at[2] : at[2] + 8]
        )
    return ahead(sums[0], 1) + sums[1] + back(sums[2], 1)


def zero_edges(ref):
    edge = jnp.zeros(ref.shape[1:], ref.dtype)
    ref[0] = edge
    ref[ref.shape[0] - 1] = edge


def each(count, body, unroll=1):
    def step(i, carry):
        body(i)
        return carry

    lax.fori_loop(0, count, step, 0, unroll=unroll)


def pack_kernel(target, noise, land_mask, level, packed):
    power = level[...].astype(F32) / (LEVELS - 1)
    sigma = jnp.broadcast_to(0.02 * jnp.exp(power * math.log(4000.0)), (1, OWN))
    weight = 1.0 + land_mask[...].astype(F32)
    for p in range(packed.shape[0]):
        lanes = slice(p * OWN, (p + 1) * OWN)
        for r in range(2):
            packed[p, r, 0:1] = weight[r : r + 1, lanes]
            packed[p, r, 1:2] = sigma
            packed[p, r, 2:4] = jnp.zeros((2, OWN), F32)
            packed[p, r, 4:8] = target[:, r, lanes]
            packed[p, r, 8:12] = jnp.zeros((4, OWN), F32)
            packed[p, r, 12:16] = noise[:, r, lanes]


def stack_inputs(ref, weight, room):
    ref[...] = jnp.zeros_like(ref)
    count = weight.shape[2]
    for a in range(3):
        for b in range(3):
            ref[a, b * room : b * room + count] = weight[a, b].astype(F32)
    return ref[...].astype(BF).reshape(3 * OWN, OWN)


def stack_outputs(ref, weight):
    ref[...] = jnp.zeros_like(ref)
    for a in range(3):
        for b in range(3):
            at = (a * 3 + b) * 8 + 4
            ref[at : at + 4] = weight[a, b].astype(F32)
    return ref[...].astype(BF)


def step_kernel(
    scale,
    place,
    own,
    left,
    right,
    w_first,
    w_middle,
    w_last,
    w_in,
    w_down,
    w_up,
    w_out,
    mine,
    other,
    tiles,
    *scratch,
):
    (
        stack,
        stack_o,
        field,
        net,
        hid,
        act_c,
        taps,
        residuals,
        noisies,
        slope_a,
        act_a,
        pairs,
        pooled,
        act_b,
        slope_b,
        up_taps,
        phases,
        slope_c,
        grad_f,
        spread_f,
        back_c,
        grad_c,
        blocks,
        grad_b,
        grad_a,
        last_sum,
        den,
        halves,
        sems,
    ) = scratch
    for ref in (net, hid, pooled, up_taps, taps, grad_f, grad_c, grad_b):
        zero_edges(ref)
    first_w = stack_inputs(stack, w_first, 16)

    def gather(r):
        wide = with_halo(own[r], left[r], right[r])
        field[r] = wide
        net[r + 1] = to_cells(lon_shifts(wide[8:24]))

    each(ROWS, gather, CHUNK["gather"])

    n1, u1 = CHUNK["first"]

    def first(i):
        pre = mm(three_rows(net, n1 * i, n1), first_w)
        hid[pl.ds(n1 * i + 1, n1)] = jax.nn.silu(pre).astype(BF).reshape(n1, WIDE, HID1)

    each(ROWS // n1, first, u1)
    middle_w = jnp.concatenate([w_middle[a] for a in range(3)], axis=1)

    n2, u2 = CHUNK["second"]

    def second(i):
        pre = lon_sum(mm_nt(three_rows(hid, n2 * i, n2), middle_w), n2, WIDE, HID1)
        act_c[pl.ds(n2 * i, n2)] = jax.nn.silu(pre).astype(BF)

    each(ROWS // n2, second, u2)
    last_w = stack_outputs(stack_o, w_last)[0:72]

    def mean_taps(r):
        taps[r + 1] = mm_nt(last_w, to_lanes(act_c[r]))

    each(ROWS, mean_taps, CHUNK["taps"])
    in_w = stack_inputs(stack, w_in, FIELDS)
    lane = lax.broadcasted_iota(jnp.int32, (8, LANES), 1)
    held = (lane < OWN + HALO) | (lane >= LANES - HALO)
    low_half = lax.broadcasted_iota(jnp.int32, (8, LANES), 0) < 4

    def enter(r):
        mean_r = four_channels(taps, r).astype(BF).astype(F32)
        sigma = jnp.where(held, jnp.broadcast_to(field[r, 1:2], (8, LANES)), 1.0)
        residual = field[r, 0:8] - mean_r
        noisy = residual + sigma * field[r, 16:24]
        variance = sigma * sigma + 0.25
        residuals[r] = residual
        noisies[r] = noisy
        scaled = (lax.rsqrt(variance) * noisy).astype(BF).astype(F32)
        both = jnp.where(low_half, pltpu.roll(mean_r, 4, 0), scaled)
        net[r + 1] = to_cells(lon_shifts(jnp.concatenate([both, field[r, 8:24]], axis=0)))

    each(ROWS, enter, CHUNK["enter"])

    n3, u3 = CHUNK["one"]

    def level_one(i):
        pre = mm(three_rows(net, n3 * i, n3), in_w)
        gate = jax.nn.sigmoid(pre)
        slope_a[pl.ds(n3 * i, n3)] = (gate * (1.0 + pre * (1.0 - gate))).reshape(n3, WIDE, HID1)
        act = (pre * gate).astype(BF).reshape(n3, WIDE, HID1)
        act_a[pl.ds(n3 * i, n3)] = act
        wide = act.astype(F32)
        for k in range(n3 // 2):
            row = (n3 // 2) * i + k
            pairs[row] = wide[2 * k] + wide[2 * k + 1]
            total = pairs[row, pl.ds(0, WLOW, stride=2)] + pairs[row, pl.ds(1, WLOW, stride=2)]
            pooled[row + 1] = (0.25 * total).astype(BF)

    each(ROWS // n3, level_one, u3)
    down_w = jnp.concatenate([w_down[a] for a in range(3)], axis=1)

    n4, u4 = CHUNK["two"]

    def level_two(i):
        pre = lon_sum(mm_nt(three_rows(pooled, n4 * i, n4), down_w), n4, WLOW, HID2)
        gate = jax.nn.sigmoid(pre)
        slope_b[pl.ds(n4 * i, n4)] = gate * (1.0 + pre * (1.0 - gate))
        act_b[pl.ds(n4 * i, n4)] = (pre * gate).astype(BF)

    each(LOW // n4, level_two, u4)
    n5, u5 = CHUNK["up"]

    def up_products(i):
        low = act_b[pl.ds(n5 * i, n5)].reshape(n5 * WLOW, HID2)
        up_taps[pl.ds(n5 * i + 1, n5)] = mm_nt(low, w_up[...]).reshape(n5, WLOW, 9 * HID1)

    each(LOW // n5, up_products, u5)

    def level_three(i):
        for pi in range(2):
            sums = []
            for b in range(3):
                total = None
                for a in range(3):
                    row = i + 1 + (pi + a - 1) // 2
                    at = (a * 3 + b) * HID1
                    part = up_taps[row, :, at : at + HID1]
                    total = part if total is None else total + part
                sums.append(total)
            row = 2 * i + pi
            phases[row, pl.ds(0, WLOW, stride=2)] = ahead(sums[0], 0) + sums[1] + sums[2]
            phases[row, pl.ds(1, WLOW, stride=2)] = sums[0] + sums[1] + back(sums[2], 0)
            pre = phases[row]
            gate = jax.nn.sigmoid(pre)
            act_c[row] = (pre * gate + act_a[row].astype(F32)).astype(BF)
            slope_c[row] = gate * (1.0 + pre * (1.0 - gate))

    each(LOW, level_three, CHUNK["three"])
    out_w = stack_outputs(stack_o, w_out)

    def field_taps(r):
        taps[r + 1] = mm_nt(out_w[0:72], to_lanes(act_c[r]))

    each(ROWS, field_taps, CHUNK["taps"])

    def loss(i):
        for k in range(2):
            r = 2 * i + k
            value = four_channels(taps, r)
            sigma = jnp.where(held, jnp.broadcast_to(field[r, 1:2], (8, LANES)), 1.0)
            weight = jnp.broadcast_to(field[r, 0:1], (8, LANES))
            variance = sigma * sigma + 0.25
            c_out = 0.5 * sigma * lax.rsqrt(variance)
            lam = variance / (0.25 * sigma * sigma)
            denoised = (0.25 / variance) * noisies[r] + c_out * value
            den[i, 4 * k : 4 * k + 4] = denoised[4:8, :OWN]
            loss_grad = (2.0 * scale) * weight * lam * (denoised - residuals[r])
            cot = (c_out * loss_grad).astype(BF).astype(F32)
            grad_f[r + 1] = jnp.where(low_half, 0.0, cot)

    each(LOW, loss, CHUNK["loss"])
    tiles[...] = den[...].astype(BF)
    last_sum[...] = jnp.zeros_like(last_sum)

    def last_grads(r):
        parts = []
        for a in range(3):
            cot = grad_f[r + 2 - a]
            parts += [back(cot, 1), cot, ahead(cot, 1)]
        cots = jnp.concatenate(parts + [jnp.zeros((8, LANES), F32)], axis=0)
        last_sum[...] += mm(cots[:, :OWN].astype(BF), act_c[r, 0:OWN])
        spread_f[r] = to_cells(cots)

    each(ROWS, last_grads, CHUNK["last"])
    near, far = 0, 1

    def keep(half, at, value):
        halves[half, at : at + value.shape[0]] = value.astype(BF)

    def send(half):
        for core, target in ((half, mine), (1 - half, other)):

            @pl.when(place[0] == core)
            def _():
                pltpu.make_async_copy(halves.at[half], target, sems.at[half]).start()

    keep(near, BIG_ROWS, last_sum[0:LAST_ROWS])
    keep(near, BIG_ROWS + LAST_ROWS, jnp.zeros((HALF_ROWS - BIG_ROWS - LAST_ROWS, OWN), F32))

    n6, u6 = CHUNK["back_three"]

    def back_three(i):
        wide = mm(spread_f[pl.ds(n6 * i, n6)].reshape(n6 * WIDE, OWN), out_w)
        wide = wide.reshape(n6, WIDE, HID1)
        back_c[pl.ds(n6 * i, n6)] = wide
        grad_c[pl.ds(n6 * i + 1, n6)] = wide * slope_c[pl.ds(n6 * i, n6)]

    each(ROWS // n6, back_three, u6)

    def block_sums(i):
        even = [grad_c[2 * i + k, pl.ds(0, WLOW, stride=2)] for k in range(4)]
        odd = [grad_c[2 * i + k, pl.ds(1, WLOW, stride=2)] for k in range(4)]
        for a in range(3):
            e, o = even[2 - a] + even[3 - a], odd[2 - a] + odd[3 - a]
            for b, total in enumerate((o + back(e, 0), e + o, ahead(o, 0) + e)):
                at = (a * 3 + b) * HID1
                blocks[i, :, at : at + HID1] = total.astype(BF)

    each(LOW, block_sums, CHUNK["blocks"])

    n7, u7 = CHUNK["back_two"]

    def back_two(i):
        low = mm(blocks[pl.ds(n7 * i, n7)].reshape(n7 * WLOW, 9 * HID1), w_up[...])
        cot = low.reshape(n7, WLOW, HID2) * slope_b[pl.ds(n7 * i, n7)]
        shifts = jnp.concatenate([back(cot, 1), cot, ahead(cot, 1)], axis=2)
        grad_b[pl.ds(n7 * i + 1, n7)] = shifts.astype(BF)

    each(LOW // n7, back_two, u7)
    held_low = OWN // 2
    cells = LOW * held_low
    low_b = act_b[:, :held_low].reshape(cells, HID2)
    for k in range(3):
        at = 3 * HID1 * k
        up = mm_tn(blocks[:, :held_low, at : at + 3 * HID1].reshape(cells, 3 * HID1), low_b)
        keep(near, at, up[:, :HID1])
        keep(near, at + UP_ROWS, up[:, HID1:])
    send(near)
    low_a = jnp.concatenate(
        [pooled[a : a + LOW, :held_low].reshape(cells, HID1) for a in range(3)], axis=1
    )
    for b in range(3):
        at = HID2 * b
        down = mm_tn(grad_b[1 : LOW + 1, :held_low, at : at + HID2].reshape(cells, HID2), low_a)
        for a in range(3):
            keep(far, (a * 3 + b) * HID2, down[:, HID1 * a : HID1 * (a + 1)])
    n8, u8 = CHUNK["back_one"]

    def back_one(i):
        total = None
        for a in range(3):
            cot = grad_b[pl.ds(n8 * i + 2 - a, n8)].reshape(n8 * WLOW, 3 * HID2)
            part = mm(cot, w_down[a])
            total = part if total is None else total + part
        low = (0.25 * total).reshape(n8, WLOW, HID1)
        for k in range(n8):
            row = n8 * i + k
            phases[row, pl.ds(0, WLOW, stride=2)] = low[k]
            phases[row, pl.ds(1, WLOW, stride=2)] = low[k]
            spread = phases[row, 0:OWN]
            for pi in range(2):
                r = 2 * row + pi
                grad_a[r] = ((back_c[r, 0:OWN] + spread) * slope_a[r, 0:OWN]).astype(BF)

    each(LOW // n8, back_one, u8)
    near_cells = jnp.concatenate(
        [net[a : a + ROWS, :OWN].reshape(ROWS * OWN, OWN) for a in range(3)], axis=1
    )
    inputs = mm_tn(grad_a[...].reshape(ROWS * OWN, HID1), near_cells)
    for a in range(3):
        part = inputs[:, a * OWN : (a + 1) * OWN].T
        keep(far, BIG_ROWS + a * 3 * FIELDS, part[: 3 * FIELDS])
    keep(far, BIG_ROWS + IN_ROWS, jnp.zeros((HALF_ROWS - BIG_ROWS - IN_ROWS, OWN), F32))
    send(far)
    for half in (near, far):
        pltpu.make_async_copy(halves.at[half], mine, sems.at[half]).wait()


def unpack_kernel(place, *refs):
    mine, other = refs[0:4], refs[4:8]
    parts, tile, first, down, up, last, seat, sem = refs[8:]
    a = pl.program_id(0)
    even = place[0] == 0
    copy = pltpu.make_async_copy(parts.at[place[1], :, pl.ds(parts.shape[2] - CELL_ROWS, CELL_ROWS)], seat, sem)

    @pl.when(a == 0)
    def _():
        copy.start()

    def half(k, piece):
        one, two = mine[piece][...].astype(F32), other[piece][...].astype(F32)
        return jnp.where(even, one, two) if k == 0 else jnp.where(even, two, one)

    low = half(0, 0).reshape(3, HID1, HID1)
    high = half(0, 1).reshape(3, HID1, HID1)
    up[0] = jnp.concatenate([low, high], axis=2)
    down[0] = half(1, 2).reshape(3, HID2, HID1)

    def small(k, at, count):
        rows = pl.ds(pl.multiple_of(at, 8), count)
        one, two = mine[3][rows].astype(F32), other[3][rows].astype(F32)
        return jnp.where(even, one, two) if k == 0 else jnp.where(even, two, one)

    firsts = small(1, a * (3 * FIELDS), 3 * FIELDS)
    lasts = small(0, a * FIELDS, FIELDS)
    for b in range(3):
        first[0, b] = firsts[b * FIELDS : b * FIELDS + 20]
        last[0, b] = lasts[b * 8 + 4 : b * 8 + 8]

    @pl.when(a == 2)
    def _():
        copy.wait()
        blocks = seat[...].astype(F32)
        for k in range(8):
            for r in range(2):
                tile[:, r, k * OWN : (k + 1) * OWN] = blocks[k, 4 * r : 4 * r + 4]


def in_vmem(count):
    return [pl.BlockSpec(memory_space=pltpu.MemorySpace.VMEM) for _ in range(count)]


def in_smem():
    return pl.BlockSpec(memory_space=pltpu.MemorySpace.SMEM)


def pack(target, noise, land_mask, level_index):
    lats = target.shape[2] // OWN
    return pl.pallas_call(
        pack_kernel,
        out_shape=jax.ShapeDtypeStruct((lats, 2, 16, OWN), F32),
        in_specs=in_vmem(4),
        out_specs=in_vmem(1)[0],
        name="pack",
    )(target, noise, land_mask, level_index)


def step(scale, *operands):
    def kernel(*refs):
        step_kernel(scale, *refs)

    return pl.pallas_call(
        kernel,
        out_shape=(
            jax.ShapeDtypeStruct((HALF_ROWS, OWN), BF),
            jax.ShapeDtypeStruct((HALF_ROWS, OWN), BF),
            jax.ShapeDtypeStruct((LOW, CELL_ROWS, OWN), BF),
        ),
        in_specs=[in_smem(), *in_vmem(10)],
        out_specs=(*in_vmem(1), pl.BlockSpec(memory_space=pl.ANY), *in_vmem(1)),
        scratch_shapes=[
            pltpu.VMEM((3, OWN, OWN), F32),
            pltpu.VMEM((OWN, OWN), F32),
            pltpu.VMEM((ROWS, FIELDS, LANES), F32),
            pltpu.VMEM((ROWS + 2, WIDE, OWN), BF),
            pltpu.VMEM((ROWS + 2, WIDE, HID1), BF),
            pltpu.VMEM((ROWS, WIDE, HID1), BF),
            pltpu.VMEM((ROWS + 2, 72, LANES), F32),
            pltpu.VMEM((ROWS, 8, LANES), F32),
            pltpu.VMEM((ROWS, 8, LANES), F32),
            pltpu.VMEM((ROWS, WIDE, HID1), F32),
            pltpu.VMEM((ROWS, WIDE, HID1), BF),
            pltpu.VMEM((LOW, WIDE, HID1), F32),
            pltpu.VMEM((LOW + 2, WLOW, HID1), BF),
            pltpu.VMEM((LOW, WLOW, HID2), BF),
            pltpu.VMEM((LOW, WLOW, HID2), F32),
            pltpu.VMEM((LOW + 2, WLOW, 9 * HID1), F32),
            pltpu.VMEM((ROWS, WIDE, HID1), F32),
            pltpu.VMEM((ROWS, WIDE, HID1), F32),
            pltpu.VMEM((ROWS + 2, 8, LANES), F32),
            pltpu.VMEM((ROWS, WIDE, OWN), BF),
            pltpu.VMEM((ROWS, WIDE, HID1), F32),
            pltpu.VMEM((ROWS + 2, WIDE, HID1), F32),
            pltpu.VMEM((LOW, WLOW, 9 * HID1), BF),
            pltpu.VMEM((LOW + 2, WLOW, 3 * HID2), BF),
            pltpu.VMEM((ROWS, OWN, HID1), BF),
            pltpu.VMEM((80, HID1), F32),
            pltpu.VMEM((LOW, CELL_ROWS, OWN), F32),
            pltpu.VMEM((2, HALF_ROWS, OWN), BF),
            pltpu.SemaphoreType.DMA((2,)),
        ],
        name="step",
    )(*operands)


def unpack(place, mine, other, parts):
    third = 3 * HID1
    pieces = [
        pl.BlockSpec((third, OWN), lambda a: (a, 0)),
        pl.BlockSpec((third, OWN), lambda a: (a + UP_ROWS // third, 0)),
        pl.BlockSpec((2 * third, OWN), lambda a: (a, 0)),
        pl.BlockSpec((HALF_ROWS - BIG_ROWS, OWN), lambda a: (BIG_ROWS // (HALF_ROWS - BIG_ROWS), 0)),
    ]

    def taps(rows, lanes):
        return pl.BlockSpec((1, 3, rows, lanes), lambda a: (a, 0, 0, 0))

    return pl.pallas_call(
        unpack_kernel,
        grid=(3,),
        out_shape=(
            jax.ShapeDtypeStruct((4, 2, 8 * OWN), F32),
            jax.ShapeDtypeStruct((3, 3, 20, HID1), F32),
            jax.ShapeDtypeStruct((3, 3, HID2, HID1), F32),
            jax.ShapeDtypeStruct((3, 3, HID1, HID2), F32),
            jax.ShapeDtypeStruct((3, 3, 4, HID1), F32),
        ),
        in_specs=[in_smem(), *pieces, *pieces, pl.BlockSpec(memory_space=pl.ANY)],
        out_specs=(
            pl.BlockSpec((4, 2, 8 * OWN), lambda a: (0, 0, 0)),
            taps(20, HID1),
            taps(HID2, HID1),
            taps(HID1, HID2),
            taps(4, HID1),
        ),
        scratch_shapes=[pltpu.VMEM((8, CELL_ROWS, OWN), BF), pltpu.SemaphoreType.DMA(())],
        name="unpack",
    )(place, *[mine] * 4, *[other] * 4, parts)


def all_to_all(value, axes):
    return lax.all_to_all(value, axes, split_axis=0, concat_axis=0, tiled=True)


def shift_by(value, axes, step):
    count = lax.axis_size(axes)
    return lax.ppermute(value, axes, [(i, (i + step) % count) for i in range(count)])


def local(
    coarse,
    target,
    noise,
    land_mask,
    level_index,
    frozen_first,
    frozen_middle,
    frozen_last,
    diffuse_in,
    diffuse_down,
    diffuse_up,
    diffuse_out,
):
    scale = 1.0 / (target.shape[0] * math.sqrt(target.shape[1] * target.shape[2] * lax.axis_size(STRIPS)))
    place = jnp.stack([lax.axis_index("core"), lax.axis_index(("y", "x_hi"))]).astype(jnp.int32)
    packed = all_to_all(pack(target, noise, land_mask, level_index), LAT).reshape(ROWS, 16, OWN)
    fields = jnp.concatenate([packed[:, :8], coarse.transpose(1, 0, 2).astype(F32), packed[:, 12:]], axis=1)
    grads, partner, tiles = step(
        scale,
        place,
        fields,
        shift_by(fields, STRIPS, 1),
        shift_by(fields, STRIPS, -1),
        frozen_first.transpose(0, 1, 3, 2),
        frozen_middle.reshape(3, 3 * HID1, HID1),
        frozen_last,
        diffuse_in.transpose(0, 1, 3, 2),
        diffuse_down.reshape(3, 3 * HID2, HID1),
        diffuse_up.reshape(9 * HID1, HID2),
        diffuse_out,
    )
    chips = lax.axis_size(CHIPS)
    rows = HALF_ROWS // chips
    lats = tiles.shape[0]
    half = grads.astype(F32) + shift_by(partner, "core", 1).astype(F32)
    blocks = jnp.broadcast_to(tiles[None], (chips // lats, *tiles.shape)).reshape(chips, CELL_ROWS, OWN)
    sent = jnp.concatenate([half.astype(BF).reshape(chips, rows, OWN), blocks], axis=1)
    parts = all_to_all(sent, CHIPS)
    total = parts[:, :rows].astype(F32).sum(0).astype(BF)
    parts = parts.reshape(chips // lats, lats, rows + CELL_ROWS, OWN)
    with jax.named_scope("spread"):
        mine = all_to_all(jnp.broadcast_to(total[None], (chips, rows, OWN)), CHIPS).reshape(HALF_ROWS, OWN)
    tile, first, down, up, last = unpack(place, mine, shift_by(mine, "core", 1), parts)
    return (tile, first.transpose(0, 1, 3, 2), down, up, last)


def solution(mesh):
    fine = Mesh(mesh.devices.reshape(4, 2, 2, 2, 4), LON + LAT)
    tile = P(None, LAT, LON)
    return jax.shard_map(
        local,
        mesh=fine,
        in_specs=(
            P(None, None, STRIPS),
            tile,
            tile,
            P(LAT, LON),
            P(LAT, LON),
            *([P()] * 7),
        ),
        out_specs=(tile, P(), P(), P(), P()),
        check_vma=False,
    )
```

```python
import math

import jax
import jax.numpy as jnp
from jax import lax
from jax.experimental import pallas as pl
from jax.experimental.pallas import tpu as pltpu
from jax.sharding import Mesh
from jax.sharding import PartitionSpec as P

LEVELS = 32
ROWS = 16
LOW = ROWS // 2
OWN = 128
HALO = 16
WIDE = OWN + 2 * HALO
WLOW = WIDE // 2
LANES = 256
HID1 = 128
HID2 = 256
BF = jnp.bfloat16
F32 = jnp.float32

LON = ("y", "x_hi", "core")
LAT = ("x_lo", "z")
CHIPS = ("y", "x_hi", "x_lo", "z")
STRIPS = LON + LAT

FIELDS = 24
UP_ROWS = 9 * HID1
DOWN_ROWS = 9 * HID2
BIG_ROWS = 2304
LAST_ROWS = 72
IN_ROWS = 9 * FIELDS
HALF_ROWS = 2560
CELL_ROWS = 8
CHUNK = {
    "gather": 8,
    "first": (8, 1),
    "second": (4, 4),
    "taps": 8,
    "enter": 8,
    "one": (8, 1),
    "two": (4, 2),
    "up": (8, 1),
    "three": 2,
    "loss": 4,
    "last": 8,
    "back_three": (8, 1),
    "blocks": 4,
    "back_two": (2, 4),
    "back_one": (4, 2),
}


def mm(x, w):
    return lax.dot_general(x, w, (((1,), (0,)), ((), ())), preferred_element_type=F32)


def mm_nt(x, w):
    return lax.dot_general(x, w, (((1,), (1,)), ((), ())), preferred_element_type=F32)


def mm_tn(x, w):
    return lax.dot_general(x, w, (((0,), (0,)), ((), ())), preferred_element_type=F32)


def back(x, axis):
    return pltpu.roll(x, x.shape[axis] - 1, axis)


def ahead(x, axis):
    return pltpu.roll(x, 1, axis)


def with_halo(own, left, right):
    lane = lax.broadcasted_iota(jnp.int32, own.shape, 1)
    halo = jnp.where(lane < HALO, right, jnp.where(lane >= OWN - HALO, left, 0.0))
    return jnp.concatenate([own, halo], axis=1)


def to_cells(stack):
    pad = OWN - stack.shape[0]
    if pad:
        stack = jnp.concatenate([stack, jnp.zeros((pad, LANES), F32)], axis=0)
    cells = stack.T
    return jnp.concatenate([cells[: OWN + HALO], cells[LANES - HALO :]], axis=0).astype(BF)


def to_lanes(cells):
    gap = jnp.zeros((LANES - WIDE, cells.shape[1]), cells.dtype)
    return jnp.concatenate([cells[: OWN + HALO], gap, cells[OWN + HALO :]], axis=0)


def lon_shifts(field):
    return jnp.concatenate([ahead(field, 1), field, back(field, 1)], axis=0)


def three_rows(ref, start, count):
    width = ref.shape[1]
    return jnp.concatenate(
        [ref[pl.ds(start + a, count)].reshape(count * width, ref.shape[2]) for a in range(3)], axis=1
    )


def lon_sum(taps, count, width, out):
    first, second, third = (
        taps[:, b * out : (b + 1) * out].reshape(count, width, out) for b in range(3)
    )
    return ahead(first, 1) + second + back(third, 1)


def four_channels(ref, row):
    sums = []
    for b in range(3):
        at = [(a * 3 + b) * 8 for a in range(3)]
        sums.append(
            ref[row, at[0] : at[0] + 8]
            + ref[row + 1, at[1] : at[1] + 8]
            + ref[row + 2, at[2] : at[2] + 8]
        )
    return ahead(sums[0], 1) + sums[1] + back(sums[2], 1)


def zero_edges(ref):
    edge = jnp.zeros(ref.shape[1:], ref.dtype)
    ref[0] = edge
    ref[ref.shape[0] - 1] = edge


def each(count, body, unroll=1):
    def step(i, carry):
        body(i)
        return carry

    lax.fori_loop(0, count, step, 0, unroll=unroll)


def pack_kernel(target, noise, land_mask, level, packed):
    power = level[...].astype(F32) / (LEVELS - 1)
    sigma = jnp.broadcast_to(0.02 * jnp.exp(power * math.log(4000.0)), (1, OWN))
    weight = 1.0 + land_mask[...].astype(F32)
    for p in range(packed.shape[0]):
        lanes = slice(p * OWN, (p + 1) * OWN)
        for r in range(2):
            packed[p, r, 0:1] = weight[r : r + 1, lanes]
            packed[p, r, 1:2] = sigma
            packed[p, r, 2:4] = jnp.zeros((2, OWN), F32)
            packed[p, r, 4:8] = target[:, r, lanes]
            packed[p, r, 8:12] = jnp.zeros((4, OWN), F32)
            packed[p, r, 12:16] = noise[:, r, lanes]


def stack_inputs(ref, weight, room):
    ref[...] = jnp.zeros_like(ref)
    count = weight.shape[2]
    for a in range(3):
        for b in range(3):
            ref[a, b * room : b * room + count] = weight[a, b].astype(F32)
    return ref[...].astype(BF).reshape(3 * OWN, OWN)


def stack_outputs(ref, weight):
    ref[...] = jnp.zeros_like(ref)
    for a in range(3):
        for b in range(3):
            at = (a * 3 + b) * 8 + 4
            ref[at : at + 4] = weight[a, b].astype(F32)
    return ref[...].astype(BF)


def step_kernel(
    scale,
    place,
    own,
    pair,
    across,
    w_first,
    w_middle,
    w_last,
    w_in,
    w_down,
    w_up,
    w_out,
    mine,
    other,
    tiles,
    *scratch,
):
    (
        stack,
        stack_o,
        field,
        net,
        hid,
        act_c,
        taps,
        residuals,
        noisies,
        slope_a,
        act_a,
        pairs,
        pooled,
        act_b,
        slope_b,
        up_taps,
        phases,
        slope_c,
        grad_f,
        spread_f,
        back_c,
        grad_c,
        blocks,
        grad_b,
        grad_a,
        last_sum,
        den,
        halves,
        sems,
    ) = scratch
    for ref in (net, hid, pooled, up_taps, taps, grad_f, grad_c, grad_b):
        zero_edges(ref)
    even = place[1] == 0
    first_w = stack_inputs(stack, w_first, 16)

    def gather(r):
        near, far = pair[r], across[r]
        wide = with_halo(own[r], jnp.where(even, far, near), jnp.where(even, near, far))
        field[r] = wide
        net[r + 1] = to_cells(lon_shifts(wide[8:24]))

    each(ROWS, gather, CHUNK["gather"])

    n1, u1 = CHUNK["first"]

    def first(i):
        pre = mm(three_rows(net, n1 * i, n1), first_w)
        hid[pl.ds(n1 * i + 1, n1)] = jax.nn.silu(pre).astype(BF).reshape(n1, WIDE, HID1)

    each(ROWS // n1, first, u1)
    middle_w = jnp.concatenate([w_middle[a] for a in range(3)], axis=1)

    n2, u2 = CHUNK["second"]

    def second(i):
        pre = lon_sum(mm_nt(three_rows(hid, n2 * i, n2), middle_w), n2, WIDE, HID1)
        act_c[pl.ds(n2 * i, n2)] = jax.nn.silu(pre).astype(BF)

    each(ROWS // n2, second, u2)
    last_w = stack_outputs(stack_o, w_last)[0:72]

    def mean_taps(r):
        taps[r + 1] = mm_nt(last_w, to_lanes(act_c[r]))

    each(ROWS, mean_taps, CHUNK["taps"])
    in_w = stack_inputs(stack, w_in, FIELDS)
    lane = lax.broadcasted_iota(jnp.int32, (8, LANES), 1)
    held = (lane < OWN + HALO) | (lane >= LANES - HALO)
    low_half = lax.broadcasted_iota(jnp.int32, (8, LANES), 0) < 4

    def enter(r):
        mean_r = four_channels(taps, r).astype(BF).astype(F32)
        sigma = jnp.where(held, jnp.broadcast_to(field[r, 1:2], (8, LANES)), 1.0)
        residual = field[r, 0:8] - mean_r
        noisy = residual + sigma * field[r, 16:24]
        variance = sigma * sigma + 0.25
        residuals[r] = residual
        noisies[r] = noisy
        scaled = (lax.rsqrt(variance) * noisy).astype(BF).astype(F32)
        both = jnp.where(low_half, pltpu.roll(mean_r, 4, 0), scaled)
        net[r + 1] = to_cells(lon_shifts(jnp.concatenate([both, field[r, 8:24]], axis=0)))

    each(ROWS, enter, CHUNK["enter"])

    n3, u3 = CHUNK["one"]

    def level_one(i):
        pre = mm(three_rows(net, n3 * i, n3), in_w)
        gate = jax.nn.sigmoid(pre)
        slope_a[pl.ds(n3 * i, n3)] = (gate * (1.0 + pre * (1.0 - gate))).reshape(n3, WIDE, HID1)
        act = (pre * gate).astype(BF).reshape(n3, WIDE, HID1)
        act_a[pl.ds(n3 * i, n3)] = act
        wide = act.astype(F32)
        for k in range(n3 // 2):
            row = (n3 // 2) * i + k
            pairs[row] = wide[2 * k] + wide[2 * k + 1]
            total = pairs[row, pl.ds(0, WLOW, stride=2)] + pairs[row, pl.ds(1, WLOW, stride=2)]
            pooled[row + 1] = (0.25 * total).astype(BF)

    each(ROWS // n3, level_one, u3)
    down_w = jnp.concatenate([w_down[a] for a in range(3)], axis=1)

    n4, u4 = CHUNK["two"]

    def level_two(i):
        pre = lon_sum(mm_nt(three_rows(pooled, n4 * i, n4), down_w), n4, WLOW, HID2)
        gate = jax.nn.sigmoid(pre)
        slope_b[pl.ds(n4 * i, n4)] = gate * (1.0 + pre * (1.0 - gate))
        act_b[pl.ds(n4 * i, n4)] = (pre * gate).astype(BF)

    each(LOW // n4, level_two, u4)
    n5, u5 = CHUNK["up"]

    def up_products(i):
        low = act_b[pl.ds(n5 * i, n5)].reshape(n5 * WLOW, HID2)
        up_taps[pl.ds(n5 * i + 1, n5)] = mm_nt(low, w_up[...]).reshape(n5, WLOW, 9 * HID1)

    each(LOW // n5, up_products, u5)

    def level_three(i):
        for pi in range(2):
            sums = []
            for b in range(3):
                total = None
                for a in range(3):
                    row = i + 1 + (pi + a - 1) // 2
                    at = (a * 3 + b) * HID1
                    part = up_taps[row, :, at : at + HID1]
                    total = part if total is None else total + part
                sums.append(total)
            row = 2 * i + pi
            phases[row, pl.ds(0, WLOW, stride=2)] = ahead(sums[0], 0) + sums[1] + sums[2]
            phases[row, pl.ds(1, WLOW, stride=2)] = sums[0] + sums[1] + back(sums[2], 0)
            pre = phases[row]
            gate = jax.nn.sigmoid(pre)
            act_c[row] = (pre * gate + act_a[row].astype(F32)).astype(BF)
            slope_c[row] = gate * (1.0 + pre * (1.0 - gate))

    each(LOW, level_three, CHUNK["three"])
    out_w = stack_outputs(stack_o, w_out)

    def field_taps(r):
        taps[r + 1] = mm_nt(out_w[0:72], to_lanes(act_c[r]))

    each(ROWS, field_taps, CHUNK["taps"])

    def loss(i):
        for k in range(2):
            r = 2 * i + k
            value = four_channels(taps, r)
            sigma = jnp.where(held, jnp.broadcast_to(field[r, 1:2], (8, LANES)), 1.0)
            weight = jnp.broadcast_to(field[r, 0:1], (8, LANES))
            variance = sigma * sigma + 0.25
            c_out = 0.5 * sigma * lax.rsqrt(variance)
            lam = variance / (0.25 * sigma * sigma)
            denoised = (0.25 / variance) * noisies[r] + c_out * value
            den[i, 4 * k : 4 * k + 4] = denoised[4:8, :OWN]
            loss_grad = (2.0 * scale) * weight * lam * (denoised - residuals[r])
            cot = (c_out * loss_grad).astype(BF).astype(F32)
            grad_f[r + 1] = jnp.where(low_half, 0.0, cot)

    each(LOW, loss, CHUNK["loss"])
    tiles[...] = den[...].astype(BF)
    last_sum[...] = jnp.zeros_like(last_sum)

    def last_grads(r):
        parts = []
        for a in range(3):
            cot = grad_f[r + 2 - a]
            parts += [back(cot, 1), cot, ahead(cot, 1)]
        cots = jnp.concatenate(parts + [jnp.zeros((8, LANES), F32)], axis=0)
        last_sum[...] += mm(cots[:, :OWN].astype(BF), act_c[r, 0:OWN])
        spread_f[r] = to_cells(cots)

    each(ROWS, last_grads, CHUNK["last"])
    near, far = 0, 1

    def keep(half, at, value):
        halves[half, at : at + value.shape[0]] = value.astype(BF)

    def send(half):
        for core, target in ((half, mine), (1 - half, other)):

            @pl.when(place[0] == core)
            def _():
                pltpu.make_async_copy(halves.at[half], target, sems.at[half]).start()

    keep(near, BIG_ROWS, last_sum[0:LAST_ROWS])
    keep(near, BIG_ROWS + LAST_ROWS, jnp.zeros((HALF_ROWS - BIG_ROWS - LAST_ROWS, OWN), F32))

    n6, u6 = CHUNK["back_three"]

    def back_three(i):
        wide = mm(spread_f[pl.ds(n6 * i, n6)].reshape(n6 * WIDE, OWN), out_w)
        wide = wide.reshape(n6, WIDE, HID1)
        back_c[pl.ds(n6 * i, n6)] = wide
        grad_c[pl.ds(n6 * i + 1, n6)] = wide * slope_c[pl.ds(n6 * i, n6)]

    each(ROWS // n6, back_three, u6)

    def block_sums(i):
        even = [grad_c[2 * i + k, pl.ds(0, WLOW, stride=2)] for k in range(4)]
        odd = [grad_c[2 * i + k, pl.ds(1, WLOW, stride=2)] for k in range(4)]
        for a in range(3):
            e, o = even[2 - a] + even[3 - a], odd[2 - a] + odd[3 - a]
            for b, total in enumerate((o + back(e, 0), e + o, ahead(o, 0) + e)):
                at = (a * 3 + b) * HID1
                blocks[i, :, at : at + HID1] = total.astype(BF)

    each(LOW, block_sums, CHUNK["blocks"])

    n7, u7 = CHUNK["back_two"]

    def back_two(i):
        low = mm(blocks[pl.ds(n7 * i, n7)].reshape(n7 * WLOW, 9 * HID1), w_up[...])
        cot = low.reshape(n7, WLOW, HID2) * slope_b[pl.ds(n7 * i, n7)]
        shifts = jnp.concatenate([back(cot, 1), cot, ahead(cot, 1)], axis=2)
        grad_b[pl.ds(n7 * i + 1, n7)] = shifts.astype(BF)

    each(LOW // n7, back_two, u7)
    held_low = OWN // 2
    cells = LOW * held_low
    low_b = act_b[:, :held_low].reshape(cells, HID2)
    for k in range(3):
        at = 3 * HID1 * k
        up = mm_tn(blocks[:, :held_low, at : at + 3 * HID1].reshape(cells, 3 * HID1), low_b)
        keep(near, at, up[:, :HID1])
        keep(near, at + UP_ROWS, up[:, HID1:])
    send(near)
    low_a = jnp.concatenate(
        [pooled[a : a + LOW, :held_low].reshape(cells, HID1) for a in range(3)], axis=1
    )
    for b in range(3):
        at = HID2 * b
        down = mm_tn(grad_b[1 : LOW + 1, :held_low, at : at + HID2].reshape(cells, HID2), low_a)
        for a in range(3):
            keep(far, (a * 3 + b) * HID2, down[:, HID1 * a : HID1 * (a + 1)])
    n8, u8 = CHUNK["back_one"]

    def back_one(i):
        total = None
        for a in range(3):
            cot = grad_b[pl.ds(n8 * i + 2 - a, n8)].reshape(n8 * WLOW, 3 * HID2)
            part = mm(cot, w_down[a])
            total = part if total is None else total + part
        low = (0.25 * total).reshape(n8, WLOW, HID1)
        for k in range(n8):
            row = n8 * i + k
            phases[row, pl.ds(0, WLOW, stride=2)] = low[k]
            phases[row, pl.ds(1, WLOW, stride=2)] = low[k]
            spread = phases[row, 0:OWN]
            for pi in range(2):
                r = 2 * row + pi
                grad_a[r] = ((back_c[r, 0:OWN] + spread) * slope_a[r, 0:OWN]).astype(BF)

    each(LOW // n8, back_one, u8)
    near_cells = jnp.concatenate(
        [net[a : a + ROWS, :OWN].reshape(ROWS * OWN, OWN) for a in range(3)], axis=1
    )
    inputs = mm_tn(grad_a[...].reshape(ROWS * OWN, HID1), near_cells)
    for a in range(3):
        part = inputs[:, a * OWN : (a + 1) * OWN].T
        keep(far, BIG_ROWS + a * 3 * FIELDS, part[: 3 * FIELDS])
    keep(far, BIG_ROWS + IN_ROWS, jnp.zeros((HALF_ROWS - BIG_ROWS - IN_ROWS, OWN), F32))
    send(far)
    for half in (near, far):
        pltpu.make_async_copy(halves.at[half], mine, sems.at[half]).wait()


def unpack_kernel(place, mine, other, parts, tile, first, down, up, last, halves, seat, downs, ups, sems):
    seats = parts.at[place[2], :, pl.ds(parts.shape[2] - CELL_ROWS, CELL_ROWS)]
    arrive = [
        pltpu.make_async_copy(mine, halves.at[0], sems.at[0]),
        pltpu.make_async_copy(other, halves.at[1], sems.at[1]),
        pltpu.make_async_copy(seats, seat, sems.at[2]),
    ]
    for copy in arrive:
        copy.start()
    for copy in arrive:
        copy.wait()
    low, high = place[0], 1 - place[0]

    def leave(a, ups_a, downs_a):
        return (
            pltpu.make_async_copy(ups_a, up.at[a], sems.at[0]),
            pltpu.make_async_copy(downs_a, down.at[a], sems.at[1]),
        )

    def thirds(a):
        at = pl.multiple_of(a * (3 * HID1), 3 * HID1)
        for k in range(2):
            piece = halves[low, pl.ds(at + k * UP_ROWS, 3 * HID1)]
            ups[a, :, :, k * HID1 : (k + 1) * HID1] = piece.astype(F32).reshape(3, HID1, HID1)
        piece = halves[high, pl.ds(2 * at, 3 * HID2)]
        downs[a] = piece.astype(F32).reshape(3, HID2, HID1)
        for copy in leave(a, ups.at[a], downs.at[a]):
            copy.start()

    each(3, thirds)
    firsts = halves[high, BIG_ROWS : BIG_ROWS + IN_ROWS].astype(F32)
    lasts = halves[low, BIG_ROWS : BIG_ROWS + 80].astype(F32)
    for a in range(3):
        for b in range(3):
            at = (a * 3 + b) * FIELDS
            first[a, b] = firsts[at : at + 20]
            at = (a * 3 + b) * 8 + 4
            last[a, b] = lasts[at : at + 4]
    blocks = seat[...].astype(F32)
    for k in range(8):
        for r in range(2):
            tile[:, r, k * OWN : (k + 1) * OWN] = blocks[k, 4 * r : 4 * r + 4]
    for a in range(3):
        for copy in leave(a, ups.at[a], downs.at[a]):
            copy.wait()


def in_vmem(count):
    return [pl.BlockSpec(memory_space=pltpu.MemorySpace.VMEM) for _ in range(count)]


def in_smem():
    return pl.BlockSpec(memory_space=pltpu.MemorySpace.SMEM)


def pack(target, noise, land_mask, level_index):
    lats = target.shape[2] // OWN
    return pl.pallas_call(
        pack_kernel,
        out_shape=jax.ShapeDtypeStruct((lats, 2, 16, OWN), F32),
        in_specs=in_vmem(4),
        out_specs=in_vmem(1)[0],
        name="pack",
    )(target, noise, land_mask, level_index)


def step(scale, *operands):
    def kernel(*refs):
        step_kernel(scale, *refs)

    return pl.pallas_call(
        kernel,
        out_shape=(
            jax.ShapeDtypeStruct((HALF_ROWS, OWN), BF),
            jax.ShapeDtypeStruct((HALF_ROWS, OWN), BF),
            jax.ShapeDtypeStruct((LOW, CELL_ROWS, OWN), BF),
        ),
        in_specs=[in_smem(), *in_vmem(10)],
        out_specs=tuple(in_vmem(3)),
        scratch_shapes=[
            pltpu.VMEM((3, OWN, OWN), F32),
            pltpu.VMEM((OWN, OWN), F32),
            pltpu.VMEM((ROWS, FIELDS, LANES), F32),
            pltpu.VMEM((ROWS + 2, WIDE, OWN), BF),
            pltpu.VMEM((ROWS + 2, WIDE, HID1), BF),
            pltpu.VMEM((ROWS, WIDE, HID1), BF),
            pltpu.VMEM((ROWS + 2, 72, LANES), F32),
            pltpu.VMEM((ROWS, 8, LANES), F32),
            pltpu.VMEM((ROWS, 8, LANES), F32),
            pltpu.VMEM((ROWS, WIDE, HID1), F32),
            pltpu.VMEM((ROWS, WIDE, HID1), BF),
            pltpu.VMEM((LOW, WIDE, HID1), F32),
            pltpu.VMEM((LOW + 2, WLOW, HID1), BF),
            pltpu.VMEM((LOW, WLOW, HID2), BF),
            pltpu.VMEM((LOW, WLOW, HID2), F32),
            pltpu.VMEM((LOW + 2, WLOW, 9 * HID1), F32),
            pltpu.VMEM((ROWS, WIDE, HID1), F32),
            pltpu.VMEM((ROWS, WIDE, HID1), F32),
            pltpu.VMEM((ROWS + 2, 8, LANES), F32),
            pltpu.VMEM((ROWS, WIDE, OWN), BF),
            pltpu.VMEM((ROWS, WIDE, HID1), F32),
            pltpu.VMEM((ROWS + 2, WIDE, HID1), F32),
            pltpu.VMEM((LOW, WLOW, 9 * HID1), BF),
            pltpu.VMEM((LOW + 2, WLOW, 3 * HID2), BF),
            pltpu.VMEM((ROWS, OWN, HID1), BF),
            pltpu.VMEM((80, HID1), F32),
            pltpu.VMEM((LOW, CELL_ROWS, OWN), F32),
            pltpu.VMEM((2, HALF_ROWS, OWN), BF),
            pltpu.SemaphoreType.DMA((2,)),
        ],
        name="step",
    )(*operands)


def unpack(place, mine, other, parts):
    anywhere = pl.BlockSpec(memory_space=pl.ANY)
    vmem = in_vmem(1)[0]
    return pl.pallas_call(
        unpack_kernel,
        out_shape=(
            jax.ShapeDtypeStruct((4, 2, 8 * OWN), F32),
            jax.ShapeDtypeStruct((3, 3, 20, HID1), F32),
            jax.ShapeDtypeStruct((3, 3, HID2, HID1), F32),
            jax.ShapeDtypeStruct((3, 3, HID1, HID2), F32),
            jax.ShapeDtypeStruct((3, 3, 4, HID1), F32),
        ),
        in_specs=[in_smem(), *[pl.BlockSpec(memory_space=pltpu.MemorySpace.HBM)] * 3],
        out_specs=(vmem, vmem, anywhere, anywhere, vmem),
        scratch_shapes=[
            pltpu.VMEM((2, HALF_ROWS, OWN), BF),
            pltpu.VMEM((8, CELL_ROWS, OWN), BF),
            pltpu.VMEM((3, 3, HID2, HID1), F32),
            pltpu.VMEM((3, 3, HID1, HID2), F32),
            pltpu.SemaphoreType.DMA((3,)),
        ],
        name="unpack",
    )(place, mine, other, parts)


def all_to_all(value, axes):
    return lax.all_to_all(value, axes, split_axis=0, concat_axis=0, tiled=True)


def swap(value, axes, offset):
    count = lax.axis_size(axes)
    pairs = []
    for i in range(offset, count + offset, 2):
        here, there = i % count, (i + 1) % count
        pairs += [(here, there), (there, here)]
    return lax.ppermute(value, axes, sorted(set(pairs)))


def local(
    coarse,
    target,
    noise,
    land_mask,
    level_index,
    frozen_first,
    frozen_middle,
    frozen_last,
    diffuse_in,
    diffuse_down,
    diffuse_up,
    diffuse_out,
):
    scale = 1.0 / (target.shape[0] * math.sqrt(target.shape[1] * target.shape[2] * lax.axis_size(STRIPS)))
    place = jnp.stack([lax.axis_index("core"), lax.axis_index("z") % 2, lax.axis_index(("y", "x_hi"))])
    place = place.astype(jnp.int32)
    packed = all_to_all(pack(target, noise, land_mask, level_index), LAT).reshape(ROWS, 16, OWN)
    fields = jnp.concatenate([packed[:, :8], coarse.transpose(1, 0, 2).astype(F32), packed[:, 12:]], axis=1)
    across = swap(fields, STRIPS, 1)
    pair = swap(fields, STRIPS, 0)
    grads, partner, tiles = step(
        scale,
        place,
        fields,
        pair,
        across,
        frozen_first.transpose(0, 1, 3, 2),
        frozen_middle.reshape(3, 3 * HID1, HID1),
        frozen_last,
        diffuse_in.transpose(0, 1, 3, 2),
        diffuse_down.reshape(3, 3 * HID2, HID1),
        diffuse_up.reshape(9 * HID1, HID2),
        diffuse_out,
    )
    chips = lax.axis_size(CHIPS)
    rows = HALF_ROWS // chips
    lats = tiles.shape[0]
    half = grads.astype(F32) + swap(partner, "core", 0).astype(F32)
    blocks = jnp.broadcast_to(tiles[None], (chips // lats, *tiles.shape)).reshape(chips, CELL_ROWS, OWN)
    sent = jnp.concatenate([half.astype(BF).reshape(chips, rows, OWN), blocks], axis=1)
    parts = all_to_all(sent, CHIPS)
    total = parts[:, :rows].astype(F32).sum(0).astype(BF)
    parts = parts.reshape(chips // lats, lats, rows + CELL_ROWS, OWN)
    with jax.named_scope("spread"):
        mine = all_to_all(jnp.broadcast_to(total[None], (chips, rows, OWN)), CHIPS).reshape(HALF_ROWS, OWN)
    tile, first, down, up, last = unpack(place, mine, swap(mine, "core", 0), parts)
    return (tile, first.transpose(0, 1, 3, 2), down, up, last)


def solution(mesh):
    fine = Mesh(mesh.devices.reshape(4, 2, 2, 2, 4), LON + LAT)
    tile = P(None, LAT, LON)
    return jax.shard_map(
        local,
        mesh=fine,
        in_specs=(
            P(None, None, STRIPS),
            tile,
            tile,
            P(LAT, LON),
            P(LAT, LON),
            *([P()] * 7),
        ),
        out_specs=(tile, P(), P(), P(), P()),
        check_vma=False,
    )
```

```python
import math

import jax
import jax.numpy as jnp
from jax import lax
from jax.experimental import pallas as pl
from jax.experimental.pallas import tpu as pltpu
from jax.sharding import Mesh
from jax.sharding import PartitionSpec as P

LEVELS = 32
ROWS = 16
LOW = ROWS // 2
OWN = 128
HALO = 16
WIDE = OWN + 2 * HALO
WLOW = WIDE // 2
LANES = 256
HID1 = 128
HID2 = 256
BF = jnp.bfloat16
F32 = jnp.float32

LON = ("y", "x_hi", "core")
LAT = ("x_lo", "z")
CHIPS = ("y", "x_hi", "x_lo", "z")
STRIPS = LON + LAT

FIELDS = 24
UP_ROWS = 9 * HID1
DOWN_ROWS = 9 * HID2
BIG_ROWS = 2304
LAST_ROWS = 72
IN_ROWS = 9 * FIELDS
HALF_ROWS = 2560
CELL_ROWS = 8
CHUNK = {
    "gather": 8,
    "first": (8, 1),
    "second": (4, 4),
    "taps": 8,
    "enter": 8,
    "one": (8, 1),
    "two": (4, 2),
    "up": (8, 1),
    "three": 2,
    "loss": 4,
    "last": 8,
    "back_three": (8, 1),
    "blocks": 4,
    "back_two": (2, 4),
    "back_one": (4, 2),
}


def mm(x, w):
    return lax.dot_general(x, w, (((1,), (0,)), ((), ())), preferred_element_type=F32)


def mm_nt(x, w):
    return lax.dot_general(x, w, (((1,), (1,)), ((), ())), preferred_element_type=F32)


def mm_tn(x, w):
    return lax.dot_general(x, w, (((0,), (0,)), ((), ())), preferred_element_type=F32)


def back(x, axis):
    return pltpu.roll(x, x.shape[axis] - 1, axis)


def ahead(x, axis):
    return pltpu.roll(x, 1, axis)


def with_halo(own, left, right):
    lane = lax.broadcasted_iota(jnp.int32, own.shape, 1)
    halo = jnp.where(lane < HALO, right, jnp.where(lane >= OWN - HALO, left, 0.0))
    return jnp.concatenate([own, halo], axis=1)


def to_cells(stack):
    pad = OWN - stack.shape[0]
    if pad:
        stack = jnp.concatenate([stack, jnp.zeros((pad, LANES), F32)], axis=0)
    cells = stack.T
    return jnp.concatenate([cells[: OWN + HALO], cells[LANES - HALO :]], axis=0).astype(BF)


def to_lanes(cells):
    gap = jnp.zeros((LANES - WIDE, cells.shape[1]), cells.dtype)
    return jnp.concatenate([cells[: OWN + HALO], gap, cells[OWN + HALO :]], axis=0)


def lon_shifts(field):
    return jnp.concatenate([ahead(field, 1), field, back(field, 1)], axis=0)


def three_rows(ref, start, count):
    width = ref.shape[1]
    return jnp.concatenate(
        [ref[pl.ds(start + a, count)].reshape(count * width, ref.shape[2]) for a in range(3)], axis=1
    )


def lon_sum(taps, count, width, out):
    first, second, third = (
        taps[:, b * out : (b + 1) * out].reshape(count, width, out) for b in range(3)
    )
    return ahead(first, 1) + second + back(third, 1)


def four_channels(ref, row):
    sums = []
    for b in range(3):
        at = [(a * 3 + b) * 8 for a in range(3)]
        sums.append(
            ref[row, at[0] : at[0] + 8]
            + ref[row + 1, at[1] : at[1] + 8]
            + ref[row + 2, at[2] : at[2] + 8]
        )
    return ahead(sums[0], 1) + sums[1] + back(sums[2], 1)


def zero_edges(ref):
    edge = jnp.zeros(ref.shape[1:], ref.dtype)
    ref[0] = edge
    ref[ref.shape[0] - 1] = edge


def each(count, body, unroll=1):
    def step(i, carry):
        body(i)
        return carry

    lax.fori_loop(0, count, step, 0, unroll=unroll)


def pack_kernel(level, target_far, noise_far, mask_far, packed, target, noise, land_mask, sems):
    arrive = [
        pltpu.make_async_copy(target_far, target, sems.at[0]),
        pltpu.make_async_copy(noise_far, noise, sems.at[1]),
        pltpu.make_async_copy(mask_far, land_mask, sems.at[2]),
    ]
    for copy in arrive:
        copy.start()
    power = jnp.full((1, OWN), level[0, 0], jnp.int32).astype(F32) / (LEVELS - 1)
    sigma = 0.02 * jnp.exp(power * math.log(4000.0))
    for copy in arrive:
        copy.wait()
    weight = 1.0 + land_mask[...].astype(F32)
    for p in range(packed.shape[0]):
        lanes = slice(p * OWN, (p + 1) * OWN)
        for r in range(2):
            packed[p, r, 0:1] = weight[r : r + 1, lanes]
            packed[p, r, 1:2] = sigma
            packed[p, r, 2:4] = jnp.zeros((2, OWN), F32)
            packed[p, r, 4:8] = target[:, r, lanes]
            packed[p, r, 8:12] = jnp.zeros((4, OWN), F32)
            packed[p, r, 12:16] = noise[:, r, lanes]


def stack_inputs(ref, weight, room):
    ref[...] = jnp.zeros_like(ref)
    count = weight.shape[2]
    for a in range(3):
        for b in range(3):
            ref[a, b * room : b * room + count] = weight[a, b].astype(F32)
    return ref[...].astype(BF).reshape(3 * OWN, OWN)


def stack_outputs(ref, weight):
    ref[...] = jnp.zeros_like(ref)
    for a in range(3):
        for b in range(3):
            at = (a * 3 + b) * 8 + 4
            ref[at : at + 4] = weight[a, b].astype(F32)
    return ref[...].astype(BF)


def step_kernel(
    scale,
    place,
    own,
    pair,
    across,
    w_first,
    w_middle,
    w_last,
    w_in,
    w_down,
    w_up,
    w_out,
    mine,
    other,
    tiles,
    *scratch,
):
    (
        stack,
        stack_o,
        field,
        net,
        hid,
        act_c,
        taps,
        residuals,
        noisies,
        slope_a,
        act_a,
        pairs,
        pooled,
        act_b,
        slope_b,
        up_taps,
        phases,
        slope_c,
        grad_f,
        spread_f,
        back_c,
        grad_c,
        blocks,
        grad_b,
        grad_a,
        last_sum,
        den,
        halves,
        w_near,
        sems,
    ) = scratch
    for ref in (net, hid, pooled, up_taps, taps, grad_f, grad_c, grad_b):
        zero_edges(ref)
    even = place[1] == 0
    fetch = pltpu.make_async_copy(w_middle, w_near, sems.at[2])
    fetch.start()
    first_w = stack_inputs(stack, w_first, 16)

    def gather(r):
        near, far = pair[r], across[r]
        wide = with_halo(own[r], jnp.where(even, far, near), jnp.where(even, near, far))
        field[r] = wide
        net[r + 1] = to_cells(lon_shifts(wide[8:24]))

    each(ROWS, gather, CHUNK["gather"])

    n1, u1 = CHUNK["first"]

    def first(i):
        pre = mm(three_rows(net, n1 * i, n1), first_w)
        hid[pl.ds(n1 * i + 1, n1)] = jax.nn.silu(pre).astype(BF).reshape(n1, WIDE, HID1)

    each(ROWS // n1, first, u1)
    fetch.wait()
    middle_w = jnp.concatenate([w_near[a] for a in range(3)], axis=1)

    n2, u2 = CHUNK["second"]

    def second(i):
        pre = lon_sum(mm_nt(three_rows(hid, n2 * i, n2), middle_w), n2, WIDE, HID1)
        act_c[pl.ds(n2 * i, n2)] = jax.nn.silu(pre).astype(BF)

    each(ROWS // n2, second, u2)
    last_w = stack_outputs(stack_o, w_last)[0:72]

    def mean_taps(r):
        taps[r + 1] = mm_nt(last_w, to_lanes(act_c[r]))

    each(ROWS, mean_taps, CHUNK["taps"])
    in_w = stack_inputs(stack, w_in, FIELDS)
    lane = lax.broadcasted_iota(jnp.int32, (8, LANES), 1)
    held = (lane < OWN + HALO) | (lane >= LANES - HALO)
    low_half = lax.broadcasted_iota(jnp.int32, (8, LANES), 0) < 4

    def enter(r):
        mean_r = four_channels(taps, r).astype(BF).astype(F32)
        sigma = jnp.where(held, jnp.broadcast_to(field[r, 1:2], (8, LANES)), 1.0)
        residual = field[r, 0:8] - mean_r
        noisy = residual + sigma * field[r, 16:24]
        variance = sigma * sigma + 0.25
        residuals[r] = residual
        noisies[r] = noisy
        scaled = (lax.rsqrt(variance) * noisy).astype(BF).astype(F32)
        both = jnp.where(low_half, pltpu.roll(mean_r, 4, 0), scaled)
        net[r + 1] = to_cells(lon_shifts(jnp.concatenate([both, field[r, 8:24]], axis=0)))

    each(ROWS, enter, CHUNK["enter"])

    n3, u3 = CHUNK["one"]

    def level_one(i):
        pre = mm(three_rows(net, n3 * i, n3), in_w)
        gate = jax.nn.sigmoid(pre)
        slope_a[pl.ds(n3 * i, n3)] = (gate * (1.0 + pre * (1.0 - gate))).reshape(n3, WIDE, HID1)
        act = (pre * gate).astype(BF).reshape(n3, WIDE, HID1)
        act_a[pl.ds(n3 * i, n3)] = act
        wide = act.astype(F32)
        for k in range(n3 // 2):
            row = (n3 // 2) * i + k
            pairs[row] = wide[2 * k] + wide[2 * k + 1]
            total = pairs[row, pl.ds(0, WLOW, stride=2)] + pairs[row, pl.ds(1, WLOW, stride=2)]
            pooled[row + 1] = (0.25 * total).astype(BF)

    each(ROWS // n3, level_one, u3)
    down_w = jnp.concatenate([w_down[a] for a in range(3)], axis=1)

    n4, u4 = CHUNK["two"]

    def level_two(i):
        pre = lon_sum(mm_nt(three_rows(pooled, n4 * i, n4), down_w), n4, WLOW, HID2)
        gate = jax.nn.sigmoid(pre)
        slope_b[pl.ds(n4 * i, n4)] = gate * (1.0 + pre * (1.0 - gate))
        act_b[pl.ds(n4 * i, n4)] = (pre * gate).astype(BF)

    each(LOW // n4, level_two, u4)
    n5, u5 = CHUNK["up"]

    def up_products(i):
        low = act_b[pl.ds(n5 * i, n5)].reshape(n5 * WLOW, HID2)
        up_taps[pl.ds(n5 * i + 1, n5)] = mm_nt(low, w_up[...]).reshape(n5, WLOW, 9 * HID1)

    each(LOW // n5, up_products, u5)

    def level_three(i):
        for pi in range(2):
            sums = []
            for b in range(3):
                total = None
                for a in range(3):
                    row = i + 1 + (pi + a - 1) // 2
                    at = (a * 3 + b) * HID1
                    part = up_taps[row, :, at : at + HID1]
                    total = part if total is None else total + part
                sums.append(total)
            row = 2 * i + pi
            phases[row, pl.ds(0, WLOW, stride=2)] = ahead(sums[0], 0) + sums[1] + sums[2]
            phases[row, pl.ds(1, WLOW, stride=2)] = sums[0] + sums[1] + back(sums[2], 0)
            pre = phases[row]
            gate = jax.nn.sigmoid(pre)
            act_c[row] = (pre * gate + act_a[row].astype(F32)).astype(BF)
            slope_c[row] = gate * (1.0 + pre * (1.0 - gate))

    each(LOW, level_three, CHUNK["three"])
    out_w = stack_outputs(stack_o, w_out)

    def field_taps(r):
        taps[r + 1] = mm_nt(out_w[0:72], to_lanes(act_c[r]))

    each(ROWS, field_taps, CHUNK["taps"])

    def loss(i):
        for k in range(2):
            r = 2 * i + k
            value = four_channels(taps, r)
            sigma = jnp.where(held, jnp.broadcast_to(field[r, 1:2], (8, LANES)), 1.0)
            weight = jnp.broadcast_to(field[r, 0:1], (8, LANES))
            variance = sigma * sigma + 0.25
            c_out = 0.5 * sigma * lax.rsqrt(variance)
            lam = variance / (0.25 * sigma * sigma)
            denoised = (0.25 / variance) * noisies[r] + c_out * value
            den[i, 4 * k : 4 * k + 4] = denoised[4:8, :OWN]
            loss_grad = (2.0 * scale) * weight * lam * (denoised - residuals[r])
            cot = (c_out * loss_grad).astype(BF).astype(F32)
            grad_f[r + 1] = jnp.where(low_half, 0.0, cot)

    each(LOW, loss, CHUNK["loss"])
    tiles[...] = den[...].astype(BF)
    last_sum[...] = jnp.zeros_like(last_sum)

    def last_grads(r):
        parts = []
        for a in range(3):
            cot = grad_f[r + 2 - a]
            parts += [back(cot, 1), cot, ahead(cot, 1)]
        cots = jnp.concatenate(parts + [jnp.zeros((8, LANES), F32)], axis=0)
        last_sum[...] += mm(cots[:, :OWN].astype(BF), act_c[r, 0:OWN])
        spread_f[r] = to_cells(cots)

    each(ROWS, last_grads, CHUNK["last"])
    near, far = 0, 1

    def keep(half, at, value):
        halves[half, at : at + value.shape[0]] = value.astype(BF)

    def send(half):
        for core, target in ((half, mine), (1 - half, other)):

            @pl.when(place[0] == core)
            def _():
                pltpu.make_async_copy(halves.at[half], target, sems.at[half]).start()

    keep(near, BIG_ROWS, last_sum[0:LAST_ROWS])
    keep(near, BIG_ROWS + LAST_ROWS, jnp.zeros((HALF_ROWS - BIG_ROWS - LAST_ROWS, OWN), F32))

    n6, u6 = CHUNK["back_three"]

    def back_three(i):
        wide = mm(spread_f[pl.ds(n6 * i, n6)].reshape(n6 * WIDE, OWN), out_w)
        wide = wide.reshape(n6, WIDE, HID1)
        back_c[pl.ds(n6 * i, n6)] = wide
        grad_c[pl.ds(n6 * i + 1, n6)] = wide * slope_c[pl.ds(n6 * i, n6)]

    each(ROWS // n6, back_three, u6)

    def block_sums(i):
        even = [grad_c[2 * i + k, pl.ds(0, WLOW, stride=2)] for k in range(4)]
        odd = [grad_c[2 * i + k, pl.ds(1, WLOW, stride=2)] for k in range(4)]
        for a in range(3):
            e, o = even[2 - a] + even[3 - a], odd[2 - a] + odd[3 - a]
            for b, total in enumerate((o + back(e, 0), e + o, ahead(o, 0) + e)):
                at = (a * 3 + b) * HID1
                blocks[i, :, at : at + HID1] = total.astype(BF)

    each(LOW, block_sums, CHUNK["blocks"])

    n7, u7 = CHUNK["back_two"]

    def back_two(i):
        low = mm(blocks[pl.ds(n7 * i, n7)].reshape(n7 * WLOW, 9 * HID1), w_up[...])
        cot = low.reshape(n7, WLOW, HID2) * slope_b[pl.ds(n7 * i, n7)]
        shifts = jnp.concatenate([back(cot, 1), cot, ahead(cot, 1)], axis=2)
        grad_b[pl.ds(n7 * i + 1, n7)] = shifts.astype(BF)

    each(LOW // n7, back_two, u7)
    held_low = OWN // 2
    cells = LOW * held_low
    low_b = act_b[:, :held_low].reshape(cells, HID2)
    for k in range(3):
        at = 3 * HID1 * k
        up = mm_tn(blocks[:, :held_low, at : at + 3 * HID1].reshape(cells, 3 * HID1), low_b)
        keep(near, at, up[:, :HID1])
        keep(near, at + UP_ROWS, up[:, HID1:])
    send(near)
    low_a = jnp.concatenate(
        [pooled[a : a + LOW, :held_low].reshape(cells, HID1) for a in range(3)], axis=1
    )
    for b in range(3):
        at = HID2 * b
        down = mm_tn(grad_b[1 : LOW + 1, :held_low, at : at + HID2].reshape(cells, HID2), low_a)
        for a in range(3):
            keep(far, (a * 3 + b) * HID2, down[:, HID1 * a : HID1 * (a + 1)])
    n8, u8 = CHUNK["back_one"]

    def back_one(i):
        total = None
        for a in range(3):
            cot = grad_b[pl.ds(n8 * i + 2 - a, n8)].reshape(n8 * WLOW, 3 * HID2)
            part = mm(cot, w_down[a])
            total = part if total is None else total + part
        low = (0.25 * total).reshape(n8, WLOW, HID1)
        for k in range(n8):
            row = n8 * i + k
            phases[row, pl.ds(0, WLOW, stride=2)] = low[k]
            phases[row, pl.ds(1, WLOW, stride=2)] = low[k]
            spread = phases[row, 0:OWN]
            for pi in range(2):
                r = 2 * row + pi
                grad_a[r] = ((back_c[r, 0:OWN] + spread) * slope_a[r, 0:OWN]).astype(BF)

    each(LOW // n8, back_one, u8)
    near_cells = jnp.concatenate(
        [net[a : a + ROWS, :OWN].reshape(ROWS * OWN, OWN) for a in range(3)], axis=1
    )
    inputs = mm_tn(grad_a[...].reshape(ROWS * OWN, HID1), near_cells)
    for a in range(3):
        part = inputs[:, a * OWN : (a + 1) * OWN].T
        keep(far, BIG_ROWS + a * 3 * FIELDS, part[: 3 * FIELDS])
    keep(far, BIG_ROWS + IN_ROWS, jnp.zeros((HALF_ROWS - BIG_ROWS - IN_ROWS, OWN), F32))
    send(far)
    for half in (near, far):
        pltpu.make_async_copy(halves.at[half], mine, sems.at[half]).wait()


def unpack_kernel(place, mine, other, seats, tile, first, down, up, last, downs, ups, firsts, lasts, tiles, sems):
    even = place[0] == 0

    def half(k, at, count):
        one, two = mine[pl.ds(at, count)], other[pl.ds(at, count)]
        return (jnp.where(even, one, two) if k == 0 else jnp.where(even, two, one)).astype(F32)

    def leave(a):
        return (
            pltpu.make_async_copy(ups.at[a], up.at[a], sems.at[0]),
            pltpu.make_async_copy(downs.at[a], down.at[a], sems.at[1]),
        )

    def thirds(a):
        at = pl.multiple_of(a * (3 * HID1), 3 * HID1)
        for k in range(2):
            piece = half(0, at + k * UP_ROWS, 3 * HID1)
            ups[a, :, :, k * HID1 : (k + 1) * HID1] = piece.reshape(3, HID1, HID1)
        downs[a] = half(1, 2 * at, 3 * HID2).reshape(3, HID2, HID1)
        for copy in leave(a):
            copy.start()

    each(3, thirds)
    inputs = half(1, BIG_ROWS, IN_ROWS)
    outputs = half(0, BIG_ROWS, 80)
    for a in range(3):
        for b in range(3):
            at = (a * 3 + b) * FIELDS
            firsts[a, b] = inputs[at : at + 20]
            at = (a * 3 + b) * 8 + 4
            lasts[a, b] = outputs[at : at + 4]
    small = [pltpu.make_async_copy(firsts, first, sems.at[2]), pltpu.make_async_copy(lasts, last, sems.at[3])]
    for copy in small:
        copy.start()
    blocks = seats[...].astype(F32)
    for k in range(8):
        for r in range(2):
            tiles[:, r, k * OWN : (k + 1) * OWN] = blocks[k, 4 * r : 4 * r + 4]
    small.append(pltpu.make_async_copy(tiles, tile, sems.at[4]))
    small[2].start()
    for copy in small:
        copy.wait()
    for a in range(3):
        for copy in leave(a):
            copy.wait()


def in_vmem(count):
    return [pl.BlockSpec(memory_space=pltpu.MemorySpace.VMEM) for _ in range(count)]


def in_hbm(count):
    return [pl.BlockSpec(memory_space=pltpu.MemorySpace.HBM) for _ in range(count)]


def in_smem():
    return pl.BlockSpec(memory_space=pltpu.MemorySpace.SMEM)


def pack(target, noise, land_mask, level_index):
    lats = target.shape[2] // OWN
    return pl.pallas_call(
        pack_kernel,
        out_shape=jax.ShapeDtypeStruct((lats, 2, 16, OWN), F32),
        in_specs=[in_smem(), *in_hbm(3)],
        out_specs=in_vmem(1)[0],
        scratch_shapes=[
            pltpu.VMEM(target.shape, F32),
            pltpu.VMEM(noise.shape, F32),
            pltpu.VMEM(land_mask.shape, jnp.int32),
            pltpu.SemaphoreType.DMA((3,)),
        ],
        compiler_params=pltpu.CompilerParams(vmem_limit_bytes=8 * 2**20),
        name="pack",
    )(level_index, target, noise, land_mask)


def step(scale, *operands):
    def kernel(*refs):
        step_kernel(scale, *refs)

    return pl.pallas_call(
        kernel,
        out_shape=(
            jax.ShapeDtypeStruct((HALF_ROWS, OWN), BF),
            jax.ShapeDtypeStruct((HALF_ROWS, OWN), BF),
            jax.ShapeDtypeStruct((LOW, CELL_ROWS, OWN), BF),
        ),
        in_specs=[in_smem(), *in_vmem(4), *in_hbm(1), *in_vmem(5)],
        out_specs=tuple(in_vmem(3)),
        scratch_shapes=[
            pltpu.VMEM((3, OWN, OWN), F32),
            pltpu.VMEM((OWN, OWN), F32),
            pltpu.VMEM((ROWS, FIELDS, LANES), F32),
            pltpu.VMEM((ROWS + 2, WIDE, OWN), BF),
            pltpu.VMEM((ROWS + 2, WIDE, HID1), BF),
            pltpu.VMEM((ROWS, WIDE, HID1), BF),
            pltpu.VMEM((ROWS + 2, 72, LANES), F32),
            pltpu.VMEM((ROWS, 8, LANES), F32),
            pltpu.VMEM((ROWS, 8, LANES), F32),
            pltpu.VMEM((ROWS, WIDE, HID1), F32),
            pltpu.VMEM((ROWS, WIDE, HID1), BF),
            pltpu.VMEM((LOW, WIDE, HID1), F32),
            pltpu.VMEM((LOW + 2, WLOW, HID1), BF),
            pltpu.VMEM((LOW, WLOW, HID2), BF),
            pltpu.VMEM((LOW, WLOW, HID2), F32),
            pltpu.VMEM((LOW + 2, WLOW, 9 * HID1), F32),
            pltpu.VMEM((ROWS, WIDE, HID1), F32),
            pltpu.VMEM((ROWS, WIDE, HID1), F32),
            pltpu.VMEM((ROWS + 2, 8, LANES), F32),
            pltpu.VMEM((ROWS, WIDE, OWN), BF),
            pltpu.VMEM((ROWS, WIDE, HID1), F32),
            pltpu.VMEM((ROWS + 2, WIDE, HID1), F32),
            pltpu.VMEM((LOW, WLOW, 9 * HID1), BF),
            pltpu.VMEM((LOW + 2, WLOW, 3 * HID2), BF),
            pltpu.VMEM((ROWS, OWN, HID1), BF),
            pltpu.VMEM((80, HID1), F32),
            pltpu.VMEM((LOW, CELL_ROWS, OWN), F32),
            pltpu.VMEM((2, HALF_ROWS, OWN), BF),
            pltpu.VMEM((3, 3 * HID1, HID1), BF),
            pltpu.SemaphoreType.DMA((3,)),
        ],
        compiler_params=pltpu.CompilerParams(vmem_limit_bytes=44 * 2**20),
        name="step",
    )(*operands)


def unpack(place, mine, other, seats):
    outs = (
        (4, 2, 8 * OWN),
        (3, 3, 20, HID1),
        (3, 3, HID2, HID1),
        (3, 3, HID1, HID2),
        (3, 3, 4, HID1),
    )
    return pl.pallas_call(
        unpack_kernel,
        out_shape=tuple(jax.ShapeDtypeStruct(shape, F32) for shape in outs),
        in_specs=[in_smem(), *in_vmem(3)],
        out_specs=tuple([pl.BlockSpec(memory_space=pl.ANY)] * 5),
        scratch_shapes=[
            *(pltpu.VMEM(outs[k], F32) for k in (2, 3, 1, 4, 0)),
            pltpu.SemaphoreType.DMA((5,)),
        ],
        compiler_params=pltpu.CompilerParams(vmem_limit_bytes=16 * 2**20),
        name="unpack",
    )(place, mine, other, seats)


def all_to_all(value, axes):
    return lax.all_to_all(value, axes, split_axis=0, concat_axis=0, tiled=True)


def swap(value, axes, offset):
    count = lax.axis_size(axes)
    pairs = []
    for i in range(offset, count + offset, 2):
        here, there = i % count, (i + 1) % count
        pairs += [(here, there), (there, here)]
    return lax.ppermute(value, axes, sorted(set(pairs)))


def local(
    coarse,
    target,
    noise,
    land_mask,
    level_index,
    frozen_first,
    frozen_middle,
    frozen_last,
    diffuse_in,
    diffuse_down,
    diffuse_up,
    diffuse_out,
):
    scale = 1.0 / (target.shape[0] * math.sqrt(target.shape[1] * target.shape[2] * lax.axis_size(STRIPS)))
    place = jnp.stack([lax.axis_index("core"), lax.axis_index("z") % 2])
    place = place.astype(jnp.int32)
    packed = all_to_all(pack(target, noise, land_mask, level_index), LAT).reshape(ROWS, 16, OWN)
    fields = jnp.concatenate([packed[:, :8], coarse.transpose(1, 0, 2).astype(F32), packed[:, 12:]], axis=1)
    across = swap(fields, STRIPS, 1)
    pair = swap(fields, STRIPS, 0)
    grads, partner, tiles = step(
        scale,
        place,
        fields,
        pair,
        across,
        frozen_first.transpose(0, 1, 3, 2),
        frozen_middle.reshape(3, 3 * HID1, HID1),
        frozen_last,
        diffuse_in.transpose(0, 1, 3, 2),
        diffuse_down.reshape(3, 3 * HID2, HID1),
        diffuse_up.reshape(9 * HID1, HID2),
        diffuse_out,
    )
    chips = lax.axis_size(CHIPS)
    rows = HALF_ROWS // chips
    lats = tiles.shape[0]
    half = grads.astype(F32) + swap(partner, "core", 0).astype(F32)
    blocks = jnp.broadcast_to(tiles[None], (chips // lats, *tiles.shape)).reshape(chips, CELL_ROWS, OWN)
    sent = jnp.concatenate([half.astype(BF).reshape(chips, rows, OWN), blocks], axis=1)
    parts = all_to_all(sent, CHIPS)
    total = parts[:, :rows].astype(F32).sum(0).astype(BF)
    seats = parts.reshape(chips // lats, lats, rows + CELL_ROWS, OWN)[:, :, rows:]
    seats = lax.dynamic_index_in_dim(seats, lax.axis_index(("y", "x_hi")), 0, False)
    with jax.named_scope("spread"):
        mine = all_to_all(jnp.broadcast_to(total[None], (chips, rows, OWN)), CHIPS).reshape(HALF_ROWS, OWN)
    tile, first, down, up, last = unpack(place, mine, swap(mine, "core", 0), seats)
    return (tile, first.transpose(0, 1, 3, 2), down, up, last)


def solution(mesh):
    fine = Mesh(mesh.devices.reshape(4, 2, 2, 2, 4), LON + LAT)
    tile = P(None, LAT, LON)
    return jax.shard_map(
        local,
        mesh=fine,
        in_specs=(
            P(None, None, STRIPS),
            tile,
            tile,
            P(LAT, LON),
            P(LAT, LON),
            *([P()] * 7),
        ),
        out_specs=(tile, P(), P(), P(), P()),
        check_vma=False,
    )
```

```python
import math

import jax
import jax.numpy as jnp
from jax import lax
from jax.experimental import pallas as pl
from jax.experimental.pallas import tpu as pltpu
from jax.sharding import Mesh
from jax.sharding import PartitionSpec as P

LEVELS = 32
ROWS = 16
LOW = ROWS // 2
OWN = 128
HALO = 16
WIDE = OWN + 2 * HALO
WLOW = WIDE // 2
LANES = 256
HID1 = 128
HID2 = 256
BF = jnp.bfloat16
F32 = jnp.float32

LON = ("y", "x_hi", "core")
LAT = ("x_lo", "z")
CHIPS = ("y", "x_hi", "x_lo", "z")
STRIPS = LON + LAT

FIELDS = 24
UP_ROWS = 9 * HID1
DOWN_ROWS = 9 * HID2
BIG_ROWS = 2304
LAST_ROWS = 72
IN_ROWS = 9 * FIELDS
HALF_ROWS = 2560
CELL_ROWS = 8
CHUNK = {
    "gather": 8,
    "first": (8, 1),
    "second": (2, 2),
    "taps": 8,
    "enter": 8,
    "one": (8, 1),
    "two": (4, 2),
    "up": (8, 1),
    "three": 2,
    "loss": 4,
    "last": 8,
    "back_three": (8, 1),
    "blocks": 4,
    "back_two": (2, 4),
    "back_one": 4,
}


def mm(x, w):
    return lax.dot_general(x, w, (((1,), (0,)), ((), ())), preferred_element_type=F32)


def mm_nt(x, w):
    return lax.dot_general(x, w, (((1,), (1,)), ((), ())), preferred_element_type=F32)


def mm_tn(x, w):
    return lax.dot_general(x, w, (((0,), (0,)), ((), ())), preferred_element_type=F32)


def back(x, axis):
    return pltpu.roll(x, x.shape[axis] - 1, axis)


def ahead(x, axis):
    return pltpu.roll(x, 1, axis)


def with_halo(own, left, right):
    lane = lax.broadcasted_iota(jnp.int32, own.shape, 1)
    halo = jnp.where(lane < HALO, right, jnp.where(lane >= OWN - HALO, left, 0.0))
    return jnp.concatenate([own, halo], axis=1)


def to_cells(stack):
    pad = OWN - stack.shape[0]
    if pad:
        stack = jnp.concatenate([stack, jnp.zeros((pad, LANES), F32)], axis=0)
    cells = stack.T
    return jnp.concatenate([cells[: OWN + HALO], cells[LANES - HALO :]], axis=0).astype(BF)


def to_lanes(cells):
    gap = jnp.zeros((LANES - WIDE, cells.shape[1]), cells.dtype)
    return jnp.concatenate([cells[: OWN + HALO], gap, cells[OWN + HALO :]], axis=0)


def lon_shifts(field):
    return jnp.concatenate([ahead(field, 1), field, back(field, 1)], axis=0)


def three_rows(ref, start, count):
    width = ref.shape[1]
    return jnp.concatenate(
        [ref[pl.ds(start + a, count)].reshape(count * width, ref.shape[2]) for a in range(3)], axis=1
    )


def lon_sum(taps, count, width, out):
    first, second, third = (
        taps[:, b * out : (b + 1) * out].reshape(count, width, out) for b in range(3)
    )
    return ahead(first, 1) + second + back(third, 1)


def four_channels(ref, row):
    sums = []
    for b in range(3):
        at = [(a * 3 + b) * 8 for a in range(3)]
        sums.append(
            ref[row, at[0] : at[0] + 8]
            + ref[row + 1, at[1] : at[1] + 8]
            + ref[row + 2, at[2] : at[2] + 8]
        )
    return ahead(sums[0], 1) + sums[1] + back(sums[2], 1)


def zero_edges(ref):
    edge = jnp.zeros(ref.shape[1:], ref.dtype)
    ref[0] = edge
    ref[ref.shape[0] - 1] = edge


def each(count, body, unroll=1):
    def step(i, carry):
        body(i)
        return carry

    lax.fori_loop(0, count, step, 0, unroll=unroll)


def pack_kernel(level, target_far, noise_far, mask_far, packed, target, noise, land_mask, sems):
    arrive = [
        pltpu.make_async_copy(target_far, target, sems.at[0]),
        pltpu.make_async_copy(noise_far, noise, sems.at[1]),
        pltpu.make_async_copy(mask_far, land_mask, sems.at[2]),
    ]
    for copy in arrive:
        copy.start()
    power = jnp.full((1, OWN), level[0, 0], jnp.int32).astype(F32) / (LEVELS - 1)
    sigma = 0.02 * jnp.exp(power * math.log(4000.0))
    for copy in arrive:
        copy.wait()
    weight = 1.0 + land_mask[...].astype(F32)
    for p in range(packed.shape[0]):
        lanes = slice(p * OWN, (p + 1) * OWN)
        for r in range(2):
            packed[p, r, 0:1] = weight[r : r + 1, lanes]
            packed[p, r, 1:2] = sigma
            packed[p, r, 2:4] = jnp.zeros((2, OWN), F32)
            packed[p, r, 4:8] = target[:, r, lanes]
            packed[p, r, 8:12] = jnp.zeros((4, OWN), F32)
            packed[p, r, 12:16] = noise[:, r, lanes]


def stack_inputs(ref, weight, room):
    ref[...] = jnp.zeros_like(ref)
    count = weight.shape[2]
    for a in range(3):
        for b in range(3):
            ref[a, b * room : b * room + count] = weight[a, b].astype(F32)
    return ref[...].astype(BF).reshape(3 * OWN, OWN)


def stack_outputs(ref, weight):
    ref[...] = jnp.zeros_like(ref)
    for a in range(3):
        for b in range(3):
            at = (a * 3 + b) * 8 + 4
            ref[at : at + 4] = weight[a, b].astype(F32)
    return ref[...].astype(BF)


def step_kernel(
    scale,
    place,
    own,
    pair,
    across,
    w_first,
    w_middle,
    w_last,
    w_in,
    w_down,
    w_up,
    w_out,
    mine,
    other,
    tiles,
    *scratch,
):
    (
        stack,
        stack_o,
        field,
        net,
        hid,
        act_c,
        taps,
        residuals,
        noisies,
        slope_a,
        act_a,
        pairs,
        pooled,
        act_b,
        slope_b,
        up_taps,
        phases,
        slope_c,
        grad_f,
        spread_f,
        back_c,
        grad_c,
        blocks,
        grad_b,
        grad_a,
        last_sum,
        den,
        halves,
        w_near,
        pair_w,
        low_taps,
        sems,
    ) = scratch
    for ref in (net, pooled, up_taps, taps, grad_f, grad_c, grad_b, low_taps):
        zero_edges(ref)
    hid[0, 0] = jnp.zeros((WIDE, HID1), BF)
    hid[LOW, 1] = jnp.zeros((WIDE, HID1), BF)
    even = place[1] == 0
    fetch = pltpu.make_async_copy(w_middle, w_near, sems.at[2])
    fetch.start()
    first_w = stack_inputs(stack, w_first, 16)

    def gather(r):
        near, far = pair[r], across[r]
        wide = with_halo(own[r], jnp.where(even, far, near), jnp.where(even, near, far))
        field[r] = wide
        net[r + 1] = to_cells(lon_shifts(wide[8:24]))

    each(ROWS, gather, CHUNK["gather"])

    n1, u1 = CHUNK["first"]

    def first(i):
        pre = mm(three_rows(net, n1 * i, n1), first_w)
        act = jax.nn.silu(pre).astype(BF).reshape(n1 // 2, 2, WIDE, HID1)
        hid[pl.ds((n1 // 2) * i, n1 // 2), 1] = act[:, 0]
        hid[pl.ds((n1 // 2) * i + 1, n1 // 2), 0] = act[:, 1]

    each(ROWS // n1, first, u1)
    fetch.wait()
    gap = jnp.zeros((HID1, HID1), BF)
    for b in range(3):
        taps_b = [w_near[a, b * HID1 : (b + 1) * HID1] for a in range(3)]
        pair_w[b, 0:HID1] = jnp.concatenate([*taps_b, gap], axis=1)
        pair_w[b, HID1:] = jnp.concatenate([gap, *taps_b], axis=1)
    n2, u2 = CHUNK["second"]

    def second(i):
        rows = [hid[pl.ds(n2 * i + j // 2, n2), j % 2].reshape(n2 * WIDE, HID1) for j in range(4)]
        quads = jnp.concatenate(rows, axis=1)
        parts = [mm_nt(quads, pair_w[b]).reshape(n2, WIDE, 2 * HID1) for b in range(3)]
        act = jax.nn.silu(ahead(parts[0], 1) + parts[1] + back(parts[2], 1)).astype(BF)
        for k in range(n2):
            row = 2 * (n2 * i + k)
            act_c[row] = act[k, :, :HID1]
            act_c[row + 1] = act[k, :, HID1:]

    each(LOW // n2, second, u2)
    last_w = stack_outputs(stack_o, w_last)[0:72]

    def mean_taps(r):
        taps[r + 1] = mm_nt(last_w, to_lanes(act_c[r]))

    each(ROWS, mean_taps, CHUNK["taps"])
    in_w = stack_inputs(stack, w_in, FIELDS)
    lane = lax.broadcasted_iota(jnp.int32, (8, LANES), 1)
    held = (lane < OWN + HALO) | (lane >= LANES - HALO)
    low_half = lax.broadcasted_iota(jnp.int32, (8, LANES), 0) < 4

    def enter(r):
        mean_r = four_channels(taps, r).astype(BF).astype(F32)
        sigma = jnp.where(held, jnp.broadcast_to(field[r, 1:2], (8, LANES)), 1.0)
        residual = field[r, 0:8] - mean_r
        noisy = residual + sigma * field[r, 16:24]
        variance = sigma * sigma + 0.25
        residuals[r] = residual
        noisies[r] = noisy
        scaled = (lax.rsqrt(variance) * noisy).astype(BF).astype(F32)
        both = jnp.where(low_half, pltpu.roll(mean_r, 4, 0), scaled)
        net[r + 1] = to_cells(lon_shifts(jnp.concatenate([both, field[r, 8:24]], axis=0)))

    each(ROWS, enter, CHUNK["enter"])

    n3, u3 = CHUNK["one"]

    def level_one(i):
        pre = mm(three_rows(net, n3 * i, n3), in_w)
        gate = jax.nn.sigmoid(pre)
        slope_a[pl.ds(n3 * i, n3)] = (gate * (1.0 + pre * (1.0 - gate))).reshape(n3, WIDE, HID1)
        act = (pre * gate).astype(BF).reshape(n3, WIDE, HID1)
        act_a[pl.ds(n3 * i, n3)] = act
        wide = act.astype(F32)
        for k in range(n3 // 2):
            row = (n3 // 2) * i + k
            pairs[row] = wide[2 * k] + wide[2 * k + 1]
            total = pairs[row, pl.ds(0, WLOW, stride=2)] + pairs[row, pl.ds(1, WLOW, stride=2)]
            pooled[row + 1] = (0.25 * total).astype(BF)

    each(ROWS // n3, level_one, u3)
    down_w = jnp.concatenate([w_down[a] for a in range(3)], axis=1)

    n4, u4 = CHUNK["two"]

    def level_two(i):
        pre = lon_sum(mm_nt(three_rows(pooled, n4 * i, n4), down_w), n4, WLOW, HID2)
        gate = jax.nn.sigmoid(pre)
        slope_b[pl.ds(n4 * i, n4)] = gate * (1.0 + pre * (1.0 - gate))
        act_b[pl.ds(n4 * i, n4)] = (pre * gate).astype(BF)

    each(LOW // n4, level_two, u4)
    n5, u5 = CHUNK["up"]

    def up_products(i):
        low = act_b[pl.ds(n5 * i, n5)].reshape(n5 * WLOW, HID2)
        up_taps[pl.ds(n5 * i + 1, n5)] = mm_nt(low, w_up[...]).reshape(n5, WLOW, 9 * HID1)

    each(LOW // n5, up_products, u5)

    def level_three(i):
        for pi in range(2):
            sums = []
            for b in range(3):
                total = None
                for a in range(3):
                    row = i + 1 + (pi + a - 1) // 2
                    at = (a * 3 + b) * HID1
                    part = up_taps[row, :, at : at + HID1]
                    total = part if total is None else total + part
                sums.append(total)
            row = 2 * i + pi
            phases[row, pl.ds(0, WLOW, stride=2)] = ahead(sums[0], 0) + sums[1] + sums[2]
            phases[row, pl.ds(1, WLOW, stride=2)] = sums[0] + sums[1] + back(sums[2], 0)
            pre = phases[row]
            gate = jax.nn.sigmoid(pre)
            act_c[row] = (pre * gate + act_a[row].astype(F32)).astype(BF)
            slope_c[row] = gate * (1.0 + pre * (1.0 - gate))

    each(LOW, level_three, CHUNK["three"])
    out_w = stack_outputs(stack_o, w_out)

    def field_taps(r):
        taps[r + 1] = mm_nt(out_w[0:72], to_lanes(act_c[r]))

    each(ROWS, field_taps, CHUNK["taps"])

    def loss(i):
        for k in range(2):
            r = 2 * i + k
            value = four_channels(taps, r)
            sigma = jnp.where(held, jnp.broadcast_to(field[r, 1:2], (8, LANES)), 1.0)
            weight = jnp.broadcast_to(field[r, 0:1], (8, LANES))
            variance = sigma * sigma + 0.25
            c_out = 0.5 * sigma * lax.rsqrt(variance)
            lam = variance / (0.25 * sigma * sigma)
            denoised = (0.25 / variance) * noisies[r] + c_out * value
            den[i, 4 * k : 4 * k + 4] = denoised[4:8, :OWN]
            loss_grad = (2.0 * scale) * weight * lam * (denoised - residuals[r])
            cot = (c_out * loss_grad).astype(BF).astype(F32)
            grad_f[r + 1] = jnp.where(low_half, 0.0, cot)

    each(LOW, loss, CHUNK["loss"])
    tiles[...] = den[...].astype(BF)
    last_sum[...] = jnp.zeros_like(last_sum)

    def last_grads(r):
        parts = []
        for a in range(3):
            cot = grad_f[r + 2 - a]
            parts += [back(cot, 1), cot, ahead(cot, 1)]
        cots = jnp.concatenate(parts + [jnp.zeros((8, LANES), F32)], axis=0)
        last_sum[...] += mm(cots[:, :OWN].astype(BF), act_c[r, 0:OWN])
        spread_f[r] = to_cells(cots)

    each(ROWS, last_grads, CHUNK["last"])
    near, far = 0, 1

    def keep(half, at, value):
        halves[half, at : at + value.shape[0]] = value.astype(BF)

    def send(half):
        for core, target in ((half, mine), (1 - half, other)):

            @pl.when(place[0] == core)
            def _():
                pltpu.make_async_copy(halves.at[half], target, sems.at[half]).start()

    keep(near, BIG_ROWS, last_sum[0:LAST_ROWS])
    keep(near, BIG_ROWS + LAST_ROWS, jnp.zeros((HALF_ROWS - BIG_ROWS - LAST_ROWS, OWN), F32))

    n6, u6 = CHUNK["back_three"]

    def back_three(i):
        wide = mm(spread_f[pl.ds(n6 * i, n6)].reshape(n6 * WIDE, OWN), out_w)
        wide = wide.reshape(n6, WIDE, HID1)
        back_c[pl.ds(n6 * i, n6)] = wide
        grad_c[pl.ds(n6 * i + 1, n6)] = wide * slope_c[pl.ds(n6 * i, n6)]

    each(ROWS // n6, back_three, u6)

    def block_sums(i):
        even = [grad_c[2 * i + k, pl.ds(0, WLOW, stride=2)] for k in range(4)]
        odd = [grad_c[2 * i + k, pl.ds(1, WLOW, stride=2)] for k in range(4)]
        for a in range(3):
            e, o = even[2 - a] + even[3 - a], odd[2 - a] + odd[3 - a]
            for b, total in enumerate((o + back(e, 0), e + o, ahead(o, 0) + e)):
                at = (a * 3 + b) * HID1
                blocks[i, :, at : at + HID1] = total.astype(BF)

    each(LOW, block_sums, CHUNK["blocks"])

    n7, u7 = CHUNK["back_two"]

    def back_two(i):
        low = mm(blocks[pl.ds(n7 * i, n7)].reshape(n7 * WLOW, 9 * HID1), w_up[...])
        cot = low.reshape(n7, WLOW, HID2) * slope_b[pl.ds(n7 * i, n7)]
        shifts = jnp.concatenate([back(cot, 1), cot, ahead(cot, 1)], axis=2)
        grad_b[pl.ds(n7 * i + 1, n7)] = shifts.astype(BF)

    each(LOW // n7, back_two, u7)
    held_low = OWN // 2
    cells = LOW * held_low
    low_b = act_b[:, :held_low].reshape(cells, HID2)
    for k in range(3):
        at = 3 * HID1 * k
        up = mm_tn(blocks[:, :held_low, at : at + 3 * HID1].reshape(cells, 3 * HID1), low_b)
        keep(near, at, up[:, :HID1])
        keep(near, at + UP_ROWS, up[:, HID1:])
    send(near)
    low_a = jnp.concatenate(
        [pooled[a : a + LOW, :held_low].reshape(cells, HID1) for a in range(3)], axis=1
    )
    for b in range(3):
        at = HID2 * b
        down = mm_tn(grad_b[1 : LOW + 1, :held_low, at : at + HID2].reshape(cells, HID2), low_a)
        for a in range(3):
            keep(far, (a * 3 + b) * HID2, down[:, HID1 * a : HID1 * (a + 1)])
    spread_w = jnp.concatenate([w_down[a] for a in range(3)], axis=1)
    wide = mm(grad_b[1 : LOW + 1, :held_low].reshape(cells, 3 * HID2), spread_w)
    low_taps[1 : LOW + 1] = wide.reshape(LOW, held_low, 3 * HID1)

    def back_one(i):
        low = (
            low_taps[i + 2, :, 0:HID1]
            + low_taps[i + 1, :, HID1 : 2 * HID1]
            + low_taps[i, :, 2 * HID1 :]
        )
        low = 0.25 * low
        phases[i, pl.ds(0, held_low, stride=2)] = low
        phases[i, pl.ds(1, held_low, stride=2)] = low
        spread = phases[i, 0:OWN]
        for pi in range(2):
            r = 2 * i + pi
            grad_a[r] = ((back_c[r, 0:OWN] + spread) * slope_a[r, 0:OWN]).astype(BF)

    each(LOW, back_one, CHUNK["back_one"])
    near_cells = jnp.concatenate(
        [net[a : a + ROWS, :OWN].reshape(ROWS * OWN, OWN) for a in range(3)], axis=1
    )
    inputs = mm_tn(grad_a[...].reshape(ROWS * OWN, HID1), near_cells)
    for a in range(3):
        part = inputs[:, a * OWN : (a + 1) * OWN].T
        keep(far, BIG_ROWS + a * 3 * FIELDS, part[: 3 * FIELDS])
    keep(far, BIG_ROWS + IN_ROWS, jnp.zeros((HALF_ROWS - BIG_ROWS - IN_ROWS, OWN), F32))
    send(far)
    for half in (near, far):
        pltpu.make_async_copy(halves.at[half], mine, sems.at[half]).wait()


def unpack_kernel(place, mine, other, seats, tile, first, down, up, last, downs, ups, firsts, lasts, tiles, sems):
    even = place[0] == 0

    def half(k, at, count):
        one, two = mine[pl.ds(at, count)], other[pl.ds(at, count)]
        return (jnp.where(even, one, two) if k == 0 else jnp.where(even, two, one)).astype(F32)

    def leave(a):
        return (
            pltpu.make_async_copy(ups.at[a], up.at[a], sems.at[0]),
            pltpu.make_async_copy(downs.at[a], down.at[a], sems.at[1]),
        )

    def thirds(a):
        at = pl.multiple_of(a * (3 * HID1), 3 * HID1)
        for k in range(2):
            piece = half(0, at + k * UP_ROWS, 3 * HID1)
            ups[a, :, :, k * HID1 : (k + 1) * HID1] = piece.reshape(3, HID1, HID1)
        downs[a] = half(1, 2 * at, 3 * HID2).reshape(3, HID2, HID1)
        for copy in leave(a):
            copy.start()

    each(3, thirds)
    inputs = half(1, BIG_ROWS, IN_ROWS)
    outputs = half(0, BIG_ROWS, 80)
    for a in range(3):
        for b in range(3):
            at = (a * 3 + b) * FIELDS
            firsts[a, b] = inputs[at : at + 20]
            at = (a * 3 + b) * 8 + 4
            lasts[a, b] = outputs[at : at + 4]
    small = [pltpu.make_async_copy(firsts, first, sems.at[2]), pltpu.make_async_copy(lasts, last, sems.at[3])]
    for copy in small:
        copy.start()
    blocks = seats[...].astype(F32)
    for k in range(8):
        for r in range(2):
            tiles[:, r, k * OWN : (k + 1) * OWN] = blocks[k, 4 * r : 4 * r + 4]
    small.append(pltpu.make_async_copy(tiles, tile, sems.at[4]))
    small[2].start()
    for copy in small:
        copy.wait()
    for a in range(3):
        for copy in leave(a):
            copy.wait()


def in_vmem(count):
    return [pl.BlockSpec(memory_space=pltpu.MemorySpace.VMEM) for _ in range(count)]


def in_hbm(count):
    return [pl.BlockSpec(memory_space=pltpu.MemorySpace.HBM) for _ in range(count)]


def in_smem():
    return pl.BlockSpec(memory_space=pltpu.MemorySpace.SMEM)


def pack(target, noise, land_mask, level_index):
    lats = target.shape[2] // OWN
    return pl.pallas_call(
        pack_kernel,
        out_shape=jax.ShapeDtypeStruct((lats, 2, 16, OWN), F32),
        in_specs=[in_smem(), *in_hbm(3)],
        out_specs=in_vmem(1)[0],
        scratch_shapes=[
            pltpu.VMEM(target.shape, F32),
            pltpu.VMEM(noise.shape, F32),
            pltpu.VMEM(land_mask.shape, jnp.int32),
            pltpu.SemaphoreType.DMA((3,)),
        ],
        name="pack",
    )(level_index, target, noise, land_mask)


def step(scale, *operands):
    def kernel(*refs):
        step_kernel(scale, *refs)

    return pl.pallas_call(
        kernel,
        out_shape=(
            jax.ShapeDtypeStruct((HALF_ROWS, OWN), BF),
            jax.ShapeDtypeStruct((HALF_ROWS, OWN), BF),
            jax.ShapeDtypeStruct((LOW, CELL_ROWS, OWN), BF),
        ),
        in_specs=[in_smem(), *in_vmem(4), *in_hbm(1), *in_vmem(5)],
        out_specs=tuple(in_vmem(3)),
        scratch_shapes=[
            pltpu.VMEM((3, OWN, OWN), F32),
            pltpu.VMEM((OWN, OWN), F32),
            pltpu.VMEM((ROWS, FIELDS, LANES), F32),
            pltpu.VMEM((ROWS + 2, WIDE, OWN), BF),
            pltpu.VMEM((LOW + 1, 2, WIDE, HID1), BF),
            pltpu.VMEM((ROWS, WIDE, HID1), BF),
            pltpu.VMEM((ROWS + 2, 72, LANES), F32),
            pltpu.VMEM((ROWS, 8, LANES), F32),
            pltpu.VMEM((ROWS, 8, LANES), F32),
            pltpu.VMEM((ROWS, WIDE, HID1), F32),
            pltpu.VMEM((ROWS, WIDE, HID1), BF),
            pltpu.VMEM((LOW, WIDE, HID1), F32),
            pltpu.VMEM((LOW + 2, WLOW, HID1), BF),
            pltpu.VMEM((LOW, WLOW, HID2), BF),
            pltpu.VMEM((LOW, WLOW, HID2), F32),
            pltpu.VMEM((LOW + 2, WLOW, 9 * HID1), F32),
            pltpu.VMEM((ROWS, WIDE, HID1), F32),
            pltpu.VMEM((ROWS, WIDE, HID1), F32),
            pltpu.VMEM((ROWS + 2, 8, LANES), F32),
            pltpu.VMEM((ROWS, WIDE, OWN), BF),
            pltpu.VMEM((ROWS, WIDE, HID1), F32),
            pltpu.VMEM((ROWS + 2, WIDE, HID1), F32),
            pltpu.VMEM((LOW, WLOW, 9 * HID1), BF),
            pltpu.VMEM((LOW + 2, WLOW, 3 * HID2), BF),
            pltpu.VMEM((ROWS, OWN, HID1), BF),
            pltpu.VMEM((80, HID1), F32),
            pltpu.VMEM((LOW, CELL_ROWS, OWN), F32),
            pltpu.VMEM((2, HALF_ROWS, OWN), BF),
            pltpu.VMEM((3, 3 * HID1, HID1), BF),
            pltpu.VMEM((3, 2 * HID1, 4 * HID1), BF),
            pltpu.VMEM((LOW + 2, OWN // 2, 3 * HID1), F32),
            pltpu.SemaphoreType.DMA((3,)),
        ],
        compiler_params=pltpu.CompilerParams(vmem_limit_bytes=44 * 2**20),
        name="step",
    )(*operands)


def unpack(place, mine, other, seats):
    outs = (
        (4, 2, 8 * OWN),
        (3, 3, 20, HID1),
        (3, 3, HID2, HID1),
        (3, 3, HID1, HID2),
        (3, 3, 4, HID1),
    )
    return pl.pallas_call(
        unpack_kernel,
        out_shape=tuple(jax.ShapeDtypeStruct(shape, F32) for shape in outs),
        in_specs=[in_smem(), *in_vmem(3)],
        out_specs=tuple([pl.BlockSpec(memory_space=pl.ANY)] * 5),
        scratch_shapes=[
            *(pltpu.VMEM(outs[k], F32) for k in (2, 3, 1, 4, 0)),
            pltpu.SemaphoreType.DMA((5,)),
        ],
        compiler_params=pltpu.CompilerParams(vmem_limit_bytes=16 * 2**20),
        name="unpack",
    )(place, mine, other, seats)


def all_to_all(value, axes):
    return lax.all_to_all(value, axes, split_axis=0, concat_axis=0, tiled=True)


def swap(value, axes, offset):
    count = lax.axis_size(axes)
    pairs = []
    for i in range(offset, count + offset, 2):
        here, there = i % count, (i + 1) % count
        pairs += [(here, there), (there, here)]
    return lax.ppermute(value, axes, sorted(set(pairs)))


def local(
    coarse,
    target,
    noise,
    land_mask,
    level_index,
    frozen_first,
    frozen_middle,
    frozen_last,
    diffuse_in,
    diffuse_down,
    diffuse_up,
    diffuse_out,
):
    scale = 1.0 / (target.shape[0] * math.sqrt(target.shape[1] * target.shape[2] * lax.axis_size(STRIPS)))
    place = jnp.stack([lax.axis_index("core"), lax.axis_index("z") % 2])
    place = place.astype(jnp.int32)
    packed = all_to_all(pack(target, noise, land_mask, level_index), LAT).reshape(ROWS, 16, OWN)
    fields = jnp.concatenate([packed[:, :8], coarse.transpose(1, 0, 2).astype(F32), packed[:, 12:]], axis=1)
    across = swap(fields, STRIPS, 1)
    pair = swap(fields, STRIPS, 0)
    grads, partner, tiles = step(
        scale,
        place,
        fields,
        pair,
        across,
        frozen_first.transpose(0, 1, 3, 2),
        pltpu.with_memory_space_constraint(frozen_middle.reshape(3, 3 * HID1, HID1), pltpu.HBM),
        frozen_last,
        diffuse_in.transpose(0, 1, 3, 2),
        diffuse_down.reshape(3, 3 * HID2, HID1),
        diffuse_up.reshape(9 * HID1, HID2),
        diffuse_out,
    )
    chips = lax.axis_size(CHIPS)
    rows = HALF_ROWS // chips
    lats = tiles.shape[0]
    half = grads.astype(F32) + swap(partner, "core", 0).astype(F32)
    blocks = jnp.broadcast_to(tiles[None], (chips // lats, *tiles.shape)).reshape(chips, CELL_ROWS, OWN)
    sent = jnp.concatenate([half.astype(BF).reshape(chips, rows, OWN), blocks], axis=1)
    parts = all_to_all(sent, CHIPS)
    total = parts[:, :rows].astype(F32).sum(0).astype(BF)
    seats = parts.reshape(chips // lats, lats, rows + CELL_ROWS, OWN)[:, :, rows:]
    seats = lax.dynamic_index_in_dim(seats, lax.axis_index(("y", "x_hi")), 0, False)
    with jax.named_scope("spread"):
        mine = all_to_all(jnp.broadcast_to(total[None], (chips, rows, OWN)), CHIPS).reshape(HALF_ROWS, OWN)
    tile, first, down, up, last = unpack(place, mine, swap(mine, "core", 0), seats)
    return (tile, first.transpose(0, 1, 3, 2), down, up, last)


def solution(mesh):
    fine = Mesh(mesh.devices.reshape(4, 2, 2, 2, 4), LON + LAT)
    tile = P(None, LAT, LON)
    return jax.shard_map(
        local,
        mesh=fine,
        in_specs=(
            P(None, None, STRIPS),
            tile,
            tile,
            P(LAT, LON),
            P(LAT, LON),
            *([P()] * 7),
        ),
        out_specs=(tile, P(), P(), P(), P()),
        check_vma=False,
    )
```

```python
import math

import jax
import jax.numpy as jnp
from jax import lax
from jax.experimental import pallas as pl
from jax.experimental.pallas import tpu as pltpu
from jax.sharding import Mesh
from jax.sharding import PartitionSpec as P

LEVELS = 32
ROWS = 16
LOW = ROWS // 2
OWN = 128
HALO = 16
WIDE = OWN + 2 * HALO
WLOW = WIDE // 2
LANES = 256
HID1 = 128
HID2 = 256
BF = jnp.bfloat16
F32 = jnp.float32

LON = ("y", "x_hi", "core")
LAT = ("x_lo", "z")
CHIPS = ("y", "x_hi", "x_lo", "z")
STRIPS = LON + LAT

FIELDS = 24
UP_ROWS = 9 * HID1
DOWN_ROWS = 9 * HID2
BIG_ROWS = 2304
LAST_ROWS = 72
IN_ROWS = 9 * FIELDS
HALF_ROWS = 2560
CELL_ROWS = 8
CHUNK = {
    "gather": 8,
    "first": (8, 1),
    "second": (2, 2),
    "taps": 8,
    "enter": 8,
    "one": (8, 1),
    "two": (4, 2),
    "up": (8, 1),
    "three": 2,
    "loss": 4,
    "last": 8,
    "back_three": (8, 1),
    "blocks": 4,
    "back_two": (2, 4),
    "back_one": 4,
}


def mm(x, w):
    return lax.dot_general(x, w, (((1,), (0,)), ((), ())), preferred_element_type=F32)


def mm_nt(x, w):
    return lax.dot_general(x, w, (((1,), (1,)), ((), ())), preferred_element_type=F32)


def mm_tn(x, w):
    return lax.dot_general(x, w, (((0,), (0,)), ((), ())), preferred_element_type=F32)


def back(x, axis):
    return pltpu.roll(x, x.shape[axis] - 1, axis)


def ahead(x, axis):
    return pltpu.roll(x, 1, axis)


def with_halo(own, left, right):
    lane = lax.broadcasted_iota(jnp.int32, own.shape, 1)
    halo = jnp.where(lane < HALO, right, jnp.where(lane >= OWN - HALO, left, 0.0))
    return jnp.concatenate([own, halo], axis=1)


def to_cells(stack):
    pad = OWN - stack.shape[0]
    if pad:
        stack = jnp.concatenate([stack, jnp.zeros((pad, LANES), F32)], axis=0)
    cells = stack.T
    return jnp.concatenate([cells[: OWN + HALO], cells[LANES - HALO :]], axis=0).astype(BF)


def to_lanes(cells):
    gap = jnp.zeros((LANES - WIDE, cells.shape[1]), cells.dtype)
    return jnp.concatenate([cells[: OWN + HALO], gap, cells[OWN + HALO :]], axis=0)


def lon_shifts(field):
    return jnp.concatenate([ahead(field, 1), field, back(field, 1)], axis=0)


def three_rows(ref, start, count):
    width = ref.shape[1]
    return jnp.concatenate(
        [ref[pl.ds(start + a, count)].reshape(count * width, ref.shape[2]) for a in range(3)], axis=1
    )


def lon_sum(taps, count, width, out):
    first, second, third = (
        taps[:, b * out : (b + 1) * out].reshape(count, width, out) for b in range(3)
    )
    return ahead(first, 1) + second + back(third, 1)


def four_channels(ref, row):
    sums = []
    for b in range(3):
        at = [(a * 3 + b) * 8 for a in range(3)]
        sums.append(
            ref[row, at[0] : at[0] + 8]
            + ref[row + 1, at[1] : at[1] + 8]
            + ref[row + 2, at[2] : at[2] + 8]
        )
    return ahead(sums[0], 1) + sums[1] + back(sums[2], 1)


def zero_edges(ref):
    edge = jnp.zeros(ref.shape[1:], ref.dtype)
    ref[0] = edge
    ref[ref.shape[0] - 1] = edge


def each(count, body, unroll=1):
    def step(i, carry):
        body(i)
        return carry

    lax.fori_loop(0, count, step, 0, unroll=unroll)


def pack_kernel(level, target_far, noise_far, mask_far, packed, target, noise, land_mask, sems):
    arrive = [
        pltpu.make_async_copy(target_far, target, sems.at[0]),
        pltpu.make_async_copy(noise_far, noise, sems.at[1]),
        pltpu.make_async_copy(mask_far, land_mask, sems.at[2]),
    ]
    for copy in arrive:
        copy.start()
    power = jnp.full((1, OWN), level[0, 0], jnp.int32).astype(F32) / (LEVELS - 1)
    sigma = 0.02 * jnp.exp(power * math.log(4000.0))
    for copy in arrive:
        copy.wait()
    weight = 1.0 + land_mask[...].astype(F32)
    for p in range(packed.shape[0]):
        lanes = slice(p * OWN, (p + 1) * OWN)
        for r in range(2):
            packed[p, r, 0:1] = weight[r : r + 1, lanes]
            packed[p, r, 1:2] = sigma
            packed[p, r, 2:4] = jnp.zeros((2, OWN), F32)
            packed[p, r, 4:8] = target[:, r, lanes]
            packed[p, r, 8:12] = jnp.zeros((4, OWN), F32)
            packed[p, r, 12:16] = noise[:, r, lanes]


def stack_inputs(ref, weight, room):
    ref[...] = jnp.zeros_like(ref)
    count = weight.shape[2]
    for a in range(3):
        for b in range(3):
            ref[a, b * room : b * room + count] = weight[a, b].astype(F32)
    return ref[...].astype(BF).reshape(3 * OWN, OWN)


def stack_outputs(ref, weight):
    ref[...] = jnp.zeros_like(ref)
    for a in range(3):
        for b in range(3):
            at = (a * 3 + b) * 8 + 4
            ref[at : at + 4] = weight[a, b].astype(F32)
    return ref[...].astype(BF)


def regression_kernel(
    place,
    own,
    pair,
    across,
    w_first,
    w_middle,
    w_last,
    mean,
    coarse,
    stack,
    stack_o,
    net,
    hid,
    sec,
    taps,
    w_near,
    pair_w,
    sem,
):
    zero_edges(net)
    zero_edges(taps)
    hid[0, 0] = jnp.zeros((WIDE, HID1), BF)
    hid[LOW, 1] = jnp.zeros((WIDE, HID1), BF)
    even = place[1] == 0
    fetch = pltpu.make_async_copy(w_middle, w_near, sem)
    fetch.start()
    first_w = stack_inputs(stack, w_first, 16)

    def gather(r):
        near, far = pair[r], across[r]
        wide = with_halo(own[r], jnp.where(even, far, near), jnp.where(even, near, far))
        coarse[r] = wide
        net[r + 1] = to_cells(lon_shifts(wide))

    each(ROWS, gather, CHUNK["gather"])

    n1, u1 = CHUNK["first"]

    def first(i):
        pre = mm(three_rows(net, n1 * i, n1), first_w)
        act = jax.nn.silu(pre).astype(BF).reshape(n1 // 2, 2, WIDE, HID1)
        hid[pl.ds((n1 // 2) * i, n1 // 2), 1] = act[:, 0]
        hid[pl.ds((n1 // 2) * i + 1, n1 // 2), 0] = act[:, 1]

    each(ROWS // n1, first, u1)
    fetch.wait()
    gap = jnp.zeros((HID1, HID1), BF)
    for b in range(3):
        taps_b = [w_near[a, b * HID1 : (b + 1) * HID1] for a in range(3)]
        pair_w[b, 0:HID1] = jnp.concatenate([*taps_b, gap], axis=1)
        pair_w[b, HID1:] = jnp.concatenate([gap, *taps_b], axis=1)
    n2, u2 = CHUNK["second"]

    def second(i):
        rows = [hid[pl.ds(n2 * i + j // 2, n2), j % 2].reshape(n2 * WIDE, HID1) for j in range(4)]
        quads = jnp.concatenate(rows, axis=1)
        parts = [mm_nt(quads, pair_w[b]).reshape(n2, WIDE, 2 * HID1) for b in range(3)]
        act = jax.nn.silu(ahead(parts[0], 1) + parts[1] + back(parts[2], 1)).astype(BF)
        for k in range(n2):
            row = 2 * (n2 * i + k)
            sec[row] = act[k, :, :HID1]
            sec[row + 1] = act[k, :, HID1:]

    each(LOW // n2, second, u2)
    last_w = stack_outputs(stack_o, w_last)[0:72]

    def mean_taps(r):
        taps[r + 1] = mm_nt(last_w, to_lanes(sec[r]))

    each(ROWS, mean_taps, CHUNK["taps"])
    def collect(r):
        mean[r] = four_channels(taps, r).astype(BF).astype(F32)

    each(ROWS, collect, CHUNK["taps"])


def step_kernel(
    scale,
    place,
    own,
    pair,
    across,
    mean,
    coarse,
    w_in,
    w_down,
    w_up,
    w_out,
    mine,
    other,
    tiles,
    *scratch,
):
    (
        stack,
        stack_o,
        field,
        net,
        act_c,
        taps,
        residuals,
        noisies,
        slope_a,
        act_a,
        pairs,
        pooled,
        act_b,
        slope_b,
        up_taps,
        phases,
        slope_c,
        grad_f,
        spread_f,
        back_c,
        grad_c,
        blocks,
        grad_b,
        grad_a,
        last_sum,
        den,
        halves,
        low_taps,
        sems,
    ) = scratch
    for ref in (net, pooled, up_taps, taps, grad_f, grad_c, grad_b, low_taps):
        zero_edges(ref)
    even = place[1] == 0
    in_w = stack_inputs(stack, w_in, FIELDS)
    lane = lax.broadcasted_iota(jnp.int32, (8, LANES), 1)
    held = (lane < OWN + HALO) | (lane >= LANES - HALO)
    low_half = lax.broadcasted_iota(jnp.int32, (8, LANES), 0) < 4

    def enter(r):
        near, far = pair[r], across[r]
        wide = with_halo(own[r], jnp.where(even, far, near), jnp.where(even, near, far))
        field[r] = wide[0:8]
        mean_r = mean[r]
        sigma = jnp.where(held, jnp.broadcast_to(wide[1:2], (8, LANES)), 1.0)
        residual = wide[0:8] - mean_r
        noisy = residual + sigma * wide[8:16]
        variance = sigma * sigma + 0.25
        residuals[r] = residual
        noisies[r] = noisy
        scaled = (lax.rsqrt(variance) * noisy).astype(BF).astype(F32)
        both = jnp.where(low_half, pltpu.roll(mean_r, 4, 0), scaled)
        net[r + 1] = to_cells(lon_shifts(jnp.concatenate([both, coarse[r]], axis=0)))

    each(ROWS, enter, CHUNK["enter"])

    n3, u3 = CHUNK["one"]

    def level_one(i):
        pre = mm(three_rows(net, n3 * i, n3), in_w)
        gate = jax.nn.sigmoid(pre)
        slope_a[pl.ds(n3 * i, n3)] = (gate * (1.0 + pre * (1.0 - gate))).reshape(n3, WIDE, HID1)
        act = (pre * gate).astype(BF).reshape(n3, WIDE, HID1)
        act_a[pl.ds(n3 * i, n3)] = act
        wide = act.astype(F32)
        for k in range(n3 // 2):
            row = (n3 // 2) * i + k
            pairs[row] = wide[2 * k] + wide[2 * k + 1]
            total = pairs[row, pl.ds(0, WLOW, stride=2)] + pairs[row, pl.ds(1, WLOW, stride=2)]
            pooled[row + 1] = (0.25 * total).astype(BF)

    each(ROWS // n3, level_one, u3)
    down_w = jnp.concatenate([w_down[a] for a in range(3)], axis=1)

    n4, u4 = CHUNK["two"]

    def level_two(i):
        pre = lon_sum(mm_nt(three_rows(pooled, n4 * i, n4), down_w), n4, WLOW, HID2)
        gate = jax.nn.sigmoid(pre)
        slope_b[pl.ds(n4 * i, n4)] = gate * (1.0 + pre * (1.0 - gate))
        act_b[pl.ds(n4 * i, n4)] = (pre * gate).astype(BF)

    each(LOW // n4, level_two, u4)
    n5, u5 = CHUNK["up"]

    def up_products(i):
        low = act_b[pl.ds(n5 * i, n5)].reshape(n5 * WLOW, HID2)
        up_taps[pl.ds(n5 * i + 1, n5)] = mm_nt(low, w_up[...]).reshape(n5, WLOW, 9 * HID1)

    each(LOW // n5, up_products, u5)

    def level_three(i):
        for pi in range(2):
            sums = []
            for b in range(3):
                total = None
                for a in range(3):
                    row = i + 1 + (pi + a - 1) // 2
                    at = (a * 3 + b) * HID1
                    part = up_taps[row, :, at : at + HID1]
                    total = part if total is None else total + part
                sums.append(total)
            row = 2 * i + pi
            phases[row, pl.ds(0, WLOW, stride=2)] = ahead(sums[0], 0) + sums[1] + sums[2]
            phases[row, pl.ds(1, WLOW, stride=2)] = sums[0] + sums[1] + back(sums[2], 0)
            pre = phases[row]
            gate = jax.nn.sigmoid(pre)
            act_c[row] = (pre * gate + act_a[row].astype(F32)).astype(BF)
            slope_c[row] = gate * (1.0 + pre * (1.0 - gate))

    each(LOW, level_three, CHUNK["three"])
    out_w = stack_outputs(stack_o, w_out)

    def field_taps(r):
        taps[r + 1] = mm_nt(out_w[0:72], to_lanes(act_c[r]))

    each(ROWS, field_taps, CHUNK["taps"])

    def loss(i):
        for k in range(2):
            r = 2 * i + k
            value = four_channels(taps, r)
            sigma = jnp.where(held, jnp.broadcast_to(field[r, 1:2], (8, LANES)), 1.0)
            weight = jnp.broadcast_to(field[r, 0:1], (8, LANES))
            variance = sigma * sigma + 0.25
            c_out = 0.5 * sigma * lax.rsqrt(variance)
            lam = variance / (0.25 * sigma * sigma)
            denoised = (0.25 / variance) * noisies[r] + c_out * value
            den[i, 4 * k : 4 * k + 4] = denoised[4:8, :OWN]
            loss_grad = (2.0 * scale) * weight * lam * (denoised - residuals[r])
            cot = (c_out * loss_grad).astype(BF).astype(F32)
            grad_f[r + 1] = jnp.where(low_half, 0.0, cot)

    each(LOW, loss, CHUNK["loss"])
    tiles[...] = den[...].astype(BF)
    last_sum[...] = jnp.zeros_like(last_sum)

    def last_grads(r):
        parts = []
        for a in range(3):
            cot = grad_f[r + 2 - a]
            parts += [back(cot, 1), cot, ahead(cot, 1)]
        cots = jnp.concatenate(parts + [jnp.zeros((8, LANES), F32)], axis=0)
        last_sum[...] += mm(cots[:, :OWN].astype(BF), act_c[r, 0:OWN])
        spread_f[r] = to_cells(cots)

    each(ROWS, last_grads, CHUNK["last"])
    near, far = 0, 1

    def keep(half, at, value):
        halves[half, at : at + value.shape[0]] = value.astype(BF)

    def send(half):
        for core, target in ((half, mine), (1 - half, other)):

            @pl.when(place[0] == core)
            def _():
                pltpu.make_async_copy(halves.at[half], target, sems.at[half]).start()

    keep(near, BIG_ROWS, last_sum[0:LAST_ROWS])
    keep(near, BIG_ROWS + LAST_ROWS, jnp.zeros((HALF_ROWS - BIG_ROWS - LAST_ROWS, OWN), F32))

    n6, u6 = CHUNK["back_three"]

    def back_three(i):
        wide = mm(spread_f[pl.ds(n6 * i, n6)].reshape(n6 * WIDE, OWN), out_w)
        wide = wide.reshape(n6, WIDE, HID1)
        back_c[pl.ds(n6 * i, n6)] = wide
        grad_c[pl.ds(n6 * i + 1, n6)] = wide * slope_c[pl.ds(n6 * i, n6)]

    each(ROWS // n6, back_three, u6)

    def block_sums(i):
        even = [grad_c[2 * i + k, pl.ds(0, WLOW, stride=2)] for k in range(4)]
        odd = [grad_c[2 * i + k, pl.ds(1, WLOW, stride=2)] for k in range(4)]
        for a in range(3):
            e, o = even[2 - a] + even[3 - a], odd[2 - a] + odd[3 - a]
            for b, total in enumerate((o + back(e, 0), e + o, ahead(o, 0) + e)):
                at = (a * 3 + b) * HID1
                blocks[i, :, at : at + HID1] = total.astype(BF)

    each(LOW, block_sums, CHUNK["blocks"])

    n7, u7 = CHUNK["back_two"]

    def back_two(i):
        low = mm(blocks[pl.ds(n7 * i, n7)].reshape(n7 * WLOW, 9 * HID1), w_up[...])
        cot = low.reshape(n7, WLOW, HID2) * slope_b[pl.ds(n7 * i, n7)]
        shifts = jnp.concatenate([back(cot, 1), cot, ahead(cot, 1)], axis=2)
        grad_b[pl.ds(n7 * i + 1, n7)] = shifts.astype(BF)

    each(LOW // n7, back_two, u7)
    held_low = OWN // 2
    cells = LOW * held_low
    low_b = act_b[:, :held_low].reshape(cells, HID2)
    for k in range(3):
        at = 3 * HID1 * k
        up = mm_tn(blocks[:, :held_low, at : at + 3 * HID1].reshape(cells, 3 * HID1), low_b)
        keep(near, at, up[:, :HID1])
        keep(near, at + UP_ROWS, up[:, HID1:])
    send(near)
    low_a = jnp.concatenate(
        [pooled[a : a + LOW, :held_low].reshape(cells, HID1) for a in range(3)], axis=1
    )
    for b in range(3):
        at = HID2 * b
        down = mm_tn(grad_b[1 : LOW + 1, :held_low, at : at + HID2].reshape(cells, HID2), low_a)
        for a in range(3):
            keep(far, (a * 3 + b) * HID2, down[:, HID1 * a : HID1 * (a + 1)])
    spread_w = jnp.concatenate([w_down[a] for a in range(3)], axis=1)
    wide = mm(grad_b[1 : LOW + 1, :held_low].reshape(cells, 3 * HID2), spread_w)
    low_taps[1 : LOW + 1] = wide.reshape(LOW, held_low, 3 * HID1)

    def back_one(i):
        low = (
            low_taps[i + 2, :, 0:HID1]
            + low_taps[i + 1, :, HID1 : 2 * HID1]
            + low_taps[i, :, 2 * HID1 :]
        )
        low = 0.25 * low
        phases[i, pl.ds(0, held_low, stride=2)] = low
        phases[i, pl.ds(1, held_low, stride=2)] = low
        spread = phases[i, 0:OWN]
        for pi in range(2):
            r = 2 * i + pi
            grad_a[r] = ((back_c[r, 0:OWN] + spread) * slope_a[r, 0:OWN]).astype(BF)

    each(LOW, back_one, CHUNK["back_one"])
    near_cells = jnp.concatenate(
        [net[a : a + ROWS, :OWN].reshape(ROWS * OWN, OWN) for a in range(3)], axis=1
    )
    inputs = mm_tn(grad_a[...].reshape(ROWS * OWN, HID1), near_cells)
    for a in range(3):
        part = inputs[:, a * OWN : (a + 1) * OWN].T
        keep(far, BIG_ROWS + a * 3 * FIELDS, part[: 3 * FIELDS])
    keep(far, BIG_ROWS + IN_ROWS, jnp.zeros((HALF_ROWS - BIG_ROWS - IN_ROWS, OWN), F32))
    send(far)
    for half in (near, far):
        pltpu.make_async_copy(halves.at[half], mine, sems.at[half]).wait()


def unpack_kernel(place, mine, other, seats, tile, first, down, up, last, downs, ups, firsts, lasts, tiles, sems):
    even = place[0] == 0

    def half(k, at, count):
        one, two = mine[pl.ds(at, count)], other[pl.ds(at, count)]
        return (jnp.where(even, one, two) if k == 0 else jnp.where(even, two, one)).astype(F32)

    def leave(a):
        return (
            pltpu.make_async_copy(ups.at[a], up.at[a], sems.at[0]),
            pltpu.make_async_copy(downs.at[a], down.at[a], sems.at[1]),
        )

    def thirds(a):
        at = pl.multiple_of(a * (3 * HID1), 3 * HID1)
        for k in range(2):
            piece = half(0, at + k * UP_ROWS, 3 * HID1)
            ups[a, :, :, k * HID1 : (k + 1) * HID1] = piece.reshape(3, HID1, HID1)
        downs[a] = half(1, 2 * at, 3 * HID2).reshape(3, HID2, HID1)
        for copy in leave(a):
            copy.start()

    each(3, thirds)
    inputs = half(1, BIG_ROWS, IN_ROWS)
    outputs = half(0, BIG_ROWS, 80)
    for a in range(3):
        for b in range(3):
            at = (a * 3 + b) * FIELDS
            firsts[a, b] = inputs[at : at + 20]
            at = (a * 3 + b) * 8 + 4
            lasts[a, b] = outputs[at : at + 4]
    small = [pltpu.make_async_copy(firsts, first, sems.at[2]), pltpu.make_async_copy(lasts, last, sems.at[3])]
    for copy in small:
        copy.start()
    blocks = seats[...].astype(F32)
    for k in range(8):
        for r in range(2):
            tiles[:, r, k * OWN : (k + 1) * OWN] = blocks[k, 4 * r : 4 * r + 4]
    small.append(pltpu.make_async_copy(tiles, tile, sems.at[4]))
    small[2].start()
    for copy in small:
        copy.wait()
    for a in range(3):
        for copy in leave(a):
            copy.wait()


def in_vmem(count):
    return [pl.BlockSpec(memory_space=pltpu.MemorySpace.VMEM) for _ in range(count)]


def in_hbm(count):
    return [pl.BlockSpec(memory_space=pltpu.MemorySpace.HBM) for _ in range(count)]


def in_smem():
    return pl.BlockSpec(memory_space=pltpu.MemorySpace.SMEM)


def pack(target, noise, land_mask, level_index):
    lats = target.shape[2] // OWN
    return pl.pallas_call(
        pack_kernel,
        out_shape=jax.ShapeDtypeStruct((lats, 2, 16, OWN), F32),
        in_specs=[in_smem(), *in_hbm(3)],
        out_specs=in_vmem(1)[0],
        scratch_shapes=[
            pltpu.VMEM(target.shape, F32),
            pltpu.VMEM(noise.shape, F32),
            pltpu.VMEM(land_mask.shape, jnp.int32),
            pltpu.SemaphoreType.DMA((3,)),
        ],
        name="pack",
    )(level_index, target, noise, land_mask)


def regress(*operands):
    return pl.pallas_call(
        regression_kernel,
        out_shape=(
            jax.ShapeDtypeStruct((ROWS, 8, LANES), F32),
            jax.ShapeDtypeStruct((ROWS, 16, LANES), F32),
        ),
        in_specs=[in_smem(), *in_vmem(4), *in_hbm(1), *in_vmem(1)],
        out_specs=tuple(in_vmem(2)),
        scratch_shapes=[
            pltpu.VMEM((3, OWN, OWN), F32),
            pltpu.VMEM((OWN, OWN), F32),
            pltpu.VMEM((ROWS + 2, WIDE, OWN), BF),
            pltpu.VMEM((LOW + 1, 2, WIDE, HID1), BF),
            pltpu.VMEM((ROWS, WIDE, HID1), BF),
            pltpu.VMEM((ROWS + 2, 72, LANES), F32),
            pltpu.VMEM((3, 3 * HID1, HID1), BF),
            pltpu.VMEM((3, 2 * HID1, 4 * HID1), BF),
            pltpu.SemaphoreType.DMA(()),
        ],
        compiler_params=pltpu.CompilerParams(vmem_limit_bytes=20 * 2**20),
        cost_estimate=pl.CostEstimate(flops=2 * 10**9, transcendentals=10**6, bytes_accessed=2 * 10**6),
        name="regress",
    )(*operands)


def step(scale, *operands):
    def kernel(*refs):
        step_kernel(scale, *refs)

    return pl.pallas_call(
        kernel,
        out_shape=(
            jax.ShapeDtypeStruct((HALF_ROWS, OWN), BF),
            jax.ShapeDtypeStruct((HALF_ROWS, OWN), BF),
            jax.ShapeDtypeStruct((LOW, CELL_ROWS, OWN), BF),
        ),
        in_specs=[in_smem(), *in_vmem(9)],
        out_specs=tuple(in_vmem(3)),
        scratch_shapes=[
            pltpu.VMEM((3, OWN, OWN), F32),
            pltpu.VMEM((OWN, OWN), F32),
            pltpu.VMEM((ROWS, 8, LANES), F32),
            pltpu.VMEM((ROWS + 2, WIDE, OWN), BF),
            pltpu.VMEM((ROWS, WIDE, HID1), BF),
            pltpu.VMEM((ROWS + 2, 72, LANES), F32),
            pltpu.VMEM((ROWS, 8, LANES), F32),
            pltpu.VMEM((ROWS, 8, LANES), F32),
            pltpu.VMEM((ROWS, WIDE, HID1), F32),
            pltpu.VMEM((ROWS, WIDE, HID1), BF),
            pltpu.VMEM((LOW, WIDE, HID1), F32),
            pltpu.VMEM((LOW + 2, WLOW, HID1), BF),
            pltpu.VMEM((LOW, WLOW, HID2), BF),
            pltpu.VMEM((LOW, WLOW, HID2), F32),
            pltpu.VMEM((LOW + 2, WLOW, 9 * HID1), F32),
            pltpu.VMEM((ROWS, WIDE, HID1), F32),
            pltpu.VMEM((ROWS, WIDE, HID1), F32),
            pltpu.VMEM((ROWS + 2, 8, LANES), F32),
            pltpu.VMEM((ROWS, WIDE, OWN), BF),
            pltpu.VMEM((ROWS, WIDE, HID1), F32),
            pltpu.VMEM((ROWS + 2, WIDE, HID1), F32),
            pltpu.VMEM((LOW, WLOW, 9 * HID1), BF),
            pltpu.VMEM((LOW + 2, WLOW, 3 * HID2), BF),
            pltpu.VMEM((ROWS, OWN, HID1), BF),
            pltpu.VMEM((80, HID1), F32),
            pltpu.VMEM((LOW, CELL_ROWS, OWN), F32),
            pltpu.VMEM((2, HALF_ROWS, OWN), BF),
            pltpu.VMEM((LOW + 2, OWN // 2, 3 * HID1), F32),
            pltpu.SemaphoreType.DMA((2,)),
        ],
        compiler_params=pltpu.CompilerParams(vmem_limit_bytes=44 * 2**20),
        name="step",
    )(*operands)


def unpack(place, mine, other, seats):
    outs = (
        (4, 2, 8 * OWN),
        (3, 3, 20, HID1),
        (3, 3, HID2, HID1),
        (3, 3, HID1, HID2),
        (3, 3, 4, HID1),
    )
    return pl.pallas_call(
        unpack_kernel,
        out_shape=tuple(jax.ShapeDtypeStruct(shape, F32) for shape in outs),
        in_specs=[in_smem(), *in_vmem(3)],
        out_specs=tuple([pl.BlockSpec(memory_space=pl.ANY)] * 5),
        scratch_shapes=[
            *(pltpu.VMEM(outs[k], F32) for k in (2, 3, 1, 4, 0)),
            pltpu.SemaphoreType.DMA((5,)),
        ],
        compiler_params=pltpu.CompilerParams(vmem_limit_bytes=16 * 2**20),
        name="unpack",
    )(place, mine, other, seats)


def all_to_all(value, axes):
    return lax.all_to_all(value, axes, split_axis=0, concat_axis=0, tiled=True)


def in_place(value):
    return pltpu.with_memory_space_constraint(value, pltpu.HBM)


def swap(value, axes, offset):
    count = lax.axis_size(axes)
    pairs = []
    for i in range(offset, count + offset, 2):
        here, there = i % count, (i + 1) % count
        pairs += [(here, there), (there, here)]
    return lax.ppermute(value, axes, sorted(set(pairs)))


def local(
    coarse,
    target,
    noise,
    land_mask,
    level_index,
    frozen_first,
    frozen_middle,
    frozen_last,
    diffuse_in,
    diffuse_down,
    diffuse_up,
    diffuse_out,
):
    scale = 1.0 / (target.shape[0] * math.sqrt(target.shape[1] * target.shape[2] * lax.axis_size(STRIPS)))
    place = jnp.stack([lax.axis_index("core"), lax.axis_index("z") % 2])
    place = place.astype(jnp.int32)
    packed = all_to_all(pack(target, noise, land_mask, level_index), LAT).reshape(ROWS, 16, OWN)
    strip = jnp.pad(coarse.transpose(1, 0, 2).astype(F32), ((0, 0), (0, 4), (0, 0)))
    strip_across = swap(strip, STRIPS, 1)
    strip_pair = swap(strip, STRIPS, 0)
    across = swap(packed, STRIPS, 1)
    pair = swap(packed, STRIPS, 0)
    mean, coarse_wide = regress(
        place,
        strip,
        strip_pair,
        strip_across,
        in_place(frozen_first.transpose(0, 1, 3, 2)),
        in_place(frozen_middle.reshape(3, 3 * HID1, HID1)),
        in_place(frozen_last),
    )
    grads, partner, tiles = step(
        scale,
        place,
        packed,
        pair,
        across,
        mean,
        coarse_wide,
        diffuse_in.transpose(0, 1, 3, 2),
        diffuse_down.reshape(3, 3 * HID2, HID1),
        diffuse_up.reshape(9 * HID1, HID2),
        diffuse_out,
    )
    chips = lax.axis_size(CHIPS)
    rows = HALF_ROWS // chips
    lats = tiles.shape[0]
    half = grads.astype(F32) + swap(partner, "core", 0).astype(F32)
    blocks = jnp.broadcast_to(tiles[None], (chips // lats, *tiles.shape)).reshape(chips, CELL_ROWS, OWN)
    sent = jnp.concatenate([half.astype(BF).reshape(chips, rows, OWN), blocks], axis=1)
    parts = all_to_all(sent, CHIPS)
    total = parts[:, :rows].astype(F32).sum(0).astype(BF)
    seats = parts.reshape(chips // lats, lats, rows + CELL_ROWS, OWN)[:, :, rows:]
    seats = lax.dynamic_index_in_dim(seats, lax.axis_index(("y", "x_hi")), 0, False)
    with jax.named_scope("spread"):
        mine = all_to_all(jnp.broadcast_to(total[None], (chips, rows, OWN)), CHIPS).reshape(HALF_ROWS, OWN)
    tile, first, down, up, last = unpack(place, mine, swap(mine, "core", 0), seats)
    return (tile, first.transpose(0, 1, 3, 2), down, up, last)


def solution(mesh):
    fine = Mesh(mesh.devices.reshape(4, 2, 2, 2, 4), LON + LAT)
    tile = P(None, LAT, LON)
    return jax.shard_map(
        local,
        mesh=fine,
        in_specs=(
            P(None, None, STRIPS),
            tile,
            tile,
            P(LAT, LON),
            P(LAT, LON),
            *([P()] * 7),
        ),
        out_specs=(tile, P(), P(), P(), P()),
        check_vma=False,
    )
```

```python
import math

import jax
import jax.numpy as jnp
from jax import lax
from jax.experimental import pallas as pl
from jax.experimental.pallas import tpu as pltpu
from jax.sharding import Mesh
from jax.sharding import PartitionSpec as P


LEVELS = 32
ROWS = 16
LOW = ROWS // 2
OWN = 128
HALO = 16
WIDE = OWN + 2 * HALO
WLOW = WIDE // 2
LANES = 256
HID1 = 128
HID2 = 256
BF = jnp.bfloat16
F32 = jnp.float32

LON = ("y", "x_hi", "core")
LAT = ("x_lo", "z")
CHIPS = ("y", "x_hi", "x_lo", "z")
STRIPS = LON + LAT

FIELDS = 24
UP_ROWS = 9 * HID1
BIG_ROWS = 2304
LAST_ROWS = 72
IN_ROWS = 9 * FIELDS
HALF_ROWS = 2560
CELL_ROWS = 8
CHUNK = {
    "gather": 8,
    "first": (8, 1),
    "second": (2, 2),
    "taps": 8,
    "enter": 8,
    "one": (8, 1),
    "two": (4, 2),
    "up": (8, 1),
    "three": 2,
    "loss": 4,
    "last": 8,
    "back_three": (8, 1),
    "blocks": 4,
    "back_two": (2, 4),
    "back_one": 4,
}


def mm(x, w):
    return lax.dot_general(x, w, (((1,), (0,)), ((), ())), preferred_element_type=F32)


def mm_nt(x, w):
    return lax.dot_general(x, w, (((1,), (1,)), ((), ())), preferred_element_type=F32)


def mm_tn(x, w):
    return lax.dot_general(x, w, (((0,), (0,)), ((), ())), preferred_element_type=F32)


def back(x, axis):
    return pltpu.roll(x, x.shape[axis] - 1, axis)


def ahead(x, axis):
    return pltpu.roll(x, 1, axis)


def with_halo(own, left, right):
    lane = lax.broadcasted_iota(jnp.int32, own.shape, 1)
    halo = jnp.where(lane < HALO, right, jnp.where(lane >= OWN - HALO, left, 0.0))
    return jnp.concatenate([own, halo], axis=1)


def to_cells(stack):
    pad = OWN - stack.shape[0]
    if pad:
        stack = jnp.concatenate([stack, jnp.zeros((pad, LANES), F32)], axis=0)
    cells = stack.T
    return jnp.concatenate([cells[: OWN + HALO], cells[LANES - HALO :]], axis=0).astype(BF)


def to_lanes(cells):
    gap = jnp.zeros((LANES - WIDE, cells.shape[1]), cells.dtype)
    return jnp.concatenate([cells[: OWN + HALO], gap, cells[OWN + HALO :]], axis=0)


def lon_shifts(field):
    return jnp.concatenate([ahead(field, 1), field, back(field, 1)], axis=0)


def three_rows(ref, start, count):
    width = ref.shape[1]
    return jnp.concatenate(
        [ref[pl.ds(start + a, count)].reshape(count * width, ref.shape[2]) for a in range(3)], axis=1
    )


def lon_sum(taps, count, width, out):
    first, second, third = (
        taps[:, b * out : (b + 1) * out].reshape(count, width, out) for b in range(3)
    )
    return ahead(first, 1) + second + back(third, 1)


def four_channels(ref, row):
    sums = []
    for b in range(3):
        at = [(a * 3 + b) * 8 for a in range(3)]
        sums.append(
            ref[row, at[0] : at[0] + 8]
            + ref[row + 1, at[1] : at[1] + 8]
            + ref[row + 2, at[2] : at[2] + 8]
        )
    return ahead(sums[0], 1) + sums[1] + back(sums[2], 1)


def zero_edges(ref):
    edge = jnp.zeros(ref.shape[1:], ref.dtype)
    ref[0] = edge
    ref[ref.shape[0] - 1] = edge


def each(count, body, unroll=1):
    def step(i, carry):
        body(i)
        return carry

    lax.fori_loop(0, count, step, 0, unroll=unroll)


def pack_kernel(level, target_far, noise_far, mask_far, packed, target, noise, land_mask, sems):
    arrive = [
        pltpu.make_async_copy(target_far, target, sems.at[0]),
        pltpu.make_async_copy(noise_far, noise, sems.at[1]),
        pltpu.make_async_copy(mask_far, land_mask, sems.at[2]),
    ]
    for copy in arrive:
        copy.start()
    power = jnp.full((1, OWN), level[0, 0], jnp.int32).astype(F32) / (LEVELS - 1)
    sigma = 0.02 * jnp.exp(power * math.log(4000.0))
    for copy in arrive:
        copy.wait()
    weight = 1.0 + land_mask[...].astype(F32)
    for p in range(packed.shape[0]):
        lanes = slice(p * OWN, (p + 1) * OWN)
        for r in range(2):
            packed[p, r, 0:1] = weight[r : r + 1, lanes]
            packed[p, r, 1:2] = sigma
            packed[p, r, 2:4] = jnp.zeros((2, OWN), F32)
            packed[p, r, 4:8] = target[:, r, lanes]
            packed[p, r, 8:12] = jnp.zeros((4, OWN), F32)
            packed[p, r, 12:16] = noise[:, r, lanes]


def stack_inputs(ref, weight, room):
    ref[...] = jnp.zeros_like(ref)
    count = weight.shape[2]
    for a in range(3):
        for b in range(3):
            ref[a, b * room : b * room + count] = weight[a, b].astype(F32)
    return ref[...].astype(BF).reshape(3 * OWN, OWN)


def stack_outputs(ref, weight):
    ref[...] = jnp.zeros_like(ref)
    for a in range(3):
        for b in range(3):
            at = (a * 3 + b) * 8 + 4
            ref[at : at + 4] = weight[a, b].astype(F32)
    return ref[...].astype(BF)


def regression_kernel(
    place,
    own,
    pair,
    across,
    w_first,
    w_middle,
    w_last,
    mean,
    coarse,
    stack,
    stack_o,
    net,
    hid,
    sec,
    taps,
    w_near,
    pair_w,
    sem,
):
    zero_edges(net)
    zero_edges(taps)
    hid[0, 0] = jnp.zeros((WIDE, HID1), BF)
    hid[LOW, 1] = jnp.zeros((WIDE, HID1), BF)
    even = place[1] == 0
    fetch = pltpu.make_async_copy(w_middle, w_near, sem)
    fetch.start()
    first_w = stack_inputs(stack, w_first, 16)

    def gather(r):
        near, far = pair[r], across[r]
        wide = with_halo(own[r], jnp.where(even, far, near), jnp.where(even, near, far))
        coarse[r] = wide
        net[r + 1] = to_cells(lon_shifts(wide))

    each(ROWS, gather, CHUNK["gather"])

    n1, u1 = CHUNK["first"]

    def first(i):
        pre = mm(three_rows(net, n1 * i, n1), first_w)
        act = jax.nn.silu(pre).astype(BF).reshape(n1 // 2, 2, WIDE, HID1)
        hid[pl.ds((n1 // 2) * i, n1 // 2), 1] = act[:, 0]
        hid[pl.ds((n1 // 2) * i + 1, n1 // 2), 0] = act[:, 1]

    each(ROWS // n1, first, u1)
    fetch.wait()
    gap = jnp.zeros((HID1, HID1), BF)
    for b in range(3):
        taps_b = [w_near[a, b * HID1 : (b + 1) * HID1] for a in range(3)]
        pair_w[b, 0:HID1] = jnp.concatenate([*taps_b, gap], axis=1)
        pair_w[b, HID1:] = jnp.concatenate([gap, *taps_b], axis=1)
    n2, u2 = CHUNK["second"]

    def second(i):
        rows = [hid[pl.ds(n2 * i + j // 2, n2), j % 2].reshape(n2 * WIDE, HID1) for j in range(4)]
        quads = jnp.concatenate(rows, axis=1)
        parts = [mm_nt(quads, pair_w[b]).reshape(n2, WIDE, 2 * HID1) for b in range(3)]
        act = jax.nn.silu(ahead(parts[0], 1) + parts[1] + back(parts[2], 1)).astype(BF)
        for k in range(n2):
            row = 2 * (n2 * i + k)
            sec[row] = act[k, :, :HID1]
            sec[row + 1] = act[k, :, HID1:]

    each(LOW // n2, second, u2)
    last_w = stack_outputs(stack_o, w_last)[0:72]

    def mean_taps(r):
        taps[r + 1] = mm_nt(last_w, to_lanes(sec[r]))

    each(ROWS, mean_taps, CHUNK["taps"])

    def collect(r):
        mean[r] = four_channels(taps, r).astype(BF).astype(F32)

    each(ROWS, collect, CHUNK["taps"])


def step_kernel(
    scale,
    place,
    own,
    pair,
    across,
    mean,
    coarse,
    w_in,
    w_down,
    w_up,
    w_out,
    mine,
    other,
    tiles,
    *scratch,
):
    (
        stack,
        stack_o,
        field,
        net,
        act_c,
        taps,
        residuals,
        noisies,
        slope_a,
        act_a,
        pairs,
        pooled,
        act_b,
        slope_b,
        up_taps,
        phases,
        slope_c,
        grad_f,
        spread_f,
        back_c,
        grad_c,
        blocks,
        grad_b,
        grad_a,
        last_sum,
        den,
        halves,
        low_taps,
        sems,
    ) = scratch
    for ref in (net, pooled, up_taps, taps, grad_f, grad_c, grad_b, low_taps):
        zero_edges(ref)
    even = place[1] == 0
    in_w = stack_inputs(stack, w_in, FIELDS)
    lane = lax.broadcasted_iota(jnp.int32, (8, LANES), 1)
    held = (lane < OWN + HALO) | (lane >= LANES - HALO)
    low_half = lax.broadcasted_iota(jnp.int32, (8, LANES), 0) < 4

    def enter(r):
        near, far = pair[r], across[r]
        wide = with_halo(own[r], jnp.where(even, far, near), jnp.where(even, near, far))
        field[r] = wide[0:8]
        mean_r = mean[r]
        sigma = jnp.where(held, jnp.broadcast_to(wide[1:2], (8, LANES)), 1.0)
        residual = wide[0:8] - mean_r
        noisy = residual + sigma * wide[8:16]
        variance = sigma * sigma + 0.25
        residuals[r] = residual
        noisies[r] = noisy
        scaled = (lax.rsqrt(variance) * noisy).astype(BF).astype(F32)
        both = jnp.where(low_half, pltpu.roll(mean_r, 4, 0), scaled)
        net[r + 1] = to_cells(lon_shifts(jnp.concatenate([both, coarse[r]], axis=0)))

    each(ROWS, enter, CHUNK["enter"])

    n3, u3 = CHUNK["one"]

    def level_one(i):
        pre = mm(three_rows(net, n3 * i, n3), in_w)
        gate = jax.nn.sigmoid(pre)
        slope_a[pl.ds(n3 * i, n3)] = (gate * (1.0 + pre * (1.0 - gate))).reshape(n3, WIDE, HID1)
        act = (pre * gate).astype(BF).reshape(n3, WIDE, HID1)
        act_a[pl.ds(n3 * i, n3)] = act
        wide = act.astype(F32)
        for k in range(n3 // 2):
            row = (n3 // 2) * i + k
            pairs[row] = wide[2 * k] + wide[2 * k + 1]
            total = pairs[row, pl.ds(0, WLOW, stride=2)] + pairs[row, pl.ds(1, WLOW, stride=2)]
            pooled[row + 1] = (0.25 * total).astype(BF)

    each(ROWS // n3, level_one, u3)
    down_w = jnp.concatenate([w_down[a] for a in range(3)], axis=1)

    n4, u4 = CHUNK["two"]

    def level_two(i):
        pre = lon_sum(mm_nt(three_rows(pooled, n4 * i, n4), down_w), n4, WLOW, HID2)
        gate = jax.nn.sigmoid(pre)
        slope_b[pl.ds(n4 * i, n4)] = gate * (1.0 + pre * (1.0 - gate))
        act_b[pl.ds(n4 * i, n4)] = (pre * gate).astype(BF)

    each(LOW // n4, level_two, u4)
    n5, u5 = CHUNK["up"]

    def up_products(i):
        low = act_b[pl.ds(n5 * i, n5)].reshape(n5 * WLOW, HID2)
        up_taps[pl.ds(n5 * i + 1, n5)] = mm_nt(low, w_up[...]).reshape(n5, WLOW, 9 * HID1)

    each(LOW // n5, up_products, u5)

    def level_three(i):
        for pi in range(2):
            sums = []
            for b in range(3):
                total = None
                for a in range(3):
                    row = i + 1 + (pi + a - 1) // 2
                    at = (a * 3 + b) * HID1
                    part = up_taps[row, :, at : at + HID1]
                    total = part if total is None else total + part
                sums.append(total)
            row = 2 * i + pi
            phases[row, pl.ds(0, WLOW, stride=2)] = ahead(sums[0], 0) + sums[1] + sums[2]
            phases[row, pl.ds(1, WLOW, stride=2)] = sums[0] + sums[1] + back(sums[2], 0)
            pre = phases[row]
            gate = jax.nn.sigmoid(pre)
            act_c[row] = (pre * gate + act_a[row].astype(F32)).astype(BF)
            slope_c[row] = gate * (1.0 + pre * (1.0 - gate))

    each(LOW, level_three, CHUNK["three"])
    out_w = stack_outputs(stack_o, w_out)

    def field_taps(r):
        taps[r + 1] = mm_nt(out_w[0:72], to_lanes(act_c[r]))

    each(ROWS, field_taps, CHUNK["taps"])

    def loss(i):
        for k in range(2):
            r = 2 * i + k
            value = four_channels(taps, r)
            sigma = jnp.where(held, jnp.broadcast_to(field[r, 1:2], (8, LANES)), 1.0)
            weight = jnp.broadcast_to(field[r, 0:1], (8, LANES))
            variance = sigma * sigma + 0.25
            c_out = 0.5 * sigma * lax.rsqrt(variance)
            lam = variance / (0.25 * sigma * sigma)
            denoised = (0.25 / variance) * noisies[r] + c_out * value
            den[i, 4 * k : 4 * k + 4] = denoised[4:8, :OWN]
            loss_grad = (2.0 * scale) * weight * lam * (denoised - residuals[r])
            cot = (c_out * loss_grad).astype(BF).astype(F32)
            grad_f[r + 1] = jnp.where(low_half, 0.0, cot)

    each(LOW, loss, CHUNK["loss"])
    tiles[...] = den[...].astype(BF)
    last_sum[...] = jnp.zeros_like(last_sum)

    def last_grads(r):
        parts = []
        for a in range(3):
            cot = grad_f[r + 2 - a]
            parts += [back(cot, 1), cot, ahead(cot, 1)]
        cots = jnp.concatenate(parts + [jnp.zeros((8, LANES), F32)], axis=0)
        last_sum[...] += mm(cots[:, :OWN].astype(BF), act_c[r, 0:OWN])
        spread_f[r] = to_cells(cots)

    each(ROWS, last_grads, CHUNK["last"])
    near, far = 0, 1

    def keep(half, at, value):
        halves[half, at : at + value.shape[0]] = value.astype(BF)

    def send(half):
        for core, target in ((half, mine), (1 - half, other)):

            @pl.when(place[0] == core)
            def _():
                pltpu.make_async_copy(halves.at[half], target, sems.at[half]).start()

    keep(near, BIG_ROWS, last_sum[0:LAST_ROWS])
    keep(near, BIG_ROWS + LAST_ROWS, jnp.zeros((HALF_ROWS - BIG_ROWS - LAST_ROWS, OWN), F32))

    n6, u6 = CHUNK["back_three"]

    def back_three(i):
        wide = mm(spread_f[pl.ds(n6 * i, n6)].reshape(n6 * WIDE, OWN), out_w)
        wide = wide.reshape(n6, WIDE, HID1)
        back_c[pl.ds(n6 * i, n6)] = wide
        grad_c[pl.ds(n6 * i + 1, n6)] = wide * slope_c[pl.ds(n6 * i, n6)]

    each(ROWS // n6, back_three, u6)

    def block_sums(i):
        even = [grad_c[2 * i + k, pl.ds(0, WLOW, stride=2)] for k in range(4)]
        odd = [grad_c[2 * i + k, pl.ds(1, WLOW, stride=2)] for k in range(4)]
        for a in range(3):
            e, o = even[2 - a] + even[3 - a], odd[2 - a] + odd[3 - a]
            for b, total in enumerate((o + back(e, 0), e + o, ahead(o, 0) + e)):
                at = (a * 3 + b) * HID1
                blocks[i, :, at : at + HID1] = total.astype(BF)

    each(LOW, block_sums, CHUNK["blocks"])

    n7, u7 = CHUNK["back_two"]

    def back_two(i):
        low = mm(blocks[pl.ds(n7 * i, n7)].reshape(n7 * WLOW, 9 * HID1), w_up[...])
        cot = low.reshape(n7, WLOW, HID2) * slope_b[pl.ds(n7 * i, n7)]
        shifts = jnp.concatenate([back(cot, 1), cot, ahead(cot, 1)], axis=2)
        grad_b[pl.ds(n7 * i + 1, n7)] = shifts.astype(BF)

    each(LOW // n7, back_two, u7)
    held_low = OWN // 2
    cells = LOW * held_low
    low_b = act_b[:, :held_low].reshape(cells, HID2)
    for k in range(3):
        at = 3 * HID1 * k
        up = mm_tn(blocks[:, :held_low, at : at + 3 * HID1].reshape(cells, 3 * HID1), low_b)
        keep(near, at, up[:, :HID1])
        keep(near, at + UP_ROWS, up[:, HID1:])
    send(near)
    low_a = jnp.concatenate(
        [pooled[a : a + LOW, :held_low].reshape(cells, HID1) for a in range(3)], axis=1
    )
    for b in range(3):
        at = HID2 * b
        down = mm_tn(grad_b[1 : LOW + 1, :held_low, at : at + HID2].reshape(cells, HID2), low_a)
        for a in range(3):
            keep(far, (a * 3 + b) * HID2, down[:, HID1 * a : HID1 * (a + 1)])
    spread_w = jnp.concatenate([w_down[a] for a in range(3)], axis=1)
    wide = mm(grad_b[1 : LOW + 1, :held_low].reshape(cells, 3 * HID2), spread_w)
    low_taps[1 : LOW + 1] = wide.reshape(LOW, held_low, 3 * HID1)

    def back_one(i):
        low = (
            low_taps[i + 2, :, 0:HID1]
            + low_taps[i + 1, :, HID1 : 2 * HID1]
            + low_taps[i, :, 2 * HID1 :]
        )
        low = 0.25 * low
        phases[i, pl.ds(0, held_low, stride=2)] = low
        phases[i, pl.ds(1, held_low, stride=2)] = low
        spread = phases[i, 0:OWN]
        for pi in range(2):
            r = 2 * i + pi
            grad_a[r] = ((back_c[r, 0:OWN] + spread) * slope_a[r, 0:OWN]).astype(BF)

    each(LOW, back_one, CHUNK["back_one"])
    near_cells = jnp.concatenate(
        [net[a : a + ROWS, :OWN].reshape(ROWS * OWN, OWN) for a in range(3)], axis=1
    )
    inputs = mm_tn(grad_a[...].reshape(ROWS * OWN, HID1), near_cells)
    for a in range(3):
        part = inputs[:, a * OWN : (a + 1) * OWN].T
        keep(far, BIG_ROWS + a * 3 * FIELDS, part[: 3 * FIELDS])
    keep(far, BIG_ROWS + IN_ROWS, jnp.zeros((HALF_ROWS - BIG_ROWS - IN_ROWS, OWN), F32))
    send(far)
    for half in (near, far):
        pltpu.make_async_copy(halves.at[half], mine, sems.at[half]).wait()


def unpack_kernel(place, mine, other, seats, tile, first, down, up, last, downs, ups, firsts, lasts, tiles, sems):
    even = place[0] == 0

    def half(k, at, count):
        one, two = mine[pl.ds(at, count)], other[pl.ds(at, count)]
        return (jnp.where(even, one, two) if k == 0 else jnp.where(even, two, one)).astype(F32)

    def leave(a):
        return (
            pltpu.make_async_copy(ups.at[a], up.at[a], sems.at[0]),
            pltpu.make_async_copy(downs.at[a], down.at[a], sems.at[1]),
        )

    def thirds(a):
        at = pl.multiple_of(a * (3 * HID1), 3 * HID1)
        for k in range(2):
            piece = half(0, at + k * UP_ROWS, 3 * HID1)
            ups[a, :, :, k * HID1 : (k + 1) * HID1] = piece.reshape(3, HID1, HID1)
        downs[a] = half(1, 2 * at, 3 * HID2).reshape(3, HID2, HID1)
        for copy in leave(a):
            copy.start()

    each(3, thirds)
    inputs = half(1, BIG_ROWS, IN_ROWS)
    outputs = half(0, BIG_ROWS, 80)
    for a in range(3):
        for b in range(3):
            at = (a * 3 + b) * FIELDS
            firsts[a, b] = inputs[at : at + 20]
            at = (a * 3 + b) * 8 + 4
            lasts[a, b] = outputs[at : at + 4]
    small = [pltpu.make_async_copy(firsts, first, sems.at[2]), pltpu.make_async_copy(lasts, last, sems.at[3])]
    for copy in small:
        copy.start()
    blocks = seats[...].astype(F32)
    for k in range(8):
        for r in range(2):
            tiles[:, r, k * OWN : (k + 1) * OWN] = blocks[k, 4 * r : 4 * r + 4]
    small.append(pltpu.make_async_copy(tiles, tile, sems.at[4]))
    small[2].start()
    for copy in small:
        copy.wait()
    for a in range(3):
        for copy in leave(a):
            copy.wait()


def in_vmem(count):
    return [pl.BlockSpec(memory_space=pltpu.MemorySpace.VMEM) for _ in range(count)]


def in_hbm(count):
    return [pl.BlockSpec(memory_space=pltpu.MemorySpace.HBM) for _ in range(count)]


def in_smem():
    return pl.BlockSpec(memory_space=pltpu.MemorySpace.SMEM)


def pack(target, noise, land_mask, level_index):
    lats = target.shape[2] // OWN
    return pl.pallas_call(
        pack_kernel,
        out_shape=jax.ShapeDtypeStruct((lats, 2, 16, OWN), F32),
        in_specs=[in_smem(), *in_hbm(3)],
        out_specs=in_vmem(1)[0],
        scratch_shapes=[
            pltpu.VMEM(target.shape, F32),
            pltpu.VMEM(noise.shape, F32),
            pltpu.VMEM(land_mask.shape, jnp.int32),
            pltpu.SemaphoreType.DMA((3,)),
        ],
        name="pack",
    )(level_index, target, noise, land_mask)


def regress(*operands):
    return pl.pallas_call(
        regression_kernel,
        out_shape=(
            jax.ShapeDtypeStruct((ROWS, 8, LANES), F32),
            jax.ShapeDtypeStruct((ROWS, 16, LANES), F32),
        ),
        in_specs=[in_smem(), *in_vmem(4), *in_hbm(1), *in_vmem(1)],
        out_specs=tuple(in_vmem(2)),
        scratch_shapes=[
            pltpu.VMEM((3, OWN, OWN), F32),
            pltpu.VMEM((OWN, OWN), F32),
            pltpu.VMEM((ROWS + 2, WIDE, OWN), BF),
            pltpu.VMEM((LOW + 1, 2, WIDE, HID1), BF),
            pltpu.VMEM((ROWS, WIDE, HID1), BF),
            pltpu.VMEM((ROWS + 2, 72, LANES), F32),
            pltpu.VMEM((3, 3 * HID1, HID1), BF),
            pltpu.VMEM((3, 2 * HID1, 4 * HID1), BF),
            pltpu.SemaphoreType.DMA(()),
        ],
        compiler_params=pltpu.CompilerParams(vmem_limit_bytes=20 * 2**20),
        cost_estimate=pl.CostEstimate(flops=2 * 10**9, transcendentals=10**6, bytes_accessed=2 * 10**6),
        name="regress",
    )(*operands)


def step(scale, *operands):
    def kernel(*refs):
        step_kernel(scale, *refs)

    return pl.pallas_call(
        kernel,
        out_shape=(
            jax.ShapeDtypeStruct((HALF_ROWS, OWN), BF),
            jax.ShapeDtypeStruct((HALF_ROWS, OWN), BF),
            jax.ShapeDtypeStruct((LOW, CELL_ROWS, OWN), BF),
        ),
        in_specs=[in_smem(), *in_vmem(9)],
        out_specs=tuple(in_vmem(3)),
        scratch_shapes=[
            pltpu.VMEM((3, OWN, OWN), F32),
            pltpu.VMEM((OWN, OWN), F32),
            pltpu.VMEM((ROWS, 8, LANES), F32),
            pltpu.VMEM((ROWS + 2, WIDE, OWN), BF),
            pltpu.VMEM((ROWS, WIDE, HID1), BF),
            pltpu.VMEM((ROWS + 2, 72, LANES), F32),
            pltpu.VMEM((ROWS, 8, LANES), F32),
            pltpu.VMEM((ROWS, 8, LANES), F32),
            pltpu.VMEM((ROWS, WIDE, HID1), F32),
            pltpu.VMEM((ROWS, WIDE, HID1), BF),
            pltpu.VMEM((LOW, WIDE, HID1), F32),
            pltpu.VMEM((LOW + 2, WLOW, HID1), BF),
            pltpu.VMEM((LOW, WLOW, HID2), BF),
            pltpu.VMEM((LOW, WLOW, HID2), F32),
            pltpu.VMEM((LOW + 2, WLOW, 9 * HID1), F32),
            pltpu.VMEM((ROWS, WIDE, HID1), F32),
            pltpu.VMEM((ROWS, WIDE, HID1), F32),
            pltpu.VMEM((ROWS + 2, 8, LANES), F32),
            pltpu.VMEM((ROWS, WIDE, OWN), BF),
            pltpu.VMEM((ROWS, WIDE, HID1), F32),
            pltpu.VMEM((ROWS + 2, WIDE, HID1), F32),
            pltpu.VMEM((LOW, WLOW, 9 * HID1), BF),
            pltpu.VMEM((LOW + 2, WLOW, 3 * HID2), BF),
            pltpu.VMEM((ROWS, OWN, HID1), BF),
            pltpu.VMEM((80, HID1), F32),
            pltpu.VMEM((LOW, CELL_ROWS, OWN), F32),
            pltpu.VMEM((2, HALF_ROWS, OWN), BF),
            pltpu.VMEM((LOW + 2, OWN // 2, 3 * HID1), F32),
            pltpu.SemaphoreType.DMA((2,)),
        ],
        compiler_params=pltpu.CompilerParams(vmem_limit_bytes=44 * 2**20),
        name="step",
    )(*operands)


def unpack(place, mine, other, seats):
    outs = (
        (4, 2, 8 * OWN),
        (3, 3, 20, HID1),
        (3, 3, HID2, HID1),
        (3, 3, HID1, HID2),
        (3, 3, 4, HID1),
    )
    return pl.pallas_call(
        unpack_kernel,
        out_shape=tuple(jax.ShapeDtypeStruct(shape, F32) for shape in outs),
        in_specs=[in_smem(), *in_vmem(3)],
        out_specs=tuple([pl.BlockSpec(memory_space=pl.ANY)] * 5),
        scratch_shapes=[
            *(pltpu.VMEM(outs[k], F32) for k in (2, 3, 1, 4, 0)),
            pltpu.SemaphoreType.DMA((5,)),
        ],
        compiler_params=pltpu.CompilerParams(vmem_limit_bytes=16 * 2**20),
        name="unpack",
    )(place, mine, other, seats)


def all_to_all(value, axes):
    return lax.all_to_all(value, axes, split_axis=0, concat_axis=0, tiled=True)


def in_place(value):
    return pltpu.with_memory_space_constraint(value, pltpu.HBM)


def swap(value, axes, offset):
    count = lax.axis_size(axes)
    pairs = []
    for i in range(offset, count + offset, 2):
        here, there = i % count, (i + 1) % count
        pairs += [(here, there), (there, here)]
    return lax.ppermute(value, axes, sorted(set(pairs)))


def local(
    coarse,
    target,
    noise,
    land_mask,
    level_index,
    frozen_first,
    frozen_middle,
    frozen_last,
    diffuse_in,
    diffuse_down,
    diffuse_up,
    diffuse_out,
):
    scale = 1.0 / (target.shape[0] * math.sqrt(target.shape[1] * target.shape[2] * lax.axis_size(STRIPS)))
    place = jnp.stack([lax.axis_index("core"), lax.axis_index("z") % 2])
    place = place.astype(jnp.int32)
    packed = pack(target, noise, land_mask, level_index)
    packed = all_to_all(packed, LAT).reshape(ROWS, 16, OWN)
    strip = jnp.pad(coarse.transpose(1, 0, 2).astype(F32), ((0, 0), (0, 4), (0, 0)))
    strip_across = swap(strip, STRIPS, 1)
    strip_pair = swap(strip, STRIPS, 0)
    across = swap(packed, STRIPS, 1)
    pair = swap(packed, STRIPS, 0)
    mean, coarse_wide = regress(
        place,
        strip,
        strip_pair,
        strip_across,
        in_place(frozen_first.transpose(0, 1, 3, 2)),
        in_place(frozen_middle.reshape(3, 3 * HID1, HID1)),
        in_place(frozen_last),
    )
    grads, partner, tiles = step(
        scale,
        place,
        packed,
        pair,
        across,
        mean,
        coarse_wide,
        diffuse_in.transpose(0, 1, 3, 2),
        diffuse_down.reshape(3, 3 * HID2, HID1),
        diffuse_up.reshape(9 * HID1, HID2),
        diffuse_out,
    )
    chips = lax.axis_size(CHIPS)
    rows = HALF_ROWS // chips
    lats = tiles.shape[0]
    half = grads.astype(F32) + swap(partner, "core", 0).astype(F32)
    blocks = jnp.broadcast_to(tiles[None], (chips // lats, *tiles.shape)).reshape(chips, CELL_ROWS, OWN)
    sent = jnp.concatenate([half.astype(BF).reshape(chips, rows, OWN), blocks], axis=1)
    parts = all_to_all(sent, CHIPS)
    total = parts[:, :rows].astype(F32).sum(0).astype(BF)
    seats = parts.reshape(chips // lats, lats, rows + CELL_ROWS, OWN)[:, :, rows:]
    seats = lax.dynamic_index_in_dim(seats, lax.axis_index(("y", "x_hi")), 0, False)
    mine = all_to_all(jnp.broadcast_to(total[None], (chips, rows, OWN)), CHIPS).reshape(HALF_ROWS, OWN)
    tile, first, down, up, last = unpack(place, mine, swap(mine, "core", 0), seats)
    return (tile, first.transpose(0, 1, 3, 2), down, up, last)


def solution(mesh):
    fine = Mesh(mesh.devices.reshape(4, 2, 2, 2, 4), LON + LAT)
    tile = P(None, LAT, LON)
    return jax.shard_map(
        local,
        mesh=fine,
        in_specs=(
            P(None, None, STRIPS),
            tile,
            tile,
            P(LAT, LON),
            P(LAT, LON),
            *([P()] * 7),
        ),
        out_specs=(tile, P(), P(), P(), P()),
        check_vma=False,
    )
```

```python
import math

import jax
import jax.numpy as jnp
from jax import lax
from jax.experimental import pallas as pl
from jax.experimental.pallas import tpu as pltpu
from jax.sharding import Mesh
from jax.sharding import PartitionSpec as P


LEVELS = 32
ROWS = 16
LOW = ROWS // 2
OWN = 128
HALO = 16
WIDE = OWN + 2 * HALO
WLOW = WIDE // 2
LANES = 256
HID1 = 128
HID2 = 256
BF = jnp.bfloat16
F32 = jnp.float32

LON = ("y", "x_hi", "core")
LAT = ("x_lo", "z")
CHIPS = ("y", "x_hi", "x_lo", "z")
STRIPS = LON + LAT

FIELDS = 24
UP_ROWS = 9 * HID1
BIG_ROWS = 2304
LAST_ROWS = 72
IN_ROWS = 9 * FIELDS
HALF_ROWS = 2560
CELL_ROWS = 8
CHUNK = {
    "gather": 8,
    "first": (8, 2),
    "second": (4, 2),
    "taps": 8,
    "enter": 16,
    "one": (8, 2),
    "two": (2, 4),
    "up": (4, 2),
    "three": 2,
    "loss": 8,
    "last": 16,
    "back_three": (8, 1),
    "blocks": 4,
    "back_two": (4, 2),
    "back_one": 4,
}


def mm(x, w):
    return lax.dot_general(x, w, (((1,), (0,)), ((), ())), preferred_element_type=F32)


def mm_nt(x, w):
    return lax.dot_general(x, w, (((1,), (1,)), ((), ())), preferred_element_type=F32)


def mm_tn(x, w):
    return lax.dot_general(x, w, (((0,), (0,)), ((), ())), preferred_element_type=F32)


def back(x, axis):
    return pltpu.roll(x, x.shape[axis] - 1, axis)


def ahead(x, axis):
    return pltpu.roll(x, 1, axis)


def with_halo(own, left, right):
    lane = lax.broadcasted_iota(jnp.int32, own.shape, 1)
    halo = jnp.where(lane < HALO, right, jnp.where(lane >= OWN - HALO, left, 0.0))
    return jnp.concatenate([own, halo], axis=1)


def to_cells(stack):
    pad = OWN - stack.shape[0]
    if pad:
        stack = jnp.concatenate([stack, jnp.zeros((pad, LANES), F32)], axis=0)
    cells = stack.T
    return jnp.concatenate([cells[: OWN + HALO], cells[LANES - HALO :]], axis=0).astype(BF)


def to_lanes(cells):
    gap = jnp.zeros((LANES - WIDE, cells.shape[1]), cells.dtype)
    return jnp.concatenate([cells[: OWN + HALO], gap, cells[OWN + HALO :]], axis=0)


def lon_shifts(field):
    return jnp.concatenate([ahead(field, 1), field, back(field, 1)], axis=0)


def three_rows(ref, start, count):
    width = ref.shape[1]
    return jnp.concatenate(
        [ref[pl.ds(start + a, count)].reshape(count * width, ref.shape[2]) for a in range(3)], axis=1
    )


def lon_sum(taps, count, width, out):
    first, second, third = (
        taps[:, b * out : (b + 1) * out].reshape(count, width, out) for b in range(3)
    )
    return ahead(first, 1) + second + back(third, 1)


def four_channels(ref, row):
    sums = []
    for b in range(3):
        at = [(a * 3 + b) * 8 for a in range(3)]
        sums.append(
            ref[row, at[0] : at[0] + 8]
            + ref[row + 1, at[1] : at[1] + 8]
            + ref[row + 2, at[2] : at[2] + 8]
        )
    return ahead(sums[0], 1) + sums[1] + back(sums[2], 1)


def zero_edges(ref):
    edge = jnp.zeros(ref.shape[1:], ref.dtype)
    ref[0] = edge
    ref[ref.shape[0] - 1] = edge


def each(count, body, unroll=1):
    def step(i, carry):
        body(i)
        return carry

    lax.fori_loop(0, count, step, 0, unroll=unroll)


def pack_kernel(level, target_far, noise_far, mask_far, packed, target, noise, land_mask, sems):
    arrive = [
        pltpu.make_async_copy(target_far, target, sems.at[0]),
        pltpu.make_async_copy(noise_far, noise, sems.at[1]),
        pltpu.make_async_copy(mask_far, land_mask, sems.at[2]),
    ]
    for copy in arrive:
        copy.start()
    power = jnp.full((1, OWN), level[0, 0], jnp.int32).astype(F32) / (LEVELS - 1)
    sigma = 0.02 * jnp.exp(power * math.log(4000.0))
    for copy in arrive:
        copy.wait()
    weight = 1.0 + land_mask[...].astype(F32)
    for p in range(packed.shape[0]):
        lanes = slice(p * OWN, (p + 1) * OWN)
        for r in range(2):
            packed[p, r, 0:1] = weight[r : r + 1, lanes]
            packed[p, r, 1:2] = sigma
            packed[p, r, 2:4] = jnp.zeros((2, OWN), F32)
            packed[p, r, 4:8] = target[:, r, lanes]
            packed[p, r, 8:12] = jnp.zeros((4, OWN), F32)
            packed[p, r, 12:16] = noise[:, r, lanes]


def stack_inputs(ref, weight, room):
    ref[...] = jnp.zeros_like(ref)
    count = weight.shape[2]
    for a in range(3):
        for b in range(3):
            ref[a, b * room : b * room + count] = weight[a, b].astype(F32)
    return ref[...].astype(BF).reshape(3 * OWN, OWN)


def stack_outputs(ref, weight):
    ref[...] = jnp.zeros_like(ref)
    for a in range(3):
        for b in range(3):
            at = (a * 3 + b) * 8 + 4
            ref[at : at + 4] = weight[a, b].astype(F32)
    return ref[...].astype(BF)


def regression_kernel(
    place,
    own,
    pair,
    across,
    w_first,
    w_middle,
    w_last,
    mean,
    coarse,
    stack,
    stack_o,
    net,
    hid,
    sec,
    taps,
    w_near,
    pair_w,
    sem,
):
    zero_edges(net)
    zero_edges(taps)
    hid[0, 0] = jnp.zeros((WIDE, HID1), BF)
    hid[LOW, 1] = jnp.zeros((WIDE, HID1), BF)
    even = place[1] == 0
    fetch = pltpu.make_async_copy(w_middle, w_near, sem)
    fetch.start()
    first_w = stack_inputs(stack, w_first, 16)

    def gather(r):
        near, far = pair[r].astype(F32), across[r].astype(F32)
        wide = with_halo(own[r].astype(F32), jnp.where(even, far, near), jnp.where(even, near, far))
        coarse[r] = wide
        net[r + 1] = to_cells(lon_shifts(wide))

    each(ROWS, gather, CHUNK["gather"])

    n1, u1 = CHUNK["first"]

    def first(i):
        pre = mm(three_rows(net, n1 * i, n1), first_w)
        act = jax.nn.silu(pre).astype(BF).reshape(n1 // 2, 2, WIDE, HID1)
        hid[pl.ds((n1 // 2) * i, n1 // 2), 1] = act[:, 0]
        hid[pl.ds((n1 // 2) * i + 1, n1 // 2), 0] = act[:, 1]

    each(ROWS // n1, first, u1)
    fetch.wait()
    gap = jnp.zeros((HID1, HID1), BF)
    for b in range(3):
        taps_b = [w_near[a, b * HID1 : (b + 1) * HID1] for a in range(3)]
        pair_w[b, 0:HID1] = jnp.concatenate([*taps_b, gap], axis=1)
        pair_w[b, HID1:] = jnp.concatenate([gap, *taps_b], axis=1)
    n2, u2 = CHUNK["second"]

    def second(i):
        rows = [hid[pl.ds(n2 * i + j // 2, n2), j % 2].reshape(n2 * WIDE, HID1) for j in range(4)]
        quads = jnp.concatenate(rows, axis=1)
        parts = [mm_nt(quads, pair_w[b]).reshape(n2, WIDE, 2 * HID1) for b in range(3)]
        act = jax.nn.silu(ahead(parts[0], 1) + parts[1] + back(parts[2], 1)).astype(BF)
        for k in range(n2):
            row = 2 * (n2 * i + k)
            sec[row] = act[k, :, :HID1]
            sec[row + 1] = act[k, :, HID1:]

    each(LOW // n2, second, u2)
    last_w = stack_outputs(stack_o, w_last)[0:72]

    def mean_taps(r):
        taps[r + 1] = mm_nt(last_w, to_lanes(sec[r]))

    each(ROWS, mean_taps, CHUNK["taps"])

    def collect(r):
        mean[r] = four_channels(taps, r).astype(BF).astype(F32)

    each(ROWS, collect, CHUNK["taps"])


def step_kernel(
    scale,
    place,
    own,
    pair,
    across,
    mean,
    coarse,
    w_in,
    w_down,
    w_up,
    w_out,
    mine,
    other,
    tiles,
    *scratch,
):
    (
        stack,
        stack_o,
        field,
        net,
        act_c,
        taps,
        residuals,
        noisies,
        slope_a,
        act_a,
        pairs,
        pooled,
        act_b,
        slope_b,
        up_taps,
        phases,
        slope_c,
        grad_f,
        spread_f,
        back_c,
        grad_c,
        blocks,
        grad_b,
        grad_a,
        last_sum,
        den,
        halves,
        low_taps,
        sems,
    ) = scratch
    for ref in (net, pooled, up_taps, taps, grad_f, grad_c, grad_b, low_taps):
        zero_edges(ref)
    even = place[1] == 0
    in_w = stack_inputs(stack, w_in, FIELDS)
    lane = lax.broadcasted_iota(jnp.int32, (8, LANES), 1)
    held = (lane < OWN + HALO) | (lane >= LANES - HALO)
    low_half = lax.broadcasted_iota(jnp.int32, (8, LANES), 0) < 4

    def enter(r):
        near, far = pair[r], across[r]
        wide = with_halo(own[r], jnp.where(even, far, near), jnp.where(even, near, far))
        field[r] = wide[0:8]
        mean_r = mean[r]
        sigma = jnp.where(held, jnp.broadcast_to(wide[1:2], (8, LANES)), 1.0)
        residual = wide[0:8] - mean_r
        noisy = residual + sigma * wide[8:16]
        variance = sigma * sigma + 0.25
        residuals[r] = residual
        noisies[r] = noisy
        scaled = (lax.rsqrt(variance) * noisy).astype(BF).astype(F32)
        both = jnp.where(low_half, pltpu.roll(mean_r, 4, 0), scaled)
        net[r + 1] = to_cells(lon_shifts(jnp.concatenate([both, coarse[r]], axis=0)))

    each(ROWS, enter, CHUNK["enter"])

    n3, u3 = CHUNK["one"]

    def level_one(i):
        pre = mm(three_rows(net, n3 * i, n3), in_w)
        gate = jax.nn.sigmoid(pre)
        slope_a[pl.ds(n3 * i, n3)] = (gate * (1.0 + pre * (1.0 - gate))).reshape(n3, WIDE, HID1)
        act = (pre * gate).astype(BF).reshape(n3, WIDE, HID1)
        act_a[pl.ds(n3 * i, n3)] = act
        wide = act.astype(F32)
        for k in range(n3 // 2):
            row = (n3 // 2) * i + k
            pairs[row] = wide[2 * k] + wide[2 * k + 1]
            total = pairs[row, pl.ds(0, WLOW, stride=2)] + pairs[row, pl.ds(1, WLOW, stride=2)]
            pooled[row + 1] = (0.25 * total).astype(BF)

    each(ROWS // n3, level_one, u3)
    down_w = jnp.concatenate([w_down[a] for a in range(3)], axis=1)

    n4, u4 = CHUNK["two"]

    def level_two(i):
        pre = lon_sum(mm_nt(three_rows(pooled, n4 * i, n4), down_w), n4, WLOW, HID2)
        gate = jax.nn.sigmoid(pre)
        slope_b[pl.ds(n4 * i, n4)] = gate * (1.0 + pre * (1.0 - gate))
        act_b[pl.ds(n4 * i, n4)] = (pre * gate).astype(BF)

    each(LOW // n4, level_two, u4)
    n5, u5 = CHUNK["up"]

    def up_products(i):
        low = act_b[pl.ds(n5 * i, n5)].reshape(n5 * WLOW, HID2)
        up_taps[pl.ds(n5 * i + 1, n5)] = mm_nt(low, w_up[...]).reshape(n5, WLOW, 9 * HID1)

    each(LOW // n5, up_products, u5)

    def level_three(i):
        for pi in range(2):
            sums = []
            for b in range(3):
                total = None
                for a in range(3):
                    row = i + 1 + (pi + a - 1) // 2
                    at = (a * 3 + b) * HID1
                    part = up_taps[row, :, at : at + HID1]
                    total = part if total is None else total + part
                sums.append(total)
            row = 2 * i + pi
            phases[row, pl.ds(0, WLOW, stride=2)] = ahead(sums[0], 0) + sums[1] + sums[2]
            phases[row, pl.ds(1, WLOW, stride=2)] = sums[0] + sums[1] + back(sums[2], 0)
            pre = phases[row]
            gate = jax.nn.sigmoid(pre)
            act_c[row] = (pre * gate + act_a[row].astype(F32)).astype(BF)
            slope_c[row] = gate * (1.0 + pre * (1.0 - gate))

    each(LOW, level_three, CHUNK["three"])
    out_w = stack_outputs(stack_o, w_out)

    def field_taps(r):
        taps[r + 1] = mm_nt(out_w[0:72], to_lanes(act_c[r]))

    each(ROWS, field_taps, CHUNK["taps"])

    def loss(i):
        for k in range(2):
            r = 2 * i + k
            value = four_channels(taps, r)
            sigma = jnp.where(held, jnp.broadcast_to(field[r, 1:2], (8, LANES)), 1.0)
            weight = jnp.broadcast_to(field[r, 0:1], (8, LANES))
            variance = sigma * sigma + 0.25
            c_out = 0.5 * sigma * lax.rsqrt(variance)
            lam = variance / (0.25 * sigma * sigma)
            denoised = (0.25 / variance) * noisies[r] + c_out * value
            den[i, 4 * k : 4 * k + 4] = denoised[4:8, :OWN]
            loss_grad = (2.0 * scale) * weight * lam * (denoised - residuals[r])
            cot = (c_out * loss_grad).astype(BF).astype(F32)
            grad_f[r + 1] = jnp.where(low_half, 0.0, cot)

    each(LOW, loss, CHUNK["loss"])
    tiles[...] = den[...].astype(BF)
    last_sum[...] = jnp.zeros_like(last_sum)

    def last_grads(r):
        parts = []
        for a in range(3):
            cot = grad_f[r + 2 - a]
            parts += [back(cot, 1), cot, ahead(cot, 1)]
        cots = jnp.concatenate(parts + [jnp.zeros((8, LANES), F32)], axis=0)
        last_sum[...] += mm(cots[:, :OWN].astype(BF), act_c[r, 0:OWN])
        spread_f[r] = to_cells(cots)

    each(ROWS, last_grads, CHUNK["last"])
    near, far = 0, 1

    def keep(half, at, value):
        halves[half, at : at + value.shape[0]] = value.astype(BF)

    def send(half):
        for core, target in ((half, mine), (1 - half, other)):

            @pl.when(place[0] == core)
            def _():
                pltpu.make_async_copy(halves.at[half], target, sems.at[half]).start()

    keep(near, BIG_ROWS, last_sum[0:LAST_ROWS])
    keep(near, BIG_ROWS + LAST_ROWS, jnp.zeros((HALF_ROWS - BIG_ROWS - LAST_ROWS, OWN), F32))

    n6, u6 = CHUNK["back_three"]

    def back_three(i):
        wide = mm(spread_f[pl.ds(n6 * i, n6)].reshape(n6 * WIDE, OWN), out_w)
        wide = wide.reshape(n6, WIDE, HID1)
        back_c[pl.ds(n6 * i, n6)] = wide
        grad_c[pl.ds(n6 * i + 1, n6)] = wide * slope_c[pl.ds(n6 * i, n6)]

    each(ROWS // n6, back_three, u6)

    def block_sums(i):
        even = [grad_c[2 * i + k, pl.ds(0, WLOW, stride=2)] for k in range(4)]
        odd = [grad_c[2 * i + k, pl.ds(1, WLOW, stride=2)] for k in range(4)]
        for a in range(3):
            e, o = even[2 - a] + even[3 - a], odd[2 - a] + odd[3 - a]
            for b, total in enumerate((o + back(e, 0), e + o, ahead(o, 0) + e)):
                at = (a * 3 + b) * HID1
                blocks[i, :, at : at + HID1] = total.astype(BF)

    each(LOW, block_sums, CHUNK["blocks"])

    n7, u7 = CHUNK["back_two"]

    def back_two(i):
        low = mm(blocks[pl.ds(n7 * i, n7)].reshape(n7 * WLOW, 9 * HID1), w_up[...])
        cot = low.reshape(n7, WLOW, HID2) * slope_b[pl.ds(n7 * i, n7)]
        shifts = jnp.concatenate([back(cot, 1), cot, ahead(cot, 1)], axis=2)
        grad_b[pl.ds(n7 * i + 1, n7)] = shifts.astype(BF)

    each(LOW // n7, back_two, u7)
    held_low = OWN // 2
    cells = LOW * held_low
    low_b = act_b[:, :held_low].reshape(cells, HID2)
    for k in range(3):
        at = 3 * HID1 * k
        up = mm_tn(blocks[:, :held_low, at : at + 3 * HID1].reshape(cells, 3 * HID1), low_b)
        keep(near, at, up[:, :HID1])
        keep(near, at + UP_ROWS, up[:, HID1:])
    send(near)
    low_a = jnp.concatenate(
        [pooled[a : a + LOW, :held_low].reshape(cells, HID1) for a in range(3)], axis=1
    )
    for b in range(3):
        at = HID2 * b
        down = mm_tn(grad_b[1 : LOW + 1, :held_low, at : at + HID2].reshape(cells, HID2), low_a)
        for a in range(3):
            keep(far, (a * 3 + b) * HID2, down[:, HID1 * a : HID1 * (a + 1)])
    spread_w = jnp.concatenate([w_down[a] for a in range(3)], axis=1)
    wide = mm(grad_b[1 : LOW + 1, :held_low].reshape(cells, 3 * HID2), spread_w)
    low_taps[1 : LOW + 1] = wide.reshape(LOW, held_low, 3 * HID1)

    def back_one(i):
        low = (
            low_taps[i + 2, :, 0:HID1]
            + low_taps[i + 1, :, HID1 : 2 * HID1]
            + low_taps[i, :, 2 * HID1 :]
        )
        low = 0.25 * low
        phases[i, pl.ds(0, held_low, stride=2)] = low
        phases[i, pl.ds(1, held_low, stride=2)] = low
        spread = phases[i, 0:OWN]
        for pi in range(2):
            r = 2 * i + pi
            grad_a[r] = ((back_c[r, 0:OWN] + spread) * slope_a[r, 0:OWN]).astype(BF)

    each(LOW, back_one, CHUNK["back_one"])
    near_cells = jnp.concatenate(
        [net[a : a + ROWS, :OWN].reshape(ROWS * OWN, OWN) for a in range(3)], axis=1
    )
    inputs = mm_tn(grad_a[...].reshape(ROWS * OWN, HID1), near_cells)
    for a in range(3):
        part = inputs[:, a * OWN : (a + 1) * OWN].T
        keep(far, BIG_ROWS + a * 3 * FIELDS, part[: 3 * FIELDS])
    keep(far, BIG_ROWS + IN_ROWS, jnp.zeros((HALF_ROWS - BIG_ROWS - IN_ROWS, OWN), F32))
    send(far)
    for half in (near, far):
        pltpu.make_async_copy(halves.at[half], mine, sems.at[half]).wait()


def unpack_kernel(place, mine, other, seats, tile, first, down, up, last, downs, ups, firsts, lasts, tiles, sems):
    even = place[0] == 0

    def half(k, at, count):
        one, two = mine[pl.ds(at, count)], other[pl.ds(at, count)]
        return (jnp.where(even, one, two) if k == 0 else jnp.where(even, two, one)).astype(F32)

    def leave(a):
        return (
            pltpu.make_async_copy(ups.at[a], up.at[a], sems.at[0]),
            pltpu.make_async_copy(downs.at[a], down.at[a], sems.at[1]),
        )

    def thirds(a):
        at = pl.multiple_of(a * (3 * HID1), 3 * HID1)
        for k in range(2):
            piece = half(0, at + k * UP_ROWS, 3 * HID1)
            ups[a, :, :, k * HID1 : (k + 1) * HID1] = piece.reshape(3, HID1, HID1)
        downs[a] = half(1, 2 * at, 3 * HID2).reshape(3, HID2, HID1)
        for copy in leave(a):
            copy.start()

    each(3, thirds)
    inputs = half(1, BIG_ROWS, IN_ROWS)
    outputs = half(0, BIG_ROWS, 80)
    for a in range(3):
        for b in range(3):
            at = (a * 3 + b) * FIELDS
            firsts[a, b] = inputs[at : at + 20]
            at = (a * 3 + b) * 8 + 4
            lasts[a, b] = outputs[at : at + 4]
    small = [pltpu.make_async_copy(firsts, first, sems.at[2]), pltpu.make_async_copy(lasts, last, sems.at[3])]
    for copy in small:
        copy.start()
    blocks = seats[...].astype(F32)
    for k in range(8):
        for r in range(2):
            tiles[:, r, k * OWN : (k + 1) * OWN] = blocks[k, 4 * r : 4 * r + 4]
    small.append(pltpu.make_async_copy(tiles, tile, sems.at[4]))
    small[2].start()
    for copy in small:
        copy.wait()
    for a in range(3):
        for copy in leave(a):
            copy.wait()


def in_vmem(count):
    return [pl.BlockSpec(memory_space=pltpu.MemorySpace.VMEM) for _ in range(count)]


def in_hbm(count):
    return [pl.BlockSpec(memory_space=pltpu.MemorySpace.HBM) for _ in range(count)]


def in_smem():
    return pl.BlockSpec(memory_space=pltpu.MemorySpace.SMEM)


def pack(target, noise, land_mask, level_index):
    lats = target.shape[2] // OWN
    return pl.pallas_call(
        pack_kernel,
        out_shape=jax.ShapeDtypeStruct((lats, 2, 16, OWN), F32),
        in_specs=[in_smem(), *in_hbm(3)],
        out_specs=in_vmem(1)[0],
        scratch_shapes=[
            pltpu.VMEM(target.shape, F32),
            pltpu.VMEM(noise.shape, F32),
            pltpu.VMEM(land_mask.shape, jnp.int32),
            pltpu.SemaphoreType.DMA((3,)),
        ],
        name="pack",
    )(level_index, target, noise, land_mask)


def regress(*operands):
    return pl.pallas_call(
        regression_kernel,
        out_shape=(
            jax.ShapeDtypeStruct((ROWS, 8, LANES), F32),
            jax.ShapeDtypeStruct((ROWS, 16, LANES), F32),
        ),
        in_specs=[in_smem(), *in_vmem(4), *in_hbm(1), *in_vmem(1)],
        out_specs=tuple(in_vmem(2)),
        scratch_shapes=[
            pltpu.VMEM((3, OWN, OWN), F32),
            pltpu.VMEM((OWN, OWN), F32),
            pltpu.VMEM((ROWS + 2, WIDE, OWN), BF),
            pltpu.VMEM((LOW + 1, 2, WIDE, HID1), BF),
            pltpu.VMEM((ROWS, WIDE, HID1), BF),
            pltpu.VMEM((ROWS + 2, 72, LANES), F32),
            pltpu.VMEM((3, 3 * HID1, HID1), BF),
            pltpu.VMEM((3, 2 * HID1, 4 * HID1), BF),
            pltpu.SemaphoreType.DMA(()),
        ],
        compiler_params=pltpu.CompilerParams(vmem_limit_bytes=20 * 2**20),
        cost_estimate=pl.CostEstimate(flops=2 * 10**9, transcendentals=10**6, bytes_accessed=2 * 10**6),
        name="regress",
    )(*operands)


def step(scale, *operands):
    def kernel(*refs):
        step_kernel(scale, *refs)

    return pl.pallas_call(
        kernel,
        out_shape=(
            jax.ShapeDtypeStruct((HALF_ROWS, OWN), BF),
            jax.ShapeDtypeStruct((HALF_ROWS, OWN), BF),
            jax.ShapeDtypeStruct((LOW, CELL_ROWS, OWN), BF),
        ),
        in_specs=[in_smem(), *in_vmem(9)],
        out_specs=tuple(in_vmem(3)),
        scratch_shapes=[
            pltpu.VMEM((3, OWN, OWN), F32),
            pltpu.VMEM((OWN, OWN), F32),
            pltpu.VMEM((ROWS, 8, LANES), F32),
            pltpu.VMEM((ROWS + 2, WIDE, OWN), BF),
            pltpu.VMEM((ROWS, WIDE, HID1), BF),
            pltpu.VMEM((ROWS + 2, 72, LANES), F32),
            pltpu.VMEM((ROWS, 8, LANES), F32),
            pltpu.VMEM((ROWS, 8, LANES), F32),
            pltpu.VMEM((ROWS, WIDE, HID1), F32),
            pltpu.VMEM((ROWS, WIDE, HID1), BF),
            pltpu.VMEM((LOW, WIDE, HID1), F32),
            pltpu.VMEM((LOW + 2, WLOW, HID1), BF),
            pltpu.VMEM((LOW, WLOW, HID2), BF),
            pltpu.VMEM((LOW, WLOW, HID2), F32),
            pltpu.VMEM((LOW + 2, WLOW, 9 * HID1), F32),
            pltpu.VMEM((ROWS, WIDE, HID1), F32),
            pltpu.VMEM((ROWS, WIDE, HID1), F32),
            pltpu.VMEM((ROWS + 2, 8, LANES), F32),
            pltpu.VMEM((ROWS, WIDE, OWN), BF),
            pltpu.VMEM((ROWS, WIDE, HID1), F32),
            pltpu.VMEM((ROWS + 2, WIDE, HID1), F32),
            pltpu.VMEM((LOW, WLOW, 9 * HID1), BF),
            pltpu.VMEM((LOW + 2, WLOW, 3 * HID2), BF),
            pltpu.VMEM((ROWS, OWN, HID1), BF),
            pltpu.VMEM((80, HID1), F32),
            pltpu.VMEM((LOW, CELL_ROWS, OWN), F32),
            pltpu.VMEM((2, HALF_ROWS, OWN), BF),
            pltpu.VMEM((LOW + 2, OWN // 2, 3 * HID1), F32),
            pltpu.SemaphoreType.DMA((2,)),
        ],
        compiler_params=pltpu.CompilerParams(vmem_limit_bytes=44 * 2**20),
        name="step",
    )(*operands)


def unpack(place, mine, other, seats):
    outs = (
        (4, 2, 8 * OWN),
        (3, 3, 20, HID1),
        (3, 3, HID2, HID1),
        (3, 3, HID1, HID2),
        (3, 3, 4, HID1),
    )
    return pl.pallas_call(
        unpack_kernel,
        out_shape=tuple(jax.ShapeDtypeStruct(shape, F32) for shape in outs),
        in_specs=[in_smem(), *in_vmem(3)],
        out_specs=tuple([pl.BlockSpec(memory_space=pl.ANY)] * 5),
        scratch_shapes=[
            *(pltpu.VMEM(outs[k], F32) for k in (2, 3, 1, 4, 0)),
            pltpu.SemaphoreType.DMA((5,)),
        ],
        compiler_params=pltpu.CompilerParams(vmem_limit_bytes=16 * 2**20),
        name="unpack",
    )(place, mine, other, seats)


def all_to_all(value, axes):
    return lax.all_to_all(value, axes, split_axis=0, concat_axis=0, tiled=True)


def in_place(value):
    return pltpu.with_memory_space_constraint(value, pltpu.HBM)


def swap(value, axes, offset):
    count = lax.axis_size(axes)
    pairs = []
    for i in range(offset, count + offset, 2):
        here, there = i % count, (i + 1) % count
        pairs += [(here, there), (there, here)]
    return lax.ppermute(value, axes, sorted(set(pairs)))


def local(
    coarse,
    target,
    noise,
    land_mask,
    level_index,
    frozen_first,
    frozen_middle,
    frozen_last,
    diffuse_in,
    diffuse_down,
    diffuse_up,
    diffuse_out,
):
    scale = 1.0 / (target.shape[0] * math.sqrt(target.shape[1] * target.shape[2] * lax.axis_size(STRIPS)))
    place = jnp.stack([lax.axis_index("core"), lax.axis_index("z") % 2])
    place = place.astype(jnp.int32)
    packed = pack(target, noise, land_mask, level_index)
    packed = all_to_all(packed, LAT).reshape(ROWS, 16, OWN)
    strip = jnp.pad(coarse.transpose(1, 0, 2), ((0, 0), (0, 4), (0, 0)))
    strip_across = swap(strip, STRIPS, 1)
    strip_pair = swap(strip, STRIPS, 0)
    across = swap(packed, STRIPS, 1)
    pair = swap(packed, STRIPS, 0)
    mean, coarse_wide = regress(
        place,
        strip,
        strip_pair,
        strip_across,
        in_place(frozen_first.transpose(0, 1, 3, 2)),
        in_place(frozen_middle.reshape(3, 3 * HID1, HID1)),
        in_place(frozen_last),
    )
    grads, partner, tiles = step(
        scale,
        place,
        packed,
        pair,
        across,
        mean,
        coarse_wide,
        diffuse_in.transpose(0, 1, 3, 2),
        diffuse_down.reshape(3, 3 * HID2, HID1),
        diffuse_up.reshape(9 * HID1, HID2),
        diffuse_out,
    )
    chips = lax.axis_size(CHIPS)
    rows = HALF_ROWS // chips
    lats = tiles.shape[0]
    half = grads.astype(F32) + swap(partner, "core", 0).astype(F32)
    blocks = jnp.broadcast_to(tiles[None], (chips // lats, *tiles.shape)).reshape(chips, CELL_ROWS, OWN)
    sent = jnp.concatenate([half.astype(BF).reshape(chips, rows, OWN), blocks], axis=1)
    parts = all_to_all(sent, CHIPS)
    total = parts[:, :rows].astype(F32).sum(0).astype(BF)
    seats = parts.reshape(chips // lats, lats, rows + CELL_ROWS, OWN)[:, :, rows:]
    seats = lax.dynamic_index_in_dim(seats, lax.axis_index(("y", "x_hi")), 0, False)
    mine = all_to_all(jnp.broadcast_to(total[None], (chips, rows, OWN)), CHIPS).reshape(HALF_ROWS, OWN)
    tile, first, down, up, last = unpack(place, mine, swap(mine, "core", 0), seats)
    return (tile, first.transpose(0, 1, 3, 2), down, up, last)


def solution(mesh):
    fine = Mesh(mesh.devices.reshape(4, 2, 2, 2, 4), LON + LAT)
    tile = P(None, LAT, LON)
    return jax.shard_map(
        local,
        mesh=fine,
        in_specs=(
            P(None, None, STRIPS),
            tile,
            tile,
            P(LAT, LON),
            P(LAT, LON),
            *([P()] * 7),
        ),
        out_specs=(tile, P(), P(), P(), P()),
        check_vma=False,
    )
```

```python
import math

import jax
import jax.numpy as jnp
from jax import lax
from jax.experimental import pallas as pl
from jax.experimental.pallas import tpu as pltpu
from jax.sharding import Mesh
from jax.sharding import PartitionSpec as P


LEVELS = 32
ROWS = 16
LOW = ROWS // 2
OWN = 128
HALO = 16
WIDE = OWN + 2 * HALO
WLOW = WIDE // 2
LANES = 256
HID1 = 128
HID2 = 256
BF = jnp.bfloat16
F32 = jnp.float32

LON = ("y", "x_hi", "core")
LAT = ("x_lo", "z")
CHIPS = ("y", "x_hi", "x_lo", "z")
STRIPS = LON + LAT

FIELDS = 24
UP_ROWS = 9 * HID1
BIG_ROWS = 2304
LAST_ROWS = 72
IN_ROWS = 9 * FIELDS
HALF_ROWS = 2560
CELL_ROWS = 8
CHUNK = {
    "gather": 16,
    "first": (8, 2),
    "second": (4, 2),
    "taps": 8,
    "enter": 16,
    "one": (8, 2),
    "two": (2, 4),
    "up": (4, 2),
    "three": 2,
    "loss": 8,
    "last": 16,
    "back_three": (8, 1),
    "blocks": 4,
    "back_two": (4, 2),
    "back_one": 4,
}


def mm(x, w):
    return lax.dot_general(x, w, (((1,), (0,)), ((), ())), preferred_element_type=F32)


def mm_nt(x, w):
    return lax.dot_general(x, w, (((1,), (1,)), ((), ())), preferred_element_type=F32)


def mm_tn(x, w):
    return lax.dot_general(x, w, (((0,), (0,)), ((), ())), preferred_element_type=F32)


def back(x, axis):
    return pltpu.roll(x, x.shape[axis] - 1, axis)


def ahead(x, axis):
    return pltpu.roll(x, 1, axis)


def with_halo(own, left, right):
    lane = lax.broadcasted_iota(jnp.int32, own.shape, 1)
    halo = jnp.where(lane < HALO, right, jnp.where(lane >= OWN - HALO, left, 0.0))
    return jnp.concatenate([own, halo], axis=1)


def to_cells(stack):
    pad = OWN - stack.shape[0]
    if pad:
        stack = jnp.concatenate([stack, jnp.zeros((pad, LANES), F32)], axis=0)
    cells = stack.T
    return jnp.concatenate([cells[: OWN + HALO], cells[LANES - HALO :]], axis=0).astype(BF)


def to_lanes(cells):
    gap = jnp.zeros((LANES - WIDE, cells.shape[1]), cells.dtype)
    return jnp.concatenate([cells[: OWN + HALO], gap, cells[OWN + HALO :]], axis=0)


def lon_shifts(field):
    return jnp.concatenate([ahead(field, 1), field, back(field, 1)], axis=0)


def three_rows(ref, start, count):
    width = ref.shape[1]
    return jnp.concatenate(
        [ref[pl.ds(start + a, count)].reshape(count * width, ref.shape[2]) for a in range(3)], axis=1
    )


def lon_sum(taps, count, width, out):
    first, second, third = (
        taps[:, b * out : (b + 1) * out].reshape(count, width, out) for b in range(3)
    )
    return ahead(first, 1) + second + back(third, 1)


def four_channels(ref, row):
    sums = []
    for b in range(3):
        at = [(a * 3 + b) * 8 for a in range(3)]
        sums.append(
            ref[row, at[0] : at[0] + 8]
            + ref[row + 1, at[1] : at[1] + 8]
            + ref[row + 2, at[2] : at[2] + 8]
        )
    return ahead(sums[0], 1) + sums[1] + back(sums[2], 1)


def zero_edges(ref):
    edge = jnp.zeros(ref.shape[1:], ref.dtype)
    ref[0] = edge
    ref[ref.shape[0] - 1] = edge


def each(count, body, unroll=1):
    def step(i, carry):
        body(i)
        return carry

    lax.fori_loop(0, count, step, 0, unroll=unroll)


def pack_kernel(
    level, target_far, noise_far, mask_far, coarse_far, packed, strip, target, noise, land_mask, coarse, sems
):
    arrive = [
        pltpu.make_async_copy(target_far, target, sems.at[0]),
        pltpu.make_async_copy(noise_far, noise, sems.at[1]),
        pltpu.make_async_copy(mask_far, land_mask, sems.at[2]),
        pltpu.make_async_copy(coarse_far, coarse, sems.at[3]),
    ]
    for copy in arrive:
        copy.start()
    power = jnp.full((1, OWN), level[0, 0], jnp.int32).astype(F32) / (LEVELS - 1)
    sigma = 0.02 * jnp.exp(power * math.log(4000.0))
    for copy in arrive:
        copy.wait()
    weight = 1.0 + land_mask[...].astype(F32)
    for p in range(packed.shape[0]):
        lanes = slice(p * OWN, (p + 1) * OWN)
        for r in range(2):
            packed[p, r, 0:1] = weight[r : r + 1, lanes]
            packed[p, r, 1:2] = sigma
            packed[p, r, 2:4] = jnp.zeros((2, OWN), F32)
            packed[p, r, 4:8] = target[:, r, lanes]
            packed[p, r, 8:12] = jnp.zeros((4, OWN), F32)
            packed[p, r, 12:16] = noise[:, r, lanes]
    rows = jnp.transpose(coarse[...].astype(F32), (1, 0, 2))
    strip[...] = jnp.concatenate([rows, jnp.zeros((ROWS, 4, OWN), F32)], axis=1).astype(BF)


def stack_inputs(ref, weight, room):
    ref[...] = jnp.zeros_like(ref)
    count = weight.shape[2]
    for a in range(3):
        for b in range(3):
            ref[a, b * room : b * room + count] = weight[a, b].astype(F32)
    return ref[...].astype(BF).reshape(3 * OWN, OWN)


def stack_outputs(ref, weight):
    ref[...] = jnp.zeros_like(ref)
    for a in range(3):
        for b in range(3):
            at = (a * 3 + b) * 8 + 4
            ref[at : at + 4] = weight[a, b].astype(F32)
    return ref[...].astype(BF)


def regression_kernel(
    place,
    own,
    pair,
    across,
    w_first,
    w_middle,
    w_last,
    mean,
    coarse,
    stack,
    stack_o,
    net,
    hid,
    sec,
    taps,
    w_near,
    pair_w,
    sem,
):
    zero_edges(net)
    zero_edges(taps)
    hid[0, 0] = jnp.zeros((WIDE, HID1), BF)
    hid[LOW, 1] = jnp.zeros((WIDE, HID1), BF)
    even = place[1] == 0
    fetch = pltpu.make_async_copy(w_middle, w_near, sem)
    fetch.start()
    first_w = stack_inputs(stack, w_first, 16)

    def gather(r):
        near, far = pair[r].astype(F32), across[r].astype(F32)
        wide = with_halo(own[r].astype(F32), jnp.where(even, far, near), jnp.where(even, near, far))
        coarse[r] = wide
        net[r + 1] = to_cells(lon_shifts(wide))

    each(ROWS, gather, CHUNK["gather"])

    n1, u1 = CHUNK["first"]

    def first(i):
        pre = mm(three_rows(net, n1 * i, n1), first_w)
        act = jax.nn.silu(pre).astype(BF).reshape(n1 // 2, 2, WIDE, HID1)
        hid[pl.ds((n1 // 2) * i, n1 // 2), 1] = act[:, 0]
        hid[pl.ds((n1 // 2) * i + 1, n1 // 2), 0] = act[:, 1]

    each(ROWS // n1, first, u1)
    fetch.wait()
    gap = jnp.zeros((HID1, HID1), BF)
    for b in range(3):
        taps_b = [w_near[a, b * HID1 : (b + 1) * HID1] for a in range(3)]
        pair_w[b, 0:HID1] = jnp.concatenate([*taps_b, gap], axis=1)
        pair_w[b, HID1:] = jnp.concatenate([gap, *taps_b], axis=1)
    n2, u2 = CHUNK["second"]

    def second(i):
        rows = [hid[pl.ds(n2 * i + j // 2, n2), j % 2].reshape(n2 * WIDE, HID1) for j in range(4)]
        quads = jnp.concatenate(rows, axis=1)
        parts = [mm_nt(quads, pair_w[b]).reshape(n2, WIDE, 2 * HID1) for b in range(3)]
        act = jax.nn.silu(ahead(parts[0], 1) + parts[1] + back(parts[2], 1)).astype(BF)
        for k in range(n2):
            row = 2 * (n2 * i + k)
            sec[row] = act[k, :, :HID1]
            sec[row + 1] = act[k, :, HID1:]

    each(LOW // n2, second, u2)
    last_w = stack_outputs(stack_o, w_last)[0:72]

    def mean_taps(r):
        taps[r + 1] = mm_nt(last_w, to_lanes(sec[r]))

    each(ROWS, mean_taps, CHUNK["taps"])

    def collect(r):
        mean[r] = four_channels(taps, r).astype(BF).astype(F32)

    each(ROWS, collect, CHUNK["taps"])


def step_kernel(
    scale,
    place,
    own,
    pair,
    across,
    mean,
    coarse,
    w_in,
    w_down,
    w_up,
    w_out,
    mine,
    other,
    tiles,
    *scratch,
):
    (
        stack,
        stack_o,
        field,
        net,
        act_c,
        taps,
        residuals,
        noisies,
        slope_a,
        act_a,
        pairs,
        pooled,
        act_b,
        slope_b,
        up_taps,
        phases,
        slope_c,
        grad_f,
        spread_f,
        back_c,
        grad_c,
        blocks,
        grad_b,
        grad_a,
        last_sum,
        den,
        halves,
        low_taps,
        sems,
    ) = scratch
    for ref in (net, pooled, up_taps, taps, grad_f, grad_c, grad_b, low_taps):
        zero_edges(ref)
    even = place[1] == 0
    in_w = stack_inputs(stack, w_in, FIELDS)
    lane = lax.broadcasted_iota(jnp.int32, (8, LANES), 1)
    held = (lane < OWN + HALO) | (lane >= LANES - HALO)
    low_half = lax.broadcasted_iota(jnp.int32, (8, LANES), 0) < 4

    def enter(r):
        near, far = pair[r], across[r]
        wide = with_halo(own[r], jnp.where(even, far, near), jnp.where(even, near, far))
        field[r] = wide[0:8]
        mean_r = mean[r]
        sigma = jnp.where(held, jnp.broadcast_to(wide[1:2], (8, LANES)), 1.0)
        residual = wide[0:8] - mean_r
        noisy = residual + sigma * wide[8:16]
        variance = sigma * sigma + 0.25
        residuals[r] = residual
        noisies[r] = noisy
        scaled = (lax.rsqrt(variance) * noisy).astype(BF).astype(F32)
        both = jnp.where(low_half, pltpu.roll(mean_r, 4, 0), scaled)
        net[r + 1] = to_cells(lon_shifts(jnp.concatenate([both, coarse[r]], axis=0)))

    each(ROWS, enter, CHUNK["enter"])

    n3, u3 = CHUNK["one"]

    def level_one(i):
        pre = mm(three_rows(net, n3 * i, n3), in_w)
        gate = jax.nn.sigmoid(pre)
        slope_a[pl.ds(n3 * i, n3)] = (gate * (1.0 + pre * (1.0 - gate))).reshape(n3, WIDE, HID1)
        act = (pre * gate).astype(BF).reshape(n3, WIDE, HID1)
        act_a[pl.ds(n3 * i, n3)] = act
        wide = act.astype(F32)
        for k in range(n3 // 2):
            row = (n3 // 2) * i + k
            pairs[row] = wide[2 * k] + wide[2 * k + 1]
            total = pairs[row, pl.ds(0, WLOW, stride=2)] + pairs[row, pl.ds(1, WLOW, stride=2)]
            pooled[row + 1] = (0.25 * total).astype(BF)

    each(ROWS // n3, level_one, u3)
    down_w = jnp.concatenate([w_down[a] for a in range(3)], axis=1)

    n4, u4 = CHUNK["two"]

    def level_two(i):
        pre = lon_sum(mm_nt(three_rows(pooled, n4 * i, n4), down_w), n4, WLOW, HID2)
        gate = jax.nn.sigmoid(pre)
        slope_b[pl.ds(n4 * i, n4)] = gate * (1.0 + pre * (1.0 - gate))
        act_b[pl.ds(n4 * i, n4)] = (pre * gate).astype(BF)

    each(LOW // n4, level_two, u4)
    n5, u5 = CHUNK["up"]

    def up_products(i):
        low = act_b[pl.ds(n5 * i, n5)].reshape(n5 * WLOW, HID2)
        up_taps[pl.ds(n5 * i + 1, n5)] = mm_nt(low, w_up[...]).reshape(n5, WLOW, 9 * HID1)

    each(LOW // n5, up_products, u5)

    def level_three(i):
        for pi in range(2):
            sums = []
            for b in range(3):
                total = None
                for a in range(3):
                    row = i + 1 + (pi + a - 1) // 2
                    at = (a * 3 + b) * HID1
                    part = up_taps[row, :, at : at + HID1]
                    total = part if total is None else total + part
                sums.append(total)
            row = 2 * i + pi
            phases[row, pl.ds(0, WLOW, stride=2)] = ahead(sums[0], 0) + sums[1] + sums[2]
            phases[row, pl.ds(1, WLOW, stride=2)] = sums[0] + sums[1] + back(sums[2], 0)
            pre = phases[row]
            gate = jax.nn.sigmoid(pre)
            act_c[row] = (pre * gate + act_a[row].astype(F32)).astype(BF)
            slope_c[row] = gate * (1.0 + pre * (1.0 - gate))

    each(LOW, level_three, CHUNK["three"])
    out_w = stack_outputs(stack_o, w_out)

    def field_taps(r):
        taps[r + 1] = mm_nt(out_w[0:72], to_lanes(act_c[r]))

    each(ROWS, field_taps, CHUNK["taps"])

    def loss(i):
        for k in range(2):
            r = 2 * i + k
            value = four_channels(taps, r)
            sigma = jnp.where(held, jnp.broadcast_to(field[r, 1:2], (8, LANES)), 1.0)
            weight = jnp.broadcast_to(field[r, 0:1], (8, LANES))
            variance = sigma * sigma + 0.25
            c_out = 0.5 * sigma * lax.rsqrt(variance)
            lam = variance / (0.25 * sigma * sigma)
            denoised = (0.25 / variance) * noisies[r] + c_out * value
            den[i, 4 * k : 4 * k + 4] = denoised[4:8, :OWN]
            loss_grad = (2.0 * scale) * weight * lam * (denoised - residuals[r])
            cot = (c_out * loss_grad).astype(BF).astype(F32)
            grad_f[r + 1] = jnp.where(low_half, 0.0, cot)

    each(LOW, loss, CHUNK["loss"])
    tiles[...] = den[...].astype(BF)
    last_sum[...] = jnp.zeros_like(last_sum)

    def last_grads(r):
        parts = []
        for a in range(3):
            cot = grad_f[r + 2 - a]
            parts += [back(cot, 1), cot, ahead(cot, 1)]
        cots = jnp.concatenate(parts + [jnp.zeros((8, LANES), F32)], axis=0)
        last_sum[...] += mm(cots[:, :OWN].astype(BF), act_c[r, 0:OWN])
        spread_f[r] = to_cells(cots)

    each(ROWS, last_grads, CHUNK["last"])
    near, far = 0, 1

    def keep(half, at, value):
        halves[half, at : at + value.shape[0]] = value.astype(BF)

    def send(half):
        for core, target in ((half, mine), (1 - half, other)):

            @pl.when(place[0] == core)
            def _():
                pltpu.make_async_copy(halves.at[half], target, sems.at[half]).start()

    keep(near, BIG_ROWS, last_sum[0:LAST_ROWS])
    keep(near, BIG_ROWS + LAST_ROWS, jnp.zeros((HALF_ROWS - BIG_ROWS - LAST_ROWS, OWN), F32))

    n6, u6 = CHUNK["back_three"]

    def back_three(i):
        wide = mm(spread_f[pl.ds(n6 * i, n6)].reshape(n6 * WIDE, OWN), out_w)
        wide = wide.reshape(n6, WIDE, HID1)
        back_c[pl.ds(n6 * i, n6)] = wide
        grad_c[pl.ds(n6 * i + 1, n6)] = wide * slope_c[pl.ds(n6 * i, n6)]

    each(ROWS // n6, back_three, u6)

    def block_sums(i):
        even = [grad_c[2 * i + k, pl.ds(0, WLOW, stride=2)] for k in range(4)]
        odd = [grad_c[2 * i + k, pl.ds(1, WLOW, stride=2)] for k in range(4)]
        for a in range(3):
            e, o = even[2 - a] + even[3 - a], odd[2 - a] + odd[3 - a]
            for b, total in enumerate((o + back(e, 0), e + o, ahead(o, 0) + e)):
                at = (a * 3 + b) * HID1
                blocks[i, :, at : at + HID1] = total.astype(BF)

    each(LOW, block_sums, CHUNK["blocks"])

    n7, u7 = CHUNK["back_two"]

    def back_two(i):
        low = mm(blocks[pl.ds(n7 * i, n7)].reshape(n7 * WLOW, 9 * HID1), w_up[...])
        cot = low.reshape(n7, WLOW, HID2) * slope_b[pl.ds(n7 * i, n7)]
        shifts = jnp.concatenate([back(cot, 1), cot, ahead(cot, 1)], axis=2)
        grad_b[pl.ds(n7 * i + 1, n7)] = shifts.astype(BF)

    each(LOW // n7, back_two, u7)
    held_low = OWN // 2
    cells = LOW * held_low
    low_b = act_b[:, :held_low].reshape(cells, HID2)
    for k in range(3):
        at = 3 * HID1 * k
        up = mm_tn(blocks[:, :held_low, at : at + 3 * HID1].reshape(cells, 3 * HID1), low_b)
        keep(near, at, up[:, :HID1])
        keep(near, at + UP_ROWS, up[:, HID1:])
    send(near)
    low_a = jnp.concatenate(
        [pooled[a : a + LOW, :held_low].reshape(cells, HID1) for a in range(3)], axis=1
    )
    for b in range(3):
        at = HID2 * b
        down = mm_tn(grad_b[1 : LOW + 1, :held_low, at : at + HID2].reshape(cells, HID2), low_a)
        for a in range(3):
            keep(far, (a * 3 + b) * HID2, down[:, HID1 * a : HID1 * (a + 1)])
    spread_w = jnp.concatenate([w_down[a] for a in range(3)], axis=1)
    wide = mm(grad_b[1 : LOW + 1, :held_low].reshape(cells, 3 * HID2), spread_w)
    low_taps[1 : LOW + 1] = wide.reshape(LOW, held_low, 3 * HID1)

    def back_one(i):
        low = (
            low_taps[i + 2, :, 0:HID1]
            + low_taps[i + 1, :, HID1 : 2 * HID1]
            + low_taps[i, :, 2 * HID1 :]
        )
        low = 0.25 * low
        phases[i, pl.ds(0, held_low, stride=2)] = low
        phases[i, pl.ds(1, held_low, stride=2)] = low
        spread = phases[i, 0:OWN]
        for pi in range(2):
            r = 2 * i + pi
            grad_a[r] = ((back_c[r, 0:OWN] + spread) * slope_a[r, 0:OWN]).astype(BF)

    each(LOW, back_one, CHUNK["back_one"])
    near_cells = jnp.concatenate(
        [net[a : a + ROWS, :OWN].reshape(ROWS * OWN, OWN) for a in range(3)], axis=1
    )
    inputs = mm_tn(grad_a[...].reshape(ROWS * OWN, HID1), near_cells)
    for a in range(3):
        part = inputs[:, a * OWN : (a + 1) * OWN].T
        keep(far, BIG_ROWS + a * 3 * FIELDS, part[: 3 * FIELDS])
    keep(far, BIG_ROWS + IN_ROWS, jnp.zeros((HALF_ROWS - BIG_ROWS - IN_ROWS, OWN), F32))
    send(far)
    for half in (near, far):
        pltpu.make_async_copy(halves.at[half], mine, sems.at[half]).wait()


def unpack_kernel(place, mine, other, seats, tile, first, down, up, last, downs, ups, firsts, lasts, tiles, sems):
    even = place[0] == 0

    def half(k, at, count):
        one, two = mine[pl.ds(at, count)], other[pl.ds(at, count)]
        return (jnp.where(even, one, two) if k == 0 else jnp.where(even, two, one)).astype(F32)

    def leave(a):
        return (
            pltpu.make_async_copy(ups.at[a], up.at[a], sems.at[0]),
            pltpu.make_async_copy(downs.at[a], down.at[a], sems.at[1]),
        )

    def thirds(a):
        at = pl.multiple_of(a * (3 * HID1), 3 * HID1)
        for k in range(2):
            piece = half(0, at + k * UP_ROWS, 3 * HID1)
            ups[a, :, :, k * HID1 : (k + 1) * HID1] = piece.reshape(3, HID1, HID1)
        downs[a] = half(1, 2 * at, 3 * HID2).reshape(3, HID2, HID1)
        for copy in leave(a):
            copy.start()

    each(3, thirds)
    inputs = half(1, BIG_ROWS, IN_ROWS)
    outputs = half(0, BIG_ROWS, 80)
    for a in range(3):
        for b in range(3):
            at = (a * 3 + b) * FIELDS
            firsts[a, b] = inputs[at : at + 20]
            at = (a * 3 + b) * 8 + 4
            lasts[a, b] = outputs[at : at + 4]
    small = [pltpu.make_async_copy(firsts, first, sems.at[2]), pltpu.make_async_copy(lasts, last, sems.at[3])]
    for copy in small:
        copy.start()
    blocks = seats[...].astype(F32)
    for k in range(8):
        for r in range(2):
            tiles[:, r, k * OWN : (k + 1) * OWN] = blocks[k, 4 * r : 4 * r + 4]
    small.append(pltpu.make_async_copy(tiles, tile, sems.at[4]))
    small[2].start()
    for copy in small:
        copy.wait()
    for a in range(3):
        for copy in leave(a):
            copy.wait()


def in_vmem(count):
    return [pl.BlockSpec(memory_space=pltpu.MemorySpace.VMEM) for _ in range(count)]


def in_hbm(count):
    return [pl.BlockSpec(memory_space=pltpu.MemorySpace.HBM) for _ in range(count)]


def in_smem():
    return pl.BlockSpec(memory_space=pltpu.MemorySpace.SMEM)


def pack(target, noise, land_mask, coarse, level_index):
    lats = target.shape[2] // OWN
    return pl.pallas_call(
        pack_kernel,
        out_shape=(
            jax.ShapeDtypeStruct((lats, 2, 16, OWN), F32),
            jax.ShapeDtypeStruct((ROWS, 16, OWN), BF),
        ),
        in_specs=[in_smem(), *in_hbm(4)],
        out_specs=tuple(in_vmem(2)),
        scratch_shapes=[
            pltpu.VMEM(target.shape, F32),
            pltpu.VMEM(noise.shape, F32),
            pltpu.VMEM(land_mask.shape, jnp.int32),
            pltpu.VMEM(coarse.shape, BF),
            pltpu.SemaphoreType.DMA((4,)),
        ],
        compiler_params=pltpu.CompilerParams(vmem_limit_bytes=8 * 2**20),
        name="pack",
    )(level_index, in_place(target), in_place(noise), in_place(land_mask), in_place(coarse))


def regress(*operands):
    return pl.pallas_call(
        regression_kernel,
        out_shape=(
            jax.ShapeDtypeStruct((ROWS, 8, LANES), F32),
            jax.ShapeDtypeStruct((ROWS, 16, LANES), F32),
        ),
        in_specs=[in_smem(), *in_vmem(4), *in_hbm(1), *in_vmem(1)],
        out_specs=tuple(in_vmem(2)),
        scratch_shapes=[
            pltpu.VMEM((3, OWN, OWN), F32),
            pltpu.VMEM((OWN, OWN), F32),
            pltpu.VMEM((ROWS + 2, WIDE, OWN), BF),
            pltpu.VMEM((LOW + 1, 2, WIDE, HID1), BF),
            pltpu.VMEM((ROWS, WIDE, HID1), BF),
            pltpu.VMEM((ROWS + 2, 72, LANES), F32),
            pltpu.VMEM((3, 3 * HID1, HID1), BF),
            pltpu.VMEM((3, 2 * HID1, 4 * HID1), BF),
            pltpu.SemaphoreType.DMA(()),
        ],
        compiler_params=pltpu.CompilerParams(vmem_limit_bytes=20 * 2**20),
        cost_estimate=pl.CostEstimate(flops=2 * 10**9, transcendentals=10**6, bytes_accessed=2 * 10**6),
        name="regress",
    )(*operands)


def step(scale, *operands):
    def kernel(*refs):
        step_kernel(scale, *refs)

    return pl.pallas_call(
        kernel,
        out_shape=(
            jax.ShapeDtypeStruct((HALF_ROWS, OWN), BF),
            jax.ShapeDtypeStruct((HALF_ROWS, OWN), BF),
            jax.ShapeDtypeStruct((LOW, CELL_ROWS, OWN), BF),
        ),
        in_specs=[in_smem(), *in_vmem(9)],
        out_specs=tuple(in_vmem(3)),
        scratch_shapes=[
            pltpu.VMEM((3, OWN, OWN), F32),
            pltpu.VMEM((OWN, OWN), F32),
            pltpu.VMEM((ROWS, 8, LANES), F32),
            pltpu.VMEM((ROWS + 2, WIDE, OWN), BF),
            pltpu.VMEM((ROWS, WIDE, HID1), BF),
            pltpu.VMEM((ROWS + 2, 72, LANES), F32),
            pltpu.VMEM((ROWS, 8, LANES), F32),
            pltpu.VMEM((ROWS, 8, LANES), F32),
            pltpu.VMEM((ROWS, WIDE, HID1), F32),
            pltpu.VMEM((ROWS, WIDE, HID1), BF),
            pltpu.VMEM((LOW, WIDE, HID1), F32),
            pltpu.VMEM((LOW + 2, WLOW, HID1), BF),
            pltpu.VMEM((LOW, WLOW, HID2), BF),
            pltpu.VMEM((LOW, WLOW, HID2), F32),
            pltpu.VMEM((LOW + 2, WLOW, 9 * HID1), F32),
            pltpu.VMEM((ROWS, WIDE, HID1), F32),
            pltpu.VMEM((ROWS, WIDE, HID1), F32),
            pltpu.VMEM((ROWS + 2, 8, LANES), F32),
            pltpu.VMEM((ROWS, WIDE, OWN), BF),
            pltpu.VMEM((ROWS, WIDE, HID1), F32),
            pltpu.VMEM((ROWS + 2, WIDE, HID1), F32),
            pltpu.VMEM((LOW, WLOW, 9 * HID1), BF),
            pltpu.VMEM((LOW + 2, WLOW, 3 * HID2), BF),
            pltpu.VMEM((ROWS, OWN, HID1), BF),
            pltpu.VMEM((80, HID1), F32),
            pltpu.VMEM((LOW, CELL_ROWS, OWN), F32),
            pltpu.VMEM((2, HALF_ROWS, OWN), BF),
            pltpu.VMEM((LOW + 2, OWN // 2, 3 * HID1), F32),
            pltpu.SemaphoreType.DMA((2,)),
        ],
        compiler_params=pltpu.CompilerParams(vmem_limit_bytes=44 * 2**20),
        name="step",
    )(*operands)


def unpack(place, mine, other, seats):
    outs = (
        (4, 2, 8 * OWN),
        (3, 3, 20, HID1),
        (3, 3, HID2, HID1),
        (3, 3, HID1, HID2),
        (3, 3, 4, HID1),
    )
    return pl.pallas_call(
        unpack_kernel,
        out_shape=tuple(jax.ShapeDtypeStruct(shape, F32) for shape in outs),
        in_specs=[in_smem(), *in_vmem(3)],
        out_specs=tuple([pl.BlockSpec(memory_space=pl.ANY)] * 5),
        scratch_shapes=[
            *(pltpu.VMEM(outs[k], F32) for k in (2, 3, 1, 4, 0)),
            pltpu.SemaphoreType.DMA((5,)),
        ],
        compiler_params=pltpu.CompilerParams(vmem_limit_bytes=16 * 2**20),
        name="unpack",
    )(place, mine, other, seats)


def all_to_all(value, axes):
    return lax.all_to_all(value, axes, split_axis=0, concat_axis=0, tiled=True)


def in_place(value):
    return pltpu.with_memory_space_constraint(value, pltpu.HBM)


def swap(value, axes, offset):
    count = lax.axis_size(axes)
    pairs = []
    for i in range(offset, count + offset, 2):
        here, there = i % count, (i + 1) % count
        pairs += [(here, there), (there, here)]
    return lax.ppermute(value, axes, sorted(set(pairs)))


def local(
    coarse,
    target,
    noise,
    land_mask,
    level_index,
    frozen_first,
    frozen_middle,
    frozen_last,
    diffuse_in,
    diffuse_down,
    diffuse_up,
    diffuse_out,
):
    scale = 1.0 / (target.shape[0] * math.sqrt(target.shape[1] * target.shape[2] * lax.axis_size(STRIPS)))
    place = jnp.stack([lax.axis_index("core"), lax.axis_index("z") % 2])
    place = place.astype(jnp.int32)
    packed, strip = pack(target, noise, land_mask, coarse, level_index)
    packed = all_to_all(packed, LAT).reshape(ROWS, 16, OWN)
    strip_across = swap(strip, STRIPS, 1)
    strip_pair = swap(strip, STRIPS, 0)
    across = swap(packed, STRIPS, 1)
    pair = swap(packed, STRIPS, 0)
    mean, coarse_wide = regress(
        place,
        strip,
        strip_pair,
        strip_across,
        in_place(frozen_first.transpose(0, 1, 3, 2)),
        in_place(frozen_middle.reshape(3, 3 * HID1, HID1)),
        in_place(frozen_last),
    )
    grads, partner, tiles = step(
        scale,
        place,
        packed,
        pair,
        across,
        mean,
        coarse_wide,
        diffuse_in.transpose(0, 1, 3, 2),
        diffuse_down.reshape(3, 3 * HID2, HID1),
        diffuse_up.reshape(9 * HID1, HID2),
        diffuse_out,
    )
    chips = lax.axis_size(CHIPS)
    rows = HALF_ROWS // chips
    lats = tiles.shape[0]
    half = grads.astype(F32) + swap(partner, "core", 0).astype(F32)
    blocks = jnp.broadcast_to(tiles[None], (chips // lats, *tiles.shape)).reshape(chips, CELL_ROWS, OWN)
    sent = jnp.concatenate([half.astype(BF).reshape(chips, rows, OWN), blocks], axis=1)
    parts = all_to_all(sent, CHIPS)
    total = parts[:, :rows].astype(F32).sum(0).astype(BF)
    seats = parts.reshape(chips // lats, lats, rows + CELL_ROWS, OWN)[:, :, rows:]
    seats = lax.dynamic_index_in_dim(seats, lax.axis_index(("y", "x_hi")), 0, False)
    mine = all_to_all(jnp.broadcast_to(total[None], (chips, rows, OWN)), CHIPS).reshape(HALF_ROWS, OWN)
    tile, first, down, up, last = unpack(place, mine, swap(mine, "core", 0), seats)
    return (tile, first.transpose(0, 1, 3, 2), down, up, last)


def solution(mesh):
    fine = Mesh(mesh.devices.reshape(4, 2, 2, 2, 4), LON + LAT)
    tile = P(None, LAT, LON)
    return jax.shard_map(
        local,
        mesh=fine,
        in_specs=(
            P(None, None, STRIPS),
            tile,
            tile,
            P(LAT, LON),
            P(LAT, LON),
            *([P()] * 7),
        ),
        out_specs=(tile, P(), P(), P(), P()),
        check_vma=False,
    )
```

```python
import math

import jax
import jax.numpy as jnp
from jax import lax
from jax.experimental import pallas as pl
from jax.experimental.pallas import tpu as pltpu
from jax.sharding import Mesh
from jax.sharding import PartitionSpec as P


LEVELS = 32
ROWS = 16
LOW = ROWS // 2
OWN = 128
HALO = 16
WIDE = OWN + 2 * HALO
WLOW = WIDE // 2
LANES = 256
HID1 = 128
HID2 = 256
BF = jnp.bfloat16
F32 = jnp.float32

LON = ("y", "x_hi", "core")
LAT = ("x_lo", "z")
CHIPS = ("y", "x_hi", "x_lo", "z")
STRIPS = LON + LAT

FIELDS = 24
UP_ROWS = 9 * HID1
BIG_ROWS = 2304
LAST_ROWS = 72
IN_ROWS = 9 * FIELDS
HALF_ROWS = 2560
CELL_ROWS = 8
CHUNK = {
    "gather": 8,
    "first": (8, 2),
    "second": (4, 2),
    "taps": 8,
    "enter": 16,
    "one": (8, 2),
    "two": (2, 4),
    "up": (4, 2),
    "three": 2,
    "loss": 8,
    "last": 16,
    "back_three": (16, 1),
    "blocks": 8,
    "back_two": (4, 2),
    "back_one": 4,
}


def mm(x, w):
    return lax.dot_general(x, w, (((1,), (0,)), ((), ())), preferred_element_type=F32)


def mm_nt(x, w):
    return lax.dot_general(x, w, (((1,), (1,)), ((), ())), preferred_element_type=F32)


def mm_tn(x, w):
    return lax.dot_general(x, w, (((0,), (0,)), ((), ())), preferred_element_type=F32)


def back(x, axis):
    return pltpu.roll(x, x.shape[axis] - 1, axis)


def ahead(x, axis):
    return pltpu.roll(x, 1, axis)


def with_halo(own, left, right):
    lane = lax.broadcasted_iota(jnp.int32, own.shape, 1)
    halo = jnp.where(lane < HALO, right, jnp.where(lane >= OWN - HALO, left, 0.0))
    return jnp.concatenate([own, halo], axis=1)


def to_cells(stack):
    pad = OWN - stack.shape[0]
    if pad:
        stack = jnp.concatenate([stack, jnp.zeros((pad, LANES), F32)], axis=0)
    cells = stack.T
    return jnp.concatenate([cells[: OWN + HALO], cells[LANES - HALO :]], axis=0).astype(BF)


def to_lanes(cells):
    gap = jnp.zeros((LANES - WIDE, cells.shape[1]), cells.dtype)
    return jnp.concatenate([cells[: OWN + HALO], gap, cells[OWN + HALO :]], axis=0)


def lon_shifts(field):
    return jnp.concatenate([ahead(field, 1), field, back(field, 1)], axis=0)


def three_rows(ref, start, count):
    width = ref.shape[1]
    return jnp.concatenate(
        [ref[pl.ds(start + a, count)].reshape(count * width, ref.shape[2]) for a in range(3)], axis=1
    )


def lon_sum(taps, count, width, out):
    first, second, third = (
        taps[:, b * out : (b + 1) * out].reshape(count, width, out) for b in range(3)
    )
    return ahead(first, 1) + second + back(third, 1)


def four_channels(ref, row):
    sums = []
    for b in range(3):
        at = [(a * 3 + b) * 8 for a in range(3)]
        sums.append(
            ref[row, at[0] : at[0] + 8]
            + ref[row + 1, at[1] : at[1] + 8]
            + ref[row + 2, at[2] : at[2] + 8]
        )
    return ahead(sums[0], 1) + sums[1] + back(sums[2], 1)


def zero_edges(ref):
    edge = jnp.zeros(ref.shape[1:], ref.dtype)
    ref[0] = edge
    ref[ref.shape[0] - 1] = edge


def each(count, body, unroll=1):
    def step(i, carry):
        body(i)
        return carry

    lax.fori_loop(0, count, step, 0, unroll=unroll)


def pack_kernel(
    level, target_far, noise_far, mask_far, coarse_far, packed, strip, target, noise, land_mask, coarse, sems
):
    arrive = [
        pltpu.make_async_copy(target_far, target, sems.at[0]),
        pltpu.make_async_copy(noise_far, noise, sems.at[1]),
        pltpu.make_async_copy(mask_far, land_mask, sems.at[2]),
        pltpu.make_async_copy(coarse_far, coarse, sems.at[3]),
    ]
    for copy in arrive:
        copy.start()
    power = jnp.full((1, OWN), level[0, 0], jnp.int32).astype(F32) / (LEVELS - 1)
    sigma = 0.02 * jnp.exp(power * math.log(4000.0))
    for copy in arrive:
        copy.wait()
    weight = 1.0 + land_mask[...].astype(F32)
    for p in range(packed.shape[0]):
        lanes = slice(p * OWN, (p + 1) * OWN)
        for r in range(2):
            packed[p, r, 0:1] = weight[r : r + 1, lanes]
            packed[p, r, 1:2] = sigma
            packed[p, r, 2:4] = jnp.zeros((2, OWN), F32)
            packed[p, r, 4:8] = target[:, r, lanes]
            packed[p, r, 8:12] = jnp.zeros((4, OWN), F32)
            packed[p, r, 12:16] = noise[:, r, lanes]
    rows = jnp.transpose(coarse[...].astype(F32), (1, 0, 2))
    strip[...] = jnp.concatenate([rows, jnp.zeros((ROWS, 4, OWN), F32)], axis=1).astype(BF)


def stack_inputs(ref, weight, room):
    ref[...] = jnp.zeros_like(ref)
    count = weight.shape[2]
    for a in range(3):
        for b in range(3):
            ref[a, b * room : b * room + count] = weight[a, b].astype(F32)
    return ref[...].astype(BF).reshape(3 * OWN, OWN)


def stack_outputs(ref, weight):
    ref[...] = jnp.zeros_like(ref)
    for a in range(3):
        for b in range(3):
            at = (a * 3 + b) * 8 + 4
            ref[at : at + 4] = weight[a, b].astype(F32)
    return ref[...].astype(BF)


def regression_kernel(
    place,
    own,
    pair,
    across,
    w_first,
    w_middle,
    w_last,
    mean,
    coarse,
    stack,
    stack_o,
    net,
    hid,
    sec,
    taps,
    w_near,
    pair_w,
    sem,
):
    zero_edges(net)
    zero_edges(taps)
    hid[0, 0] = jnp.zeros((WIDE, HID1), BF)
    hid[LOW, 1] = jnp.zeros((WIDE, HID1), BF)
    even = place[1] == 0
    fetch = pltpu.make_async_copy(w_middle, w_near, sem)
    fetch.start()
    first_w = stack_inputs(stack, w_first, 16)

    def gather(r):
        near, far = pair[r].astype(F32), across[r].astype(F32)
        wide = with_halo(own[r].astype(F32), jnp.where(even, far, near), jnp.where(even, near, far))
        coarse[r] = wide
        net[r + 1] = to_cells(lon_shifts(wide))

    each(ROWS, gather, CHUNK["gather"])

    n1, u1 = CHUNK["first"]

    def first(i):
        pre = mm(three_rows(net, n1 * i, n1), first_w)
        act = jax.nn.silu(pre).astype(BF).reshape(n1 // 2, 2, WIDE, HID1)
        hid[pl.ds((n1 // 2) * i, n1 // 2), 1] = act[:, 0]
        hid[pl.ds((n1 // 2) * i + 1, n1 // 2), 0] = act[:, 1]

    each(ROWS // n1, first, u1)
    fetch.wait()
    gap = jnp.zeros((HID1, HID1), BF)
    for b in range(3):
        taps_b = [w_near[a, b * HID1 : (b + 1) * HID1] for a in range(3)]
        pair_w[b, 0:HID1] = jnp.concatenate([*taps_b, gap], axis=1)
        pair_w[b, HID1:] = jnp.concatenate([gap, *taps_b], axis=1)
    n2, u2 = CHUNK["second"]

    def second(i):
        rows = [hid[pl.ds(n2 * i + j // 2, n2), j % 2].reshape(n2 * WIDE, HID1) for j in range(4)]
        quads = jnp.concatenate(rows, axis=1)
        parts = [mm_nt(quads, pair_w[b]).reshape(n2, WIDE, 2 * HID1) for b in range(3)]
        act = jax.nn.silu(ahead(parts[0], 1) + parts[1] + back(parts[2], 1)).astype(BF)
        for k in range(n2):
            row = 2 * (n2 * i + k)
            sec[row] = act[k, :, :HID1]
            sec[row + 1] = act[k, :, HID1:]

    each(LOW // n2, second, u2)
    last_w = stack_outputs(stack_o, w_last)[0:72]

    def mean_taps(r):
        taps[r + 1] = mm_nt(last_w, to_lanes(sec[r]))

    each(ROWS, mean_taps, CHUNK["taps"])

    def collect(r):
        mean[r] = four_channels(taps, r).astype(BF).astype(F32)

    each(ROWS, collect, CHUNK["taps"])


def step_kernel(
    scale,
    place,
    own,
    pair,
    across,
    mean,
    coarse,
    w_in,
    w_down,
    w_up,
    w_out,
    mine,
    other,
    tiles,
    *scratch,
):
    (
        stack,
        stack_o,
        field,
        net,
        act_c,
        taps,
        residuals,
        noisies,
        slope_a,
        act_a,
        pairs,
        pooled,
        act_b,
        slope_b,
        up_taps,
        phases,
        slope_c,
        grad_f,
        spread_f,
        back_c,
        grad_c,
        blocks,
        grad_b,
        grad_a,
        last_sum,
        den,
        halves,
        low_taps,
        sems,
    ) = scratch
    for ref in (net, pooled, up_taps, taps, grad_f, grad_c, grad_b, low_taps):
        zero_edges(ref)
    even = place[1] == 0
    in_w = stack_inputs(stack, w_in, FIELDS)
    lane = lax.broadcasted_iota(jnp.int32, (8, LANES), 1)
    held = (lane < OWN + HALO) | (lane >= LANES - HALO)
    low_half = lax.broadcasted_iota(jnp.int32, (8, LANES), 0) < 4

    def enter(r):
        near, far = pair[r], across[r]
        wide = with_halo(own[r], jnp.where(even, far, near), jnp.where(even, near, far))
        field[r] = wide[0:8]
        mean_r = mean[r]
        sigma = jnp.where(held, jnp.broadcast_to(wide[1:2], (8, LANES)), 1.0)
        residual = wide[0:8] - mean_r
        noisy = residual + sigma * wide[8:16]
        variance = sigma * sigma + 0.25
        residuals[r] = residual
        noisies[r] = noisy
        scaled = (lax.rsqrt(variance) * noisy).astype(BF).astype(F32)
        both = jnp.where(low_half, pltpu.roll(mean_r, 4, 0), scaled)
        net[r + 1] = to_cells(lon_shifts(jnp.concatenate([both, coarse[r]], axis=0)))

    each(ROWS, enter, CHUNK["enter"])

    n3, u3 = CHUNK["one"]

    def level_one(i):
        pre = mm(three_rows(net, n3 * i, n3), in_w)
        gate = jax.nn.sigmoid(pre)
        slope_a[pl.ds(n3 * i, n3)] = (gate * (1.0 + pre * (1.0 - gate))).reshape(n3, WIDE, HID1)
        act = (pre * gate).astype(BF).reshape(n3, WIDE, HID1)
        act_a[pl.ds(n3 * i, n3)] = act
        wide = act.astype(F32)
        for k in range(n3 // 2):
            row = (n3 // 2) * i + k
            pairs[row] = wide[2 * k] + wide[2 * k + 1]
            total = pairs[row, pl.ds(0, WLOW, stride=2)] + pairs[row, pl.ds(1, WLOW, stride=2)]
            pooled[row + 1] = (0.25 * total).astype(BF)

    each(ROWS // n3, level_one, u3)
    down_w = jnp.concatenate([w_down[a] for a in range(3)], axis=1)

    n4, u4 = CHUNK["two"]

    def level_two(i):
        pre = lon_sum(mm_nt(three_rows(pooled, n4 * i, n4), down_w), n4, WLOW, HID2)
        gate = jax.nn.sigmoid(pre)
        slope_b[pl.ds(n4 * i, n4)] = gate * (1.0 + pre * (1.0 - gate))
        act_b[pl.ds(n4 * i, n4)] = (pre * gate).astype(BF)

    each(LOW // n4, level_two, u4)
    n5, u5 = CHUNK["up"]

    def up_products(i):
        low = act_b[pl.ds(n5 * i, n5)].reshape(n5 * WLOW, HID2)
        up_taps[pl.ds(n5 * i + 1, n5)] = mm_nt(low, w_up[...]).reshape(n5, WLOW, 9 * HID1)

    each(LOW // n5, up_products, u5)

    def level_three(i):
        for pi in range(2):
            sums = []
            for b in range(3):
                total = None
                for a in range(3):
                    row = i + 1 + (pi + a - 1) // 2
                    at = (a * 3 + b) * HID1
                    part = up_taps[row, :, at : at + HID1]
                    total = part if total is None else total + part
                sums.append(total)
            row = 2 * i + pi
            phases[row, pl.ds(0, WLOW, stride=2)] = ahead(sums[0], 0) + sums[1] + sums[2]
            phases[row, pl.ds(1, WLOW, stride=2)] = sums[0] + sums[1] + back(sums[2], 0)
            pre = phases[row]
            gate = jax.nn.sigmoid(pre)
            act_c[row] = (pre * gate + act_a[row].astype(F32)).astype(BF)
            slope_c[row] = gate * (1.0 + pre * (1.0 - gate))

    each(LOW, level_three, CHUNK["three"])
    out_w = stack_outputs(stack_o, w_out)

    def field_taps(r):
        taps[r + 1] = mm_nt(out_w[0:72], to_lanes(act_c[r]))

    each(ROWS, field_taps, CHUNK["taps"])

    def loss(i):
        for k in range(2):
            r = 2 * i + k
            value = four_channels(taps, r)
            sigma = jnp.where(held, jnp.broadcast_to(field[r, 1:2], (8, LANES)), 1.0)
            weight = jnp.broadcast_to(field[r, 0:1], (8, LANES))
            variance = sigma * sigma + 0.25
            c_out = 0.5 * sigma * lax.rsqrt(variance)
            lam = variance / (0.25 * sigma * sigma)
            denoised = (0.25 / variance) * noisies[r] + c_out * value
            den[i, 4 * k : 4 * k + 4] = denoised[4:8, :OWN]
            loss_grad = (2.0 * scale) * weight * lam * (denoised - residuals[r])
            cot = (c_out * loss_grad).astype(BF).astype(F32)
            grad_f[r + 1] = jnp.where(low_half, 0.0, cot)

    each(LOW, loss, CHUNK["loss"])
    tiles[...] = den[...].astype(BF)
    last_sum[...] = jnp.zeros_like(last_sum)

    def last_grads(r):
        parts = []
        for a in range(3):
            cot = grad_f[r + 2 - a]
            parts += [back(cot, 1), cot, ahead(cot, 1)]
        cots = jnp.concatenate(parts + [jnp.zeros((8, LANES), F32)], axis=0)
        last_sum[...] += mm(cots[:, :OWN].astype(BF), act_c[r, 0:OWN])
        spread_f[r] = to_cells(cots)

    each(ROWS, last_grads, CHUNK["last"])
    near, far = 0, 1

    def keep(half, at, value):
        halves[half, at : at + value.shape[0]] = value.astype(BF)

    def send(half):
        for core, target in ((half, mine), (1 - half, other)):

            @pl.when(place[0] == core)
            def _():
                pltpu.make_async_copy(halves.at[half], target, sems.at[half]).start()

    keep(near, BIG_ROWS, last_sum[0:LAST_ROWS])
    keep(near, BIG_ROWS + LAST_ROWS, jnp.zeros((HALF_ROWS - BIG_ROWS - LAST_ROWS, OWN), F32))

    n6, u6 = CHUNK["back_three"]

    def back_three(i):
        wide = mm(spread_f[pl.ds(n6 * i, n6)].reshape(n6 * WIDE, OWN), out_w)
        wide = wide.reshape(n6, WIDE, HID1)
        back_c[pl.ds(n6 * i, n6)] = wide
        grad_c[pl.ds(n6 * i + 1, n6)] = wide * slope_c[pl.ds(n6 * i, n6)]

    each(ROWS // n6, back_three, u6)

    def block_sums(i):
        even = [grad_c[2 * i + k, pl.ds(0, WLOW, stride=2)] for k in range(4)]
        odd = [grad_c[2 * i + k, pl.ds(1, WLOW, stride=2)] for k in range(4)]
        for a in range(3):
            e, o = even[2 - a] + even[3 - a], odd[2 - a] + odd[3 - a]
            for b, total in enumerate((o + back(e, 0), e + o, ahead(o, 0) + e)):
                at = (a * 3 + b) * HID1
                blocks[i, :, at : at + HID1] = total.astype(BF)

    each(LOW, block_sums, CHUNK["blocks"])

    n7, u7 = CHUNK["back_two"]

    def back_two(i):
        low = mm(blocks[pl.ds(n7 * i, n7)].reshape(n7 * WLOW, 9 * HID1), w_up[...])
        cot = low.reshape(n7, WLOW, HID2) * slope_b[pl.ds(n7 * i, n7)]
        shifts = jnp.concatenate([back(cot, 1), cot, ahead(cot, 1)], axis=2)
        grad_b[pl.ds(n7 * i + 1, n7)] = shifts.astype(BF)

    each(LOW // n7, back_two, u7)
    held_low = OWN // 2
    cells = LOW * held_low
    low_b = act_b[:, :held_low].reshape(cells, HID2)
    for k in range(3):
        at = 3 * HID1 * k
        up = mm_tn(blocks[:, :held_low, at : at + 3 * HID1].reshape(cells, 3 * HID1), low_b)
        keep(near, at, up[:, :HID1])
        keep(near, at + UP_ROWS, up[:, HID1:])
    send(near)
    low_a = jnp.concatenate(
        [pooled[a : a + LOW, :held_low].reshape(cells, HID1) for a in range(3)], axis=1
    )
    for b in range(3):
        at = HID2 * b
        down = mm_tn(grad_b[1 : LOW + 1, :held_low, at : at + HID2].reshape(cells, HID2), low_a)
        for a in range(3):
            keep(far, (a * 3 + b) * HID2, down[:, HID1 * a : HID1 * (a + 1)])
    spread_w = jnp.concatenate([w_down[a] for a in range(3)], axis=1)
    wide = mm(grad_b[1 : LOW + 1, :held_low].reshape(cells, 3 * HID2), spread_w)
    low_taps[1 : LOW + 1] = wide.reshape(LOW, held_low, 3 * HID1)

    def back_one(i):
        low = (
            low_taps[i + 2, :, 0:HID1]
            + low_taps[i + 1, :, HID1 : 2 * HID1]
            + low_taps[i, :, 2 * HID1 :]
        )
        low = 0.25 * low
        phases[i, pl.ds(0, held_low, stride=2)] = low
        phases[i, pl.ds(1, held_low, stride=2)] = low
        spread = phases[i, 0:OWN]
        for pi in range(2):
            r = 2 * i + pi
            grad_a[r] = ((back_c[r, 0:OWN] + spread) * slope_a[r, 0:OWN]).astype(BF)

    each(LOW, back_one, CHUNK["back_one"])
    near_cells = jnp.concatenate(
        [net[a : a + ROWS, :OWN].reshape(ROWS * OWN, OWN) for a in range(3)], axis=1
    )
    inputs = mm_tn(grad_a[...].reshape(ROWS * OWN, HID1), near_cells)
    for a in range(3):
        part = inputs[:, a * OWN : (a + 1) * OWN].T
        keep(far, BIG_ROWS + a * 3 * FIELDS, part[: 3 * FIELDS])
    keep(far, BIG_ROWS + IN_ROWS, jnp.zeros((HALF_ROWS - BIG_ROWS - IN_ROWS, OWN), F32))
    send(far)
    for half in (near, far):
        pltpu.make_async_copy(halves.at[half], mine, sems.at[half]).wait()


def unpack_kernel(place, mine, other, seats, tile, first, down, up, last, downs, ups, firsts, lasts, tiles, sems):
    even = place[0] == 0

    def half(k, at, count):
        one, two = mine[pl.ds(at, count)], other[pl.ds(at, count)]
        return (jnp.where(even, one, two) if k == 0 else jnp.where(even, two, one)).astype(F32)

    def leave(a):
        return (
            pltpu.make_async_copy(ups.at[a], up.at[a], sems.at[0]),
            pltpu.make_async_copy(downs.at[a], down.at[a], sems.at[1]),
        )

    def thirds(a):
        at = pl.multiple_of(a * (3 * HID1), 3 * HID1)
        for k in range(2):
            piece = half(0, at + k * UP_ROWS, 3 * HID1)
            ups[a, :, :, k * HID1 : (k + 1) * HID1] = piece.reshape(3, HID1, HID1)
        downs[a] = half(1, 2 * at, 3 * HID2).reshape(3, HID2, HID1)
        for copy in leave(a):
            copy.start()

    each(3, thirds)
    inputs = half(1, BIG_ROWS, IN_ROWS)
    outputs = half(0, BIG_ROWS, 80)
    for a in range(3):
        for b in range(3):
            at = (a * 3 + b) * FIELDS
            firsts[a, b] = inputs[at : at + 20]
            at = (a * 3 + b) * 8 + 4
            lasts[a, b] = outputs[at : at + 4]
    small = [pltpu.make_async_copy(firsts, first, sems.at[2]), pltpu.make_async_copy(lasts, last, sems.at[3])]
    for copy in small:
        copy.start()
    blocks = seats[...].astype(F32)
    for k in range(8):
        for r in range(2):
            tiles[:, r, k * OWN : (k + 1) * OWN] = blocks[k, 4 * r : 4 * r + 4]
    small.append(pltpu.make_async_copy(tiles, tile, sems.at[4]))
    small[2].start()
    for copy in small:
        copy.wait()
    for a in range(3):
        for copy in leave(a):
            copy.wait()


def in_vmem(count):
    return [pl.BlockSpec(memory_space=pltpu.MemorySpace.VMEM) for _ in range(count)]


def in_hbm(count):
    return [pl.BlockSpec(memory_space=pltpu.MemorySpace.HBM) for _ in range(count)]


def in_smem():
    return pl.BlockSpec(memory_space=pltpu.MemorySpace.SMEM)


def pack(target, noise, land_mask, coarse, level_index):
    lats = target.shape[2] // OWN
    return pl.pallas_call(
        pack_kernel,
        out_shape=(
            jax.ShapeDtypeStruct((lats, 2, 16, OWN), F32),
            jax.ShapeDtypeStruct((ROWS, 16, OWN), BF),
        ),
        in_specs=[in_smem(), *in_hbm(4)],
        out_specs=tuple(in_vmem(2)),
        scratch_shapes=[
            pltpu.VMEM(target.shape, F32),
            pltpu.VMEM(noise.shape, F32),
            pltpu.VMEM(land_mask.shape, jnp.int32),
            pltpu.VMEM(coarse.shape, BF),
            pltpu.SemaphoreType.DMA((4,)),
        ],
        compiler_params=pltpu.CompilerParams(vmem_limit_bytes=8 * 2**20),
        name="pack",
    )(level_index, in_place(target), in_place(noise), in_place(land_mask), in_place(coarse))


def regress(*operands):
    return pl.pallas_call(
        regression_kernel,
        out_shape=(
            jax.ShapeDtypeStruct((ROWS, 8, LANES), F32),
            jax.ShapeDtypeStruct((ROWS, 16, LANES), F32),
        ),
        in_specs=[in_smem(), *in_vmem(4), *in_hbm(1), *in_vmem(1)],
        out_specs=tuple(in_vmem(2)),
        scratch_shapes=[
            pltpu.VMEM((3, OWN, OWN), F32),
            pltpu.VMEM((OWN, OWN), F32),
            pltpu.VMEM((ROWS + 2, WIDE, OWN), BF),
            pltpu.VMEM((LOW + 1, 2, WIDE, HID1), BF),
            pltpu.VMEM((ROWS, WIDE, HID1), BF),
            pltpu.VMEM((ROWS + 2, 72, LANES), F32),
            pltpu.VMEM((3, 3 * HID1, HID1), BF),
            pltpu.VMEM((3, 2 * HID1, 4 * HID1), BF),
            pltpu.SemaphoreType.DMA(()),
        ],
        compiler_params=pltpu.CompilerParams(vmem_limit_bytes=20 * 2**20),
        cost_estimate=pl.CostEstimate(flops=2 * 10**9, transcendentals=10**6, bytes_accessed=2 * 10**6),
        name="regress",
    )(*operands)


def step(scale, *operands):
    def kernel(*refs):
        step_kernel(scale, *refs)

    return pl.pallas_call(
        kernel,
        out_shape=(
            jax.ShapeDtypeStruct((HALF_ROWS, OWN), BF),
            jax.ShapeDtypeStruct((HALF_ROWS, OWN), BF),
            jax.ShapeDtypeStruct((LOW, CELL_ROWS, OWN), BF),
        ),
        in_specs=[in_smem(), *in_vmem(9)],
        out_specs=tuple(in_vmem(3)),
        scratch_shapes=[
            pltpu.VMEM((3, OWN, OWN), F32),
            pltpu.VMEM((OWN, OWN), F32),
            pltpu.VMEM((ROWS, 8, LANES), F32),
            pltpu.VMEM((ROWS + 2, WIDE, OWN), BF),
            pltpu.VMEM((ROWS, WIDE, HID1), BF),
            pltpu.VMEM((ROWS + 2, 72, LANES), F32),
            pltpu.VMEM((ROWS, 8, LANES), F32),
            pltpu.VMEM((ROWS, 8, LANES), F32),
            pltpu.VMEM((ROWS, WIDE, HID1), F32),
            pltpu.VMEM((ROWS, WIDE, HID1), BF),
            pltpu.VMEM((LOW, WIDE, HID1), F32),
            pltpu.VMEM((LOW + 2, WLOW, HID1), BF),
            pltpu.VMEM((LOW, WLOW, HID2), BF),
            pltpu.VMEM((LOW, WLOW, HID2), F32),
            pltpu.VMEM((LOW + 2, WLOW, 9 * HID1), F32),
            pltpu.VMEM((ROWS, WIDE, HID1), F32),
            pltpu.VMEM((ROWS, WIDE, HID1), F32),
            pltpu.VMEM((ROWS + 2, 8, LANES), F32),
            pltpu.VMEM((ROWS, WIDE, OWN), BF),
            pltpu.VMEM((ROWS, WIDE, HID1), F32),
            pltpu.VMEM((ROWS + 2, WIDE, HID1), F32),
            pltpu.VMEM((LOW, WLOW, 9 * HID1), BF),
            pltpu.VMEM((LOW + 2, WLOW, 3 * HID2), BF),
            pltpu.VMEM((ROWS, OWN, HID1), BF),
            pltpu.VMEM((80, HID1), F32),
            pltpu.VMEM((LOW, CELL_ROWS, OWN), F32),
            pltpu.VMEM((2, HALF_ROWS, OWN), BF),
            pltpu.VMEM((LOW + 2, OWN // 2, 3 * HID1), F32),
            pltpu.SemaphoreType.DMA((2,)),
        ],
        compiler_params=pltpu.CompilerParams(vmem_limit_bytes=44 * 2**20),
        name="step",
    )(*operands)


def unpack(place, mine, other, seats):
    outs = (
        (4, 2, 8 * OWN),
        (3, 3, 20, HID1),
        (3, 3, HID2, HID1),
        (3, 3, HID1, HID2),
        (3, 3, 4, HID1),
    )
    return pl.pallas_call(
        unpack_kernel,
        out_shape=tuple(jax.ShapeDtypeStruct(shape, F32) for shape in outs),
        in_specs=[in_smem(), *in_vmem(3)],
        out_specs=tuple([pl.BlockSpec(memory_space=pl.ANY)] * 5),
        scratch_shapes=[
            *(pltpu.VMEM(outs[k], F32) for k in (2, 3, 1, 4, 0)),
            pltpu.SemaphoreType.DMA((5,)),
        ],
        compiler_params=pltpu.CompilerParams(vmem_limit_bytes=16 * 2**20),
        name="unpack",
    )(place, mine, other, seats)


def all_to_all(value, axes):
    return lax.all_to_all(value, axes, split_axis=0, concat_axis=0, tiled=True)


def in_place(value):
    return pltpu.with_memory_space_constraint(value, pltpu.HBM)


def swap(value, axes, offset):
    count = lax.axis_size(axes)
    pairs = []
    for i in range(offset, count + offset, 2):
        here, there = i % count, (i + 1) % count
        pairs += [(here, there), (there, here)]
    return lax.ppermute(value, axes, sorted(set(pairs)))


def local(
    coarse,
    target,
    noise,
    land_mask,
    level_index,
    frozen_first,
    frozen_middle,
    frozen_last,
    diffuse_in,
    diffuse_down,
    diffuse_up,
    diffuse_out,
):
    scale = 1.0 / (target.shape[0] * math.sqrt(target.shape[1] * target.shape[2] * lax.axis_size(STRIPS)))
    place = jnp.stack([lax.axis_index("core"), lax.axis_index("z") % 2])
    place = place.astype(jnp.int32)
    packed, strip = pack(target, noise, land_mask, coarse, level_index)
    packed = all_to_all(packed, LAT).reshape(ROWS, 16, OWN)
    strip_across = swap(strip, STRIPS, 1)
    strip_pair = swap(strip, STRIPS, 0)
    across = swap(packed, STRIPS, 1)
    pair = swap(packed, STRIPS, 0)
    mean, coarse_wide = regress(
        place,
        strip,
        strip_pair,
        strip_across,
        in_place(frozen_first.transpose(0, 1, 3, 2)),
        in_place(frozen_middle.reshape(3, 3 * HID1, HID1)),
        in_place(frozen_last),
    )
    grads, partner, tiles = step(
        scale,
        place,
        packed,
        pair,
        across,
        mean,
        coarse_wide,
        diffuse_in.transpose(0, 1, 3, 2),
        diffuse_down.reshape(3, 3 * HID2, HID1),
        diffuse_up.reshape(9 * HID1, HID2),
        diffuse_out,
    )
    chips = lax.axis_size(CHIPS)
    rows = HALF_ROWS // chips
    lats = tiles.shape[0]
    half = grads.astype(F32) + swap(partner, "core", 0).astype(F32)
    blocks = jnp.broadcast_to(tiles[None], (chips // lats, *tiles.shape)).reshape(chips, CELL_ROWS, OWN)
    sent = jnp.concatenate([half.astype(BF).reshape(chips, rows, OWN), blocks], axis=1)
    parts = all_to_all(sent, CHIPS)
    total = parts[:, :rows].astype(F32).sum(0).astype(BF)
    seats = parts.reshape(chips // lats, lats, rows + CELL_ROWS, OWN)[:, :, rows:]
    seats = lax.dynamic_index_in_dim(seats, lax.axis_index(("y", "x_hi")), 0, False)
    mine = all_to_all(jnp.broadcast_to(total[None], (chips, rows, OWN)), CHIPS).reshape(HALF_ROWS, OWN)
    tile, first, down, up, last = unpack(place, mine, swap(mine, "core", 0), seats)
    return (tile, first.transpose(0, 1, 3, 2), down, up, last)


def solution(mesh):
    fine = Mesh(mesh.devices.reshape(4, 2, 2, 2, 4), LON + LAT)
    tile = P(None, LAT, LON)
    return jax.shard_map(
        local,
        mesh=fine,
        in_specs=(
            P(None, None, STRIPS),
            tile,
            tile,
            P(LAT, LON),
            P(LAT, LON),
            *([P()] * 7),
        ),
        out_specs=(tile, P(), P(), P(), P()),
        check_vma=False,
    )
```
